32 devices in a mesh: batch: 2 (over x), ffn: 8 (over z, y), mp: 2 (over core).
Axes of the slice: x: 2, y: 2, z: 4, core: 2. Of those that a mesh axis runs over, the one named last changes fastest.
Arguments:
- tokens: float32 [32, 512, 640], P(('batch', 'ffn', 'mp')), may hold values from -6 to 6
- qkv_weight: float32 [2, 3, 640, 640], P(None, None, ('batch', 'ffn', 'mp')), may hold values from -0.25 to 0.25
- out_weight: float32 [2, 640, 640], P(None, ('batch', 'ffn', 'mp')), may hold values from -1 to 1
- proj_bias: float32 [2, 5, 640], P(None, None, ('batch', 'ffn', 'mp')), may hold values from -1 to 1
- norm_gain: float32 [2, 2, 640], P(None, None, ('batch', 'ffn', 'mp')), may hold values from 0.5 to 1.5
- norm_shift: float32 [2, 2, 640], P(None, None, ('batch', 'ffn', 'mp')), may hold values from -1 to 1
- up_weight: float32 [2, 2560, 640], P(None, ('batch', 'ffn', 'mp')), may hold values from -0.25 to 0.25
- down_weight: float32 [2, 2560, 640], P(None, ('batch', 'ffn', 'mp')), may hold values from -0.125 to 0.125
- up_bias: float32 [2, 2560], P(None, ('batch', 'ffn', 'mp')), may hold values from -1 to 1
- seq_order: int32 [32], P(('batch', 'ffn', 'mp')), may hold values from 0 to 31, each once
- seq_length: int32 [32], replicated, may hold values from 1 to 512, 12288 in all
- mlm_mask: int32 [32, 512], P(('batch', 'ffn', 'mp')), may hold values from 0 to 1
- cotangent: float32 [32, 512, 640], P(('batch', 'ffn', 'mp')), may hold values from -6 to 6
Outputs:
- output: float32 [32, 512, 640], P(('batch', 'ffn', 'mp'))
- tokens_grad: float32 [32, 512, 640], P(('batch', 'ffn', 'mp'))
- qkv_weight_grad: float32 [2, 3, 640, 640], P(None, None, ('batch', 'ffn', 'mp'))
- out_weight_grad: float32 [2, 640, 640], P(None, ('batch', 'ffn', 'mp'))
- proj_bias_grad: float32 [2, 5, 640], P(None, None, ('batch', 'ffn', 'mp'))
- norm_gain_grad: float32 [2, 2, 640], P(None, None, ('batch', 'ffn', 'mp'))
- norm_shift_grad: float32 [2, 2, 640], P(None, None, ('batch', 'ffn', 'mp'))
- up_weight_grad: float32 [2, 2560, 640], P(None, ('batch', 'ffn', 'mp'))
- down_weight_grad: float32 [2, 2560, 640], P(None, ('batch', 'ffn', 'mp'))
- up_bias_grad: float32 [2, 2560], P(None, ('batch', 'ffn', 'mp'))
The draws below stay inside these ranges and needn't reach their ends.
Inputs may be any that keep to these rules, and one draw needn't show every extreme that they name: `seq_order`: every sequence number appears exactly once. `seq_length`: the valid tokens of each sequence number; they sum to 12288 and the longest has exactly 512.
All inputs are finite; a program needn't handle non-finite values.
Results may differ from the reference program's by a relative error of at most 0.018.
Values may be sent and summed in bfloat16 or wider, within the bound.
No kernel may reach another device: no remote copies, remote signals or barrier semaphores. Data moves between devices by JAX's collectives and lax.ppermute only.
A program may use at most 256 MiB of HBM per device.

```python
import math
import jax
import jax.numpy as jnp
import numpy as np
from jax import lax

D = 640
FF = 2560
HEADS = 20
HEAD_DIM = 32
LAYERS = 2
LEN = 512
SEQS = 32


def draw_mlm_mask(key, part):
    slot_index = jnp.arange(SEQS, dtype=jnp.int32)[:, None]
    cutoff = 60 + 180 * slot_index // max(SEQS - 1, 1)
    rolls = jax.random.randint(key, (SEQS, LEN), 0, 1000, dtype=jnp.int32)
    return jnp.where(rolls < cutoff, 1, 0).astype(jnp.int32)


def shard_levels(key, dims, shards, low, top_value):
    level, own = 1.0, jax.random.fold_in(key, 6)
    for axis_at, parts in shards:
        heights = jnp.exp(jax.random.uniform(jax.random.fold_in(own, axis_at), (parts,), jnp.float32, low / len(shards), top_value / len(shards)))
        level = level * jnp.repeat(heights, dims[axis_at] // parts).reshape([-1 if axis == axis_at else 1 for axis in range(len(dims))])
    return level


def length_profile(count, total, limit, lean):
    portions = [(1 << 20) // math.isqrt(grade ** lean) + 1 for grade in range(2, count + 1)]
    rest, holding = total - limit - (count - 1), [1] * (count - 1)
    while rest > 0:
        movable = [i for i in range(count - 1) if holding[i] < limit]
        whole, left = sum([portions[i] for i in movable]), rest
        for i in movable:
            addition = min(limit - holding[i], max(1, left * portions[i] // whole), rest)
            holding[i] = holding[i] + addition
            rest = rest - addition
    return np.array([limit] + holding)


def ragged_sizes(rng, number_of, total, reach, skew):
    if number_of == 2:
        one = jax.random.randint(rng, (), max(1, total - reach), min(reach, total - 1) + 1)
        return jnp.stack([one, total - one])
    sizes = jnp.asarray(length_profile(number_of, total, reach, skew), jnp.int32)
    twos = (number_of - 1) // 2
    giver, sink = sizes[1:1 + 2 * twos:2], sizes[2:2 + 2 * twos:2]
    margin = jnp.minimum(giver - 1, reach - sink)
    passed = jax.random.randint(jax.random.fold_in(rng, 1), (twos,), 0, 1 << 20) % (margin + 1)
    sizes = sizes.at[1:1 + 2 * twos:2].set(giver - passed).at[2:2 + 2 * twos:2].set(sink + passed)
    return sizes[jax.random.permutation(jax.random.fold_in(rng, 2), number_of)]


def normal_values(key, extent, spread, limit, split=(), kind=jnp.bfloat16):
    entries = spread * jax.random.normal(key, extent, jnp.float32)
    if split:
        entries = entries * shard_levels(key, extent, split, -0.22, 0.18)
    return jnp.clip(entries, -limit, limit).astype(kind)


def setup_inputs(seed: int = 0) -> dict:
    streams_of = jax.random.split(jax.random.key(seed), 14)
    return {
        "tokens": normal_values(streams_of[0], (SEQS, LEN, D), 1.0, 6.0, ((0, 32),), jnp.float32),
        "qkv_weight": normal_values(streams_of[1], (LAYERS, 3, D, D), D ** -0.5, 0.25, ((2, 32),), jnp.float32),
        "out_weight": normal_values(streams_of[2], (LAYERS, D, D), (D // 16) ** -0.5, 1.0, ((1, 32),), jnp.float32),
        "proj_bias": normal_values(streams_of[3], (LAYERS, 5, D), 0.2, 1.0, ((2, 32),), jnp.float32),
        "norm_gain": jnp.clip(1.0 + 0.1 * jax.random.normal(streams_of[4], (LAYERS, 2, D), jnp.float32), 0.5, 1.5),
        "norm_shift": normal_values(streams_of[5], (LAYERS, 2, D), 0.2, 1.0, ((2, 32),), jnp.float32),
        "up_weight": normal_values(streams_of[6], (LAYERS, FF, D), D ** -0.5, 0.25, ((1, 32),), jnp.float32),
        "down_weight": normal_values(streams_of[7], (LAYERS, FF, D), FF ** -0.5, 0.125, ((1, 32),), jnp.float32),
        "up_bias": normal_values(streams_of[8], (LAYERS, FF), 0.2, 1.0, ((1, 32),), jnp.float32),
        "seq_order": jax.random.permutation(streams_of[9], SEQS).astype(jnp.int32),
        "seq_length": ragged_sizes(streams_of[10], SEQS, SEQS * LEN * 3 // 4, LEN, 0).astype(jnp.int32),
        "mlm_mask": draw_mlm_mask(jax.random.fold_in(streams_of[13], 71), 0),
        "cotangent": normal_values(streams_of[12], (SEQS, LEN, D), 1.0, 6.0, ((0, 32),), jnp.float32),
    }


highest_precision = lax.Precision.HIGHEST
norm_eps = 1e-05
mask_value = -1e+30
group_seqs = 4

@jax.custom_vjp
def low(v):
    return lax.optimization_barrier(v.astype(jnp.bfloat16)).astype(jnp.float32)

@jax.custom_vjp
def low_back(v):
    return v

def low_keep(v):
    return (low(v), None)

def low_pass(kept, grad):
    return (grad,)

def back_keep(v):
    return (v, None)

def back_low(kept, grad):
    return (low(grad),)
low.defvjp(low_keep, low_pass)
low_back.defvjp(back_keep, back_low)

def low_both(values):
    return low_back(low(values))

def layer_norm(values, gain_vec, shift_vec):
    row_mean = lax.optimization_barrier(jnp.mean(values, axis=-1, keepdims=True))
    centred = values - row_mean
    variance = lax.optimization_barrier(jnp.mean(centred * centred, axis=-1, keepdims=True))
    return centred * lax.rsqrt(variance + norm_eps) * gain_vec + shift_vec

def rope_tables(length, head_width):
    half_width = head_width // 2
    freqs = jnp.exp(jnp.arange(half_width, dtype=jnp.float32) * (-2.0 * math.log(10000.0) / head_width))
    angles = jnp.arange(length, dtype=jnp.float32)[:, None] * freqs[None, :]
    return (jnp.cos(angles), jnp.sin(angles))

def rotate(values, cos_table, sin_table):
    half_width = values.shape[-1] // 2
    first_half = values[..., :half_width]
    second_half = values[..., half_width:]
    cos_rows = cos_table[:, None, :]
    sin_rows = sin_table[:, None, :]
    return jnp.concatenate([first_half * cos_rows - second_half * sin_rows, second_half * cos_rows + first_half * sin_rows], axis=-1)

def attend_sequence(queries, keys_rot, values, key_ok):
    length = queries.shape[0]
    block_rows = min(512, length)
    blocks = queries.reshape((length // block_rows, block_rows) + queries.shape[1:])

    def one_block(query_block):
        scores = jnp.einsum('qhd,khd->hqk', query_block, keys_rot, precision=highest_precision)
        scores = low_back(jnp.where(key_ok[None, None, :], scores, mask_value))
        softmaxed = low(jax.nn.softmax(scores, axis=-1))
        return jnp.einsum('hqk,khd->qhd', softmaxed, values, precision=highest_precision)
    attended_values = lax.map(jax.checkpoint(one_block), blocks)
    return attended_values.reshape(queries.shape)

def layer_forward(stream, weights, key_ok, cos_table, sin_table):
    query_key_value_weight, output_matrix, bias_broadcast_rows, gain_rows, shift_rows, expand_weight, contract_weight, expand_bias = weights
    seq_count, length, width = stream.shape
    hidden_first = low(layer_norm(stream, gain_rows[0], shift_rows[0]))
    projected_rows = jnp.einsum('bpu,guw->gbpw', hidden_first, query_key_value_weight, precision=highest_precision) + bias_broadcast_rows[:3, None, None, :]
    head_shape = (seq_count, length, HEADS, HEAD_DIM)
    queries = low_both(rotate(low_back(projected_rows[0]).reshape(head_shape), cos_table, sin_table) * HEAD_DIM ** (-0.5))
    keys_rot = low_both(rotate(low_back(projected_rows[1]).reshape(head_shape), cos_table, sin_table))
    values = low_both(projected_rows[2].reshape(head_shape))
    attended_values = jax.vmap(attend_sequence)(queries, keys_rot, values, key_ok)
    attended_values = low_both(attended_values.reshape(seq_count, length, width))
    residual_branch = low_back(jnp.einsum('qtn,nx->qtx', attended_values, output_matrix, precision=highest_precision) + bias_broadcast_rows[3])
    middle = stream + residual_branch
    hidden_second = low(layer_norm(middle, gain_rows[1], shift_rows[1]))
    preactivation_rows = low_back(jnp.einsum('cbp,rp->cbr', hidden_second, expand_weight, precision=highest_precision) + expand_bias)
    gelu_activated_rows = low(jax.nn.gelu(preactivation_rows, approximate=False))
    feedforward_output = low_back(jnp.einsum('hbq,qa->hba', gelu_activated_rows, contract_weight, precision=highest_precision) + bias_broadcast_rows[4])
    return middle + feedforward_output

def reference(tokens, qkv_weight, out_weight, proj_bias, norm_gain, norm_shift, up_weight, down_weight, up_bias, seq_order, seq_length, mlm_mask, cotangent):
    cos_table, sin_table = rope_tables(LEN, HEAD_DIM)
    slot_length = seq_length[seq_order]
    key_ok = jnp.arange(LEN, dtype=jnp.int32)[None, :] < slot_length[:, None]
    loss_weight = jnp.where(key_ok & (mlm_mask > 0), 1.0, 0.0).astype(jnp.float32)
    masked_total = jnp.sum(loss_weight)
    factor = SEQS * LEN / jnp.maximum(masked_total, 1.0)
    grad_out = cotangent * loss_weight[:, :, None] * factor
    masters = (qkv_weight, out_weight, proj_bias, norm_gain, norm_shift, up_weight, down_weight, up_bias)
    group_count = SEQS // group_seqs

    def split_groups(values):
        return values.reshape((group_count, group_seqs) + values.shape[1:])

    def one_group(totals, packed):
        stream, grad_stream, group_ok = packed

        def forward(stream_in, params):
            rounded = jax.tree.map(low, params)
            current = stream_in
            for layer_index in range(LAYERS):
                weights = tuple((param[layer_index] for param in rounded))
                current = layer_forward(current, weights, group_ok, cos_table, sin_table)
            return current
        result, backward = jax.vjp(forward, stream, masters)
        grad_input, grad_params = backward(grad_stream)
        return (jax.tree.map(jnp.add, totals, grad_params), (result, grad_input))
    zero_totals = jax.tree.map(jnp.zeros_like, masters)
    totals, (results, grad_inputs) = lax.scan(one_group, zero_totals, (split_groups(tokens), split_groups(grad_out), split_groups(key_ok)))
    return (results.reshape(tokens.shape), grad_inputs.reshape(tokens.shape), totals[0], totals[1], totals[2], totals[3], totals[4], totals[5], totals[6], totals[7])
```

```python
from functools import partial
import math

import jax
import jax.numpy as jnp
from jax import lax
from jax.experimental import pallas as pl
from jax.experimental.pallas import tpu as pltpu
from jax.sharding import PartitionSpec as P

HEADS = 20
HEAD_DIM = 32


norm_eps = 1e-05
mask_value = -1e30


def rope_tables(length, head_width):
    half_width = head_width // 2
    freqs = jnp.exp(
        jnp.arange(half_width, dtype=jnp.float32) * (-2.0 * math.log(10000.0) / head_width)
    )
    angles = jnp.arange(length, dtype=jnp.float32)[:, None] * freqs[None, :]
    return (jnp.cos(angles), jnp.sin(angles))


AXES = ("batch", "ffn", "mp")


def axis_bits(size, unit):
    bits = []
    while size > 1:
        size //= 2
        bits.append(size * unit)
    return bits


def step_orders(sizes):
    batch_size, ffn_size, core_size = sizes
    ffn_bits = axis_bits(ffn_size, core_size)
    batch_bits = axis_bits(batch_size, core_size * ffn_size)
    core_bits = axis_bits(core_size, 1)
    first = ffn_bits[:-1] + ffn_bits[-1:] + batch_bits + core_bits
    second = ffn_bits[:-1] + batch_bits + ffn_bits[-1:] + core_bits
    return (first, second)


def swap_with(values, bit, count):
    return lax.ppermute(values, AXES, [(i, i ^ bit) for i in range(count)])


def gather_pieces(piece, order, count, axis):
    for bit in order:
        piece = jnp.concatenate([piece, swap_with(piece, bit, count)], axis=axis)
    return piece


def reduce_pieces(pieces, order, count, axis):
    for bit in reversed(order):
        kept, sent = jnp.split(pieces, 2, axis=axis)
        came = swap_with(sent, bit, count)
        pieces = (kept.astype(jnp.float32) + came.astype(jnp.float32)).astype(jnp.bfloat16)
    return pieces


def piece_codes(order):
    codes = [0]
    for bit in order:
        codes = codes + [code ^ bit for code in codes]
    return jnp.array(codes, jnp.int32)


def pad_rows(rows):
    return -(-(rows + 1) // 8) * 8


GROUP = 128 // HEAD_DIM


def dot_nn(left, right):
    return lax.dot_general(
        left, right, (((1,), (0,)), ((), ())), preferred_element_type=jnp.float32
    )


def dot_nt(left, right):
    return lax.dot_general(
        left, right, (((1,), (1,)), ((), ())), preferred_element_type=jnp.float32
    )


def dot_tn(left, right):
    return lax.dot_general(
        left, right, (((0,), (0,)), ((), ())), preferred_element_type=jnp.float32
    )


def norm_parts(values):
    centred = values - jnp.mean(values, axis=-1, keepdims=True)
    variance = jnp.mean(centred * centred, axis=-1, keepdims=True)
    inverse = lax.rsqrt(variance + norm_eps)
    return (centred * inverse, inverse)


def norm_grad(grad, values, gain_row):
    unit, inverse = norm_parts(values)
    scaled = grad * gain_row
    mean_one = jnp.mean(scaled, axis=-1, keepdims=True)
    mean_two = jnp.mean(scaled * unit, axis=-1, keepdims=True)
    into = inverse * (scaled - mean_one - unit * mean_two)
    grad_gain = jnp.sum(grad * unit, axis=0, keepdims=True)
    grad_shift = jnp.sum(grad, axis=0, keepdims=True)
    return (into, grad_gain, grad_shift)


def turn(values, cos_ref, sin_ref, sign):
    half = HEAD_DIM // 2
    lanes = lax.broadcasted_iota(jnp.int32, (values.shape[0], 128), 1)
    low_half = lanes % HEAD_DIM < half
    parts = []
    for start in range(0, values.shape[1], 128):
        part = values[:, start : start + 128]
        partner = jnp.where(
            low_half, pltpu.roll(part, 128 - half, 1), pltpu.roll(part, half, 1)
        )
        parts.append(part * cos_ref[...] + sign * (partner * sin_ref[...]))
    return jnp.concatenate(parts, axis=1)


def head_lanes(block, head):
    lanes = lax.broadcasted_iota(jnp.int32, block.shape, 1)
    return jnp.where(lanes // HEAD_DIM == head, block, jnp.zeros_like(block))


def attn_fwd_kernel(
    x_ref, w_ref, spread_ref, vec_ref, cos_ref, sin_ref, mask_ref,
    mid_ref, wabs_ref, h_rel_ref, q_ref, kt_ref, v_ref, att_t_ref, att_rel_ref, probs_ref,
    qt_ref, k_ref, vt_ref,
):
    step = pl.program_id(0)

    @pl.when(step == 0)
    def _():
        unit, _ = norm_parts(x_ref[...])
        h_one = (unit * vec_ref[4:5] + vec_ref[5:6]).astype(jnp.bfloat16)
        h_rel_ref[...] = dot_nn(h_one, spread_ref[...]).astype(jnp.bfloat16)
        for j in range(4):
            wabs_ref[j] = dot_nn(spread_ref[...], w_ref[j]).astype(jnp.bfloat16)
        query = dot_nn(h_one, wabs_ref[0]) + vec_ref[0:1]
        query = turn(query, cos_ref, sin_ref, 1.0) * HEAD_DIM ** (-0.5)
        q_ref[...] = query.astype(jnp.bfloat16)
        qt_ref[...] = query.T.astype(jnp.bfloat16)
        key = turn(dot_nn(h_one, wabs_ref[1]) + vec_ref[1:2], cos_ref, sin_ref, 1.0)
        key_bf = key.astype(jnp.bfloat16)
        for start in range(key.shape[1] // 128):
            k_ref[start] = key_bf[:, 128 * start : 128 * start + 128]
        kt_ref[...] = key.T.astype(jnp.bfloat16)
        value = dot_nn(h_one, wabs_ref[2]) + vec_ref[2:3]
        v_ref[...] = value.astype(jnp.bfloat16)
        vt_ref[...] = value.T.astype(jnp.bfloat16)

    key_block = k_ref[step]
    query_t = qt_ref[pl.ds(pl.multiple_of(step * 128, 128), 128), :]
    for head in range(GROUP):
        scores = dot_nn(head_lanes(key_block, head), query_t) + mask_ref[...]
        top = jnp.max(scores, axis=0, keepdims=True)
        shifted = jnp.exp(scores - top)
        total = jnp.sum(shifted, axis=0, keepdims=True)
        probs = (shifted * (1.0 / total)).astype(jnp.bfloat16)
        probs_ref[head] = probs
        rows = pl.ds(pl.multiple_of(step * 128 + head * HEAD_DIM, HEAD_DIM), HEAD_DIM)
        att_t_ref[rows, :] = dot_nn(vt_ref[rows, :], probs)

    @pl.when(step == pl.num_programs(0) - 1)
    def _():
        att = att_t_ref[...].T.astype(jnp.bfloat16)
        att_rel_ref[...] = dot_nn(att, spread_ref[...]).astype(jnp.bfloat16)
        mid_ref[...] = x_ref[...] + (dot_nn(att, wabs_ref[3]) + vec_ref[3:4])


def whole(shape):
    return pl.BlockSpec(shape, lambda *_: (0,) * len(shape))


def sds(shape, dtype):
    return jax.ShapeDtypeStruct(shape, dtype)


VMEM_LIMIT = 56 * 1024 * 1024


def attn_forward(stream, weights, spread, vecs, cos, sin, mask):
    length, width = stream.shape
    spots = spread.shape[1]
    groups = width // 128
    b16 = jnp.bfloat16
    outs = [
        ((length, width), jnp.float32),
        ((4, width, width), b16),
        ((length, spots), b16),
        ((length, width), b16),
        ((width, length), b16),
        ((length, width), b16),
        ((width, length), jnp.float32),
        ((length, spots), b16),
    ]
    return pl.pallas_call(
        attn_fwd_kernel,
        grid=(groups,),
        in_specs=[whole(a.shape) for a in (stream, weights, spread, vecs, cos, sin, mask)],
        out_specs=[whole(s) for s, _ in outs]
        + [pl.BlockSpec((GROUP, length, length), lambda i: (i, 0, 0))],
        out_shape=[sds(s, d) for s, d in outs] + [sds((HEADS, length, length), b16)],
        scratch_shapes=[
            pltpu.VMEM((width, length), b16),
            pltpu.VMEM((groups, length, 128), b16),
            pltpu.VMEM((width, length), b16),
        ],
        compiler_params=pltpu.CompilerParams(vmem_limit_bytes=VMEM_LIMIT),
        cost_estimate=pl.CostEstimate(
            flops=20_000_000_000, bytes_accessed=25_000_000, transcendentals=HEADS * length * length
        ),
        name="attn_fwd",
    )(stream, weights, spread, vecs, cos, sin, mask)


def ffn_fwd_kernel(
    mid_ref, vec_ref, up_ref, down_ref, bias_ref,
    out_ref, h_two_ref, act_ref, slope_ref,
):
    step = pl.program_id(0)

    @pl.when(step == 0)
    def _():
        unit, _ = norm_parts(mid_ref[...])
        h_two_ref[...] = (unit * vec_ref[6:7] + vec_ref[7:8]).astype(jnp.bfloat16)
        out_ref[...] = mid_ref[...] + vec_ref[8:9]

    pre = dot_nt(h_two_ref[...], up_ref[...]) + bias_ref[0]
    cdf = 0.5 * (1.0 + lax.erf(pre * (0.5**0.5)))
    act = (pre * cdf).astype(jnp.bfloat16)
    act_ref[...] = act
    slope = cdf + pre * (jnp.exp(-0.5 * pre * pre) * (1.0 / math.sqrt(2.0 * math.pi)))
    slope_ref[...] = slope.astype(jnp.bfloat16)
    out_ref[...] += dot_nn(act, down_ref[...])


def ffn_forward(middle, vecs, up_all, down_all, bias, block):
    length, width = middle.shape
    hidden = up_all.shape[0]
    b16 = jnp.bfloat16
    return pl.pallas_call(
        ffn_fwd_kernel,
        grid=(hidden // block,),
        in_specs=[
            whole(middle.shape),
            whole(vecs.shape),
            pl.BlockSpec((block, width), lambda i: (i, 0)),
            pl.BlockSpec((block, width), lambda i: (i, 0)),
            pl.BlockSpec((1, 1, block), lambda i: (i, 0, 0)),
        ],
        out_specs=[
            whole((length, width)),
            whole((length, width)),
            pl.BlockSpec((length, block), lambda i: (0, i)),
            pl.BlockSpec((length, block), lambda i: (0, i)),
        ],
        out_shape=[
            sds((length, width), jnp.float32),
            sds((length, width), b16),
            sds((length, hidden), b16),
            sds((length, hidden), b16),
        ],
        compiler_params=pltpu.CompilerParams(vmem_limit_bytes=VMEM_LIMIT),
        cost_estimate=pl.CostEstimate(
            flops=10_000_000_000, bytes_accessed=15_000_000, transcendentals=2 * length * hidden
        ),
        name="ffn_fwd",
    )(middle, vecs, up_all, down_all, bias.reshape(hidden // block, 1, block))


def ffn_bwd_kernel(
    g_ref, mid_ref, vec_ref, h_two_ref, act_ref, slope_ref, up_ref, down_ref,
    gmid_ref, gup_ref, gdown_ref, gbias_ref, sums_ref,
    gf_ref, gh_ref,
):
    step = pl.program_id(0)

    @pl.when(step == 0)
    def _():
        gf_ref[...] = g_ref[...].astype(jnp.bfloat16)
        gh_ref[...] = jnp.zeros_like(gh_ref)

    gf = gf_ref[...]
    gdown_ref[...] = dot_tn(act_ref[...], gf).astype(jnp.bfloat16)
    g_act = dot_nt(gf, down_ref[...])
    g_pre = (g_act * slope_ref[...].astype(jnp.float32)).astype(jnp.bfloat16)
    gup_ref[...] = dot_tn(g_pre, h_two_ref[...]).astype(jnp.bfloat16)
    gbias_ref[0] = jnp.sum(g_pre.astype(jnp.float32), axis=0, keepdims=True)
    gh_ref[...] += dot_nn(g_pre, up_ref[...])

    @pl.when(step == pl.num_programs(0) - 1)
    def _():
        into, grad_gain, grad_shift = norm_grad(gh_ref[...], mid_ref[...], vec_ref[6:7])
        gmid_ref[...] = g_ref[...] + into
        sums_ref[...] = jnp.zeros_like(sums_ref)
        sums_ref[0:1] = grad_gain
        sums_ref[1:2] = grad_shift
        sums_ref[2:3] = jnp.sum(gf_ref[...].astype(jnp.float32), axis=0, keepdims=True)


def ffn_backward(grad, middle, vecs, h_two, act, slope, up_all, down_all, block):
    length, width = middle.shape
    hidden = up_all.shape[0]
    b16 = jnp.bfloat16
    tall = pl.BlockSpec((block, width), lambda i: (i, 0))
    wide = pl.BlockSpec((length, block), lambda i: (0, i))
    return pl.pallas_call(
        ffn_bwd_kernel,
        grid=(hidden // block,),
        in_specs=[
            whole(grad.shape), whole(middle.shape), whole(vecs.shape), whole(h_two.shape),
            wide, wide, tall, tall,
        ],
        out_specs=[
            whole((length, width)), tall, tall,
            pl.BlockSpec((1, 1, block), lambda i: (i, 0, 0)),
            whole((8, width)),
        ],
        out_shape=[
            sds((length, width), jnp.float32),
            sds((hidden, width), b16),
            sds((hidden, width), b16),
            sds((hidden // block, 1, block), jnp.float32),
            sds((8, width), jnp.float32),
        ],
        scratch_shapes=[pltpu.VMEM((length, width), b16), pltpu.VMEM((length, width), jnp.float32)],
        compiler_params=pltpu.CompilerParams(vmem_limit_bytes=VMEM_LIMIT),
        cost_estimate=pl.CostEstimate(
            flops=20_000_000_000, bytes_accessed=25_000_000, transcendentals=0
        ),
        name="ffn_bwd",
    )(grad, middle, vecs, h_two, act, slope, up_all, down_all)


def attn_bwd_kernel(
    gmid_ref, x_ref, wabs_ref, vec_ref, cos_ref, sin_ref, h_rel_ref, q_ref, kt_ref, v_ref,
    att_t_ref, att_rel_ref, probs_ref,
    gx_ref, gw_ref, sums_ref,
    ga_ref, gatt_ref, gatt_t_ref, inner_ref, dqt_ref, dk_ref, dv_ref, qs_ref, vs_ref,
):
    step = pl.program_id(0)
    groups = pl.num_programs(0)

    @pl.when(step == 0)
    def _():
        ga_ref[...] = gmid_ref[...].astype(jnp.bfloat16)
        gw_ref[3] = dot_tn(att_rel_ref[...], ga_ref[...]).astype(jnp.bfloat16)
        gatt = dot_nt(ga_ref[...], wabs_ref[3]).astype(jnp.bfloat16)
        for start in range(gatt.shape[1] // 128):
            lanes = slice(128 * start, 128 * start + 128)
            gatt_ref[start] = gatt[:, lanes]
            qs_ref[start] = q_ref[:, lanes]
            vs_ref[start] = v_ref[:, lanes]
        gatt_t = gatt.astype(jnp.float32).T
        gatt_t_ref[...] = gatt_t.astype(jnp.bfloat16)
        for head in range(HEADS):
            rows = slice(head * HEAD_DIM, (head + 1) * HEAD_DIM)
            inner_ref[head] = jnp.sum(gatt_t[rows] * att_t_ref[rows], axis=0, keepdims=True)

    gatt_block = gatt_ref[step]
    q_block = qs_ref[step]
    v_block = vs_ref[step]
    gatt_t = gatt_t_ref[pl.ds(pl.multiple_of(step * 128, 128), 128), :]
    dk = jnp.zeros(q_block.shape, jnp.float32)
    dv = jnp.zeros(q_block.shape, jnp.float32)
    for head in range(GROUP):
        probs = probs_ref[head]
        gprobs = dot_nn(head_lanes(v_block, head), gatt_t)
        gscores = (probs.astype(jnp.float32) * (gprobs - inner_ref[step * GROUP + head])).astype(
            jnp.bfloat16
        )
        dv += dot_nn(probs, head_lanes(gatt_block, head))
        dk += dot_nn(gscores, head_lanes(q_block, head))
        rows = pl.ds(pl.multiple_of(step * 128 + head * HEAD_DIM, HEAD_DIM), HEAD_DIM)
        dqt_ref[rows, :] = dot_nn(kt_ref[rows, :], gscores)
    dk_ref[step] = dk
    dv_ref[step] = dv

    @pl.when(step == groups - 1)
    def _():
        def joined(ref):
            return jnp.concatenate([ref[i] for i in range(ref.shape[0])], axis=1)

        def rounded(values):
            return values.astype(jnp.bfloat16).astype(jnp.float32)

        gq = rounded(dqt_ref[...].T) * HEAD_DIM ** (-0.5)
        gproj = [
            turn(gq, cos_ref, sin_ref, -1.0).astype(jnp.bfloat16),
            turn(rounded(joined(dk_ref)), cos_ref, sin_ref, -1.0).astype(jnp.bfloat16),
            joined(dv_ref).astype(jnp.bfloat16),
        ]
        sums_ref[...] = jnp.zeros_like(sums_ref)
        gh = jnp.zeros(gx_ref.shape, jnp.float32)
        for j in range(3):
            gw_ref[j] = dot_tn(h_rel_ref[...], gproj[j]).astype(jnp.bfloat16)
            sums_ref[j : j + 1] = jnp.sum(gproj[j].astype(jnp.float32), axis=0, keepdims=True)
            gh += dot_nt(gproj[j], wabs_ref[j])
        into, grad_gain, grad_shift = norm_grad(gh, x_ref[...], vec_ref[4:5])
        gx_ref[...] = gmid_ref[...] + into
        sums_ref[3:4] = jnp.sum(ga_ref[...].astype(jnp.float32), axis=0, keepdims=True)
        sums_ref[4:5] = grad_gain
        sums_ref[5:6] = grad_shift


def attn_backward(grad, stream, wabs, vecs, cos, sin, h_rel, q, kt, v, att_t, att_rel, probs):
    length, width = stream.shape
    spots = h_rel.shape[1]
    groups = width // 128
    b16 = jnp.bfloat16
    full = (grad, stream, wabs, vecs, cos, sin, h_rel, q, kt, v, att_t, att_rel)
    outs = [((length, width), jnp.float32), ((4, spots, width), b16), ((8, width), jnp.float32)]
    return pl.pallas_call(
        attn_bwd_kernel,
        grid=(groups,),
        in_specs=[whole(a.shape) for a in full]
        + [pl.BlockSpec((GROUP, length, length), lambda i: (i, 0, 0))],
        out_specs=[whole(s) for s, _ in outs],
        out_shape=[sds(s, d) for s, d in outs],
        scratch_shapes=[
            pltpu.VMEM((length, width), b16),
            pltpu.VMEM((groups, length, 128), b16),
            pltpu.VMEM((width, length), b16),
            pltpu.VMEM((HEADS, 1, length), jnp.float32),
            pltpu.VMEM((width, length), jnp.float32),
            pltpu.VMEM((groups, length, 128), jnp.float32),
            pltpu.VMEM((groups, length, 128), jnp.float32),
            pltpu.VMEM((groups, length, 128), b16),
            pltpu.VMEM((groups, length, 128), b16),
        ],
        compiler_params=pltpu.CompilerParams(vmem_limit_bytes=VMEM_LIMIT),
        cost_estimate=pl.CostEstimate(
            flops=30_000_000_000, bytes_accessed=30_000_000, transcendentals=0
        ),
        name="attn_bwd",
    )(*full, probs)


def shards(
    sizes,
    tokens,
    qkv_weight,
    out_weight,
    proj_bias,
    norm_gain,
    norm_shift,
    up_weight,
    down_weight,
    up_bias,
    seq_order,
    seq_length,
    mlm_mask,
    cotangent,
):
    _, length, width = tokens.shape
    layer_count = qkv_weight.shape[0]
    count = sizes[0] * sizes[1] * sizes[2]
    first, second = step_orders(sizes)
    own_id = lax.axis_index(AXES)
    rows = qkv_weight.shape[2]
    slots = pad_rows(rows)
    hidden = up_weight.shape[1]
    b16 = jnp.bfloat16

    order_ids = jnp.arange(seq_length.shape[0], dtype=jnp.int32)
    slot_length = jnp.sum(jnp.where(seq_order[0] == order_ids, seq_length, 0))
    key_ok = jnp.arange(length, dtype=jnp.int32) < slot_length
    loss_weight = jnp.where(key_ok & (mlm_mask[0] > 0), 1.0, 0.0).astype(jnp.float32)
    local_count = jnp.sum(loss_weight)
    count_high = jnp.floor(local_count / 256.0)
    count_low = local_count - 256.0 * count_high
    small_len = 9 * rows + hidden
    small_row = jnp.concatenate(
        [
            part.reshape(-1)
            for layer in range(layer_count)
            for part in (proj_bias[layer], norm_gain[layer], norm_shift[layer], up_bias[layer])
        ]
        + [count_high[None], count_low[None]]
    ).astype(b16)
    small_row = jnp.pad(small_row, (0, width - small_row.shape[0]))
    gathered = []
    for layer in range(layer_count):
        attn_piece = jnp.concatenate([qkv_weight[layer], out_weight[layer][None]], axis=0)
        attn_piece = jnp.pad(attn_piece.astype(b16), ((0, 0), (0, slots - rows), (0, 0)))
        if layer == 0:
            attn_piece = attn_piece.at[0, rows].set(small_row)
        gathered.append(
            (
                gather_pieces(attn_piece, first, count, 1),
                gather_pieces(up_weight[layer].astype(b16), first, count, 0),
                gather_pieces(down_weight[layer].astype(b16), first, count, 0),
            )
        )

    owners = own_id ^ piece_codes(first)
    owner_hot = (owners[:, None] == jnp.arange(count, dtype=jnp.int32)[None, :]).astype(b16)
    slot_ids = jnp.arange(slots, dtype=jnp.int32)
    source_row = jnp.where(
        slot_ids[None, :] < rows, owners[:, None] * rows + slot_ids[None, :], -1
    ).reshape(count * slots)
    spread = (jnp.arange(width, dtype=jnp.int32)[:, None] == source_row[None, :]).astype(b16)
    cos_half, sin_half = rope_tables(length, HEAD_DIM)
    cos = jnp.tile(jnp.concatenate([cos_half, cos_half], axis=1), (1, GROUP))
    sin = jnp.tile(jnp.concatenate([-sin_half, sin_half], axis=1), (1, GROUP))
    mask = jnp.where(key_ok, 0.0, mask_value).astype(jnp.float32)[:, None]

    small_rel = gathered[0][0][0].reshape(count, slots, width)[:, rows, :]
    small_all = dot_tn(owner_hot, small_rel)
    spot = layer_count * small_len
    masked_total = jnp.sum(small_all[:, spot] * 256.0 + small_all[:, spot + 1])
    factor = seq_length.shape[0] * length / jnp.maximum(masked_total, 1.0)

    block = count * hidden // 4
    stream = tokens[0]
    saved = []
    for layer in range(layer_count):
        attn_all, up_all, down_all = gathered[layer]
        small = small_all[:, layer * small_len : layer * small_len + 9 * rows]
        vecs = small.reshape(count, 9, rows).transpose(1, 0, 2).reshape(9, width)
        vecs = jnp.concatenate([vecs[:4], vecs[5:6], vecs[7:8], vecs[6:7], vecs[8:9], vecs[4:5]])
        vecs = jnp.pad(vecs, ((0, 7), (0, 0)))
        bias = small_rel[:, layer * small_len + 9 * rows : (layer + 1) * small_len]
        bias = bias.reshape(count * hidden).astype(jnp.float32)
        middle, wabs, *kept, probs = attn_forward(
            stream, attn_all, spread, vecs, cos, sin, mask
        )
        result, h_two, act, slope = ffn_forward(middle, vecs, up_all, down_all, bias, block)
        saved.append((stream, middle, vecs, wabs, kept, probs, h_two, act, slope, up_all, down_all))
        stream = result

    grad = cotangent[0] * (loss_weight[:, None] * factor)
    results = [None] * layer_count
    for layer in reversed(range(layer_count)):
        into, middle, vecs, wabs, kept, probs, h_two, act, slope, up_all, down_all = saved[layer]
        grad_mid, grad_up, grad_down, grad_bias, ffn_sums = ffn_backward(
            grad, middle, vecs, h_two, act, slope, up_all, down_all, block
        )
        own_up = reduce_pieces(grad_up, first, count, 0)
        own_down = reduce_pieces(grad_down, first, count, 0)
        grad, grad_w, attn_sums = attn_backward(
            grad_mid, into, wabs, vecs, cos, sin, *kept, probs
        )
        sums = jnp.concatenate(
            [
                attn_sums[:4],
                ffn_sums[2:3],
                attn_sums[4:5],
                ffn_sums[0:1],
                attn_sums[5:6],
                ffn_sums[1:2],
            ]
        )
        sums = sums.reshape(9, count, rows).transpose(1, 0, 2).reshape(count, 9 * rows)
        sums = dot_nn(owner_hot, sums.astype(b16))
        sums = jnp.concatenate([sums, grad_bias.reshape(count, hidden)], axis=1)
        sums = jnp.pad(sums, ((0, 0), (0, width - small_len))).astype(b16)
        grad_w = grad_w.reshape(4, count, slots, width).at[0, :, rows, :].set(sums)
        own = reduce_pieces(grad_w.reshape(4, count * slots, width), first, count, 1)
        results[layer] = (own.astype(jnp.float32), own_up, own_down)
    own_attn = jnp.stack([entry[0] for entry in results])
    own_small = own_attn[:, 0, rows]
    return (
        stream[None],
        grad[None],
        own_attn[:, :3, :rows],
        own_attn[:, 3, :rows],
        own_small[:, : 5 * rows].reshape(layer_count, 5, rows),
        own_small[:, 5 * rows : 7 * rows].reshape(layer_count, 2, rows),
        own_small[:, 7 * rows : 9 * rows].reshape(layer_count, 2, rows),
        jnp.stack([entry[1] for entry in results]).astype(jnp.float32),
        jnp.stack([entry[2] for entry in results]).astype(jnp.float32),
        own_small[:, 9 * rows : small_len],
    )


def solution(mesh):
    in_specs = (
        P(("batch", "ffn", "mp"), None, None),
        P(None, None, ("batch", "ffn", "mp"), None),
        P(None, ("batch", "ffn", "mp"), None),
        P(None, None, ("batch", "ffn", "mp")),
        P(None, None, ("batch", "ffn", "mp")),
        P(None, None, ("batch", "ffn", "mp")),
        P(None, ("batch", "ffn", "mp"), None),
        P(None, ("batch", "ffn", "mp"), None),
        P(None, ("batch", "ffn", "mp")),
        P(("batch", "ffn", "mp")),
        P(),
        P(("batch", "ffn", "mp"), None),
        P(("batch", "ffn", "mp"), None, None),
    )
    out_specs = (
        P(("batch", "ffn", "mp"), None, None),
        P(("batch", "ffn", "mp"), None, None),
        P(None, None, ("batch", "ffn", "mp"), None),
        P(None, ("batch", "ffn", "mp"), None),
        P(None, None, ("batch", "ffn", "mp")),
        P(None, None, ("batch", "ffn", "mp")),
        P(None, None, ("batch", "ffn", "mp")),
        P(None, ("batch", "ffn", "mp"), None),
        P(None, ("batch", "ffn", "mp"), None),
        P(None, ("batch", "ffn", "mp")),
    )
    sizes = tuple(mesh.shape[name] for name in AXES)
    return jax.shard_map(partial(shards, sizes), mesh=mesh, in_specs=in_specs, out_specs=out_specs, check_vma=False)
```

```python
from functools import partial
import math

import jax
import jax.numpy as jnp
from jax import lax
from jax.experimental import pallas as pl
from jax.experimental.pallas import tpu as pltpu
from jax.sharding import PartitionSpec as P

HEADS = 20
HEAD_DIM = 32


norm_eps = 1e-05
mask_value = -1e30


def rope_tables(length, head_width):
    half_width = head_width // 2
    freqs = jnp.exp(
        jnp.arange(half_width, dtype=jnp.float32) * (-2.0 * math.log(10000.0) / head_width)
    )
    angles = jnp.arange(length, dtype=jnp.float32)[:, None] * freqs[None, :]
    return (jnp.cos(angles), jnp.sin(angles))


AXES = ("batch", "ffn", "mp")
CUT = 2


def after(value, *others):
    return lax.optimization_barrier((value, *others))[0]


def pad_rows(rows):
    return -(-(rows + 1) // 8) * 8


GROUP = 128 // HEAD_DIM
VMEM_LIMIT = 56 * 1024 * 1024


def dot_nn(left, right):
    return lax.dot_general(
        left, right, (((1,), (0,)), ((), ())), preferred_element_type=jnp.float32
    )


def dot_nt(left, right):
    return lax.dot_general(
        left, right, (((1,), (1,)), ((), ())), preferred_element_type=jnp.float32
    )


def dot_tn(left, right):
    return lax.dot_general(
        left, right, (((0,), (0,)), ((), ())), preferred_element_type=jnp.float32
    )


def norm_parts(values):
    centred = values - jnp.mean(values, axis=-1, keepdims=True)
    variance = jnp.mean(centred * centred, axis=-1, keepdims=True)
    inverse = lax.rsqrt(variance + norm_eps)
    return (centred * inverse, inverse)


def norm_grad(grad, values, gain_row):
    unit, inverse = norm_parts(values)
    scaled = grad * gain_row
    mean_one = jnp.mean(scaled, axis=-1, keepdims=True)
    mean_two = jnp.mean(scaled * unit, axis=-1, keepdims=True)
    into = inverse * (scaled - mean_one - unit * mean_two)
    grad_gain = jnp.sum(grad * unit, axis=0, keepdims=True)
    grad_shift = jnp.sum(grad, axis=0, keepdims=True)
    return (into, grad_gain, grad_shift)


def turn(values, cos_ref, sin_ref, sign):
    half = HEAD_DIM // 2
    lanes = lax.broadcasted_iota(jnp.int32, (values.shape[0], 128), 1)
    low_half = lanes % HEAD_DIM < half
    parts = []
    for start in range(0, values.shape[1], 128):
        part = values[:, start : start + 128]
        partner = jnp.where(
            low_half, pltpu.roll(part, 128 - half, 1), pltpu.roll(part, half, 1)
        )
        parts.append(part * cos_ref[...] + sign * (partner * sin_ref[...]))
    return jnp.concatenate(parts, axis=1)


def head_lanes(block, head):
    lanes = lax.broadcasted_iota(jnp.int32, block.shape, 1)
    return jnp.where(lanes // HEAD_DIM == head, block, jnp.zeros_like(block))


def sds(shape, dtype):
    return jax.ShapeDtypeStruct(shape, dtype)


def whole(shape):
    return pl.BlockSpec(shape, lambda *_: (0,) * len(shape))


def call(body, name, grid, ins, outs, scratch, flops, moved, prefetch=None, aliases=None):
    names = list(ins) + list(outs) + list(scratch)
    lead = 0 if prefetch is None else 1

    def kernel(*refs):
        named = dict(zip(names, refs[lead:]))
        body(named)

    in_specs = [spec or whole(array.shape) for array, spec in ins.values()]
    out_specs = [spec or whole(shape) for shape, _, spec in outs.values()]
    out_shape = [sds(shape, dtype) for shape, dtype, _ in outs.values()]
    scratch_shapes = [pltpu.VMEM(shape, dtype) for shape, dtype in scratch.values()]
    operands = ([] if prefetch is None else [prefetch]) + [array for array, _ in ins.values()]
    in_names, out_names = list(ins), list(outs)
    pairs = {
        in_names.index(a) + lead: out_names.index(b) for a, b in (aliases or {}).items()
    }
    results = pl.pallas_call(
        kernel,
        grid_spec=pltpu.PrefetchScalarGridSpec(
            num_scalar_prefetch=lead,
            grid=grid,
            in_specs=in_specs,
            out_specs=out_specs,
            scratch_shapes=scratch_shapes,
        ),
        out_shape=out_shape,
        input_output_aliases=pairs,
        compiler_params=pltpu.CompilerParams(vmem_limit_bytes=VMEM_LIMIT),
        cost_estimate=pl.CostEstimate(flops=flops, bytes_accessed=moved, transcendentals=0),
        name=name,
    )(*operands)
    return dict(zip(out_names, results))


def attn_open(r):
    unit, _ = norm_parts(r["x"][...])
    h_one = (unit * r["vec"][4:5] + r["vec"][5:6]).astype(jnp.bfloat16)
    r["h_rel"][...] = dot_nn(h_one, r["sg" if "sg" in r else "sa"][...]).astype(jnp.bfloat16)
    wabs = r["wabs"]
    half = r["wa"].shape[1]
    for j in range(4):
        spread = r["sa"] if j < 2 or "sb" not in r else r["sb"]
        own, came = ("wa", "wa2") if j < 2 else ("wb", "wb2")
        placed = dot_nn(spread[:, :half], r[own][j % 2])
        placed += dot_nn(spread[:, half:], r[came][j % 2])
        wabs[j] = placed.astype(jnp.bfloat16)
    query = dot_nn(h_one, wabs[0]) + r["vec"][0:1]
    query = turn(query, r["cos"], r["sin"], 1.0) * HEAD_DIM ** (-0.5)
    r["q"][...] = query.astype(jnp.bfloat16)
    r["qt"][...] = query.T.astype(jnp.bfloat16)
    key = turn(dot_nn(h_one, wabs[1]) + r["vec"][1:2], r["cos"], r["sin"], 1.0)
    key_bf = key.astype(jnp.bfloat16)
    for start in range(key.shape[1] // 128):
        r["k"][start] = key_bf[:, 128 * start : 128 * start + 128]
    r["kt"][...] = key.T.astype(jnp.bfloat16)
    value = dot_nn(h_one, wabs[2]) + r["vec"][2:3]
    r["v"][...] = value.astype(jnp.bfloat16)
    r["vt"][...] = value.T.astype(jnp.bfloat16)


def attn_heads(r, group):
    key_block = r["k"][group]
    query_t = r["qt"][pl.ds(pl.multiple_of(group * 128, 128), 128), :]
    for head in range(GROUP):
        scores = dot_nn(head_lanes(key_block, head), query_t) + r["mask"][...]
        top = jnp.max(scores, axis=0, keepdims=True)
        shifted = jnp.exp(scores - top)
        total = jnp.sum(shifted, axis=0, keepdims=True)
        probs = (shifted * (1.0 / total)).astype(jnp.bfloat16)
        r["probs"][head] = probs
        rows = pl.ds(pl.multiple_of(group * 128 + head * HEAD_DIM, HEAD_DIM), HEAD_DIM)
        r["att_t"][rows, :] = dot_nn(r["vt"][rows, :], probs)


def attn_close(r):
    att = r["att_t"][...].T.astype(jnp.bfloat16)
    r["att_rel"][...] = dot_nn(att, r["sg" if "sg" in r else "sa"][...]).astype(jnp.bfloat16)
    r["mid"][...] = r["x"][...] + (dot_nn(att, r["wabs"][3]) + r["vec"][3:4])


def attn_forward(x, parts, spreads, vec, cos, sin, mask, cut, between):
    length, width = x.shape
    spots = spreads["sa"].shape[1]
    groups = width // 128
    b16, f32 = jnp.bfloat16, jnp.float32
    opening = {"x": x, **parts, **spreads}
    tables = {"vec": vec, "cos": cos, "sin": sin, "mask": mask}
    made = {
        "wabs": ((4, width, width), b16, None),
        "h_rel": ((length, spots), b16, None),
        "q": ((length, width), b16, None),
        "kt": ((width, length), b16, None),
        "v": ((length, width), b16, None),
    }
    work = {
        "qt": ((width, length), b16),
        "k": ((groups, length, 128), b16),
        "vt": ((width, length), b16),
    }
    att_t = {"att_t": ((width, length), f32, None)}
    closing = {"att_rel": ((length, spots), b16, None), "mid": ((length, width), f32, None)}

    def probs_out(base):
        spec = pl.BlockSpec((GROUP, length, length), lambda i: (i + base, 0, 0))
        return {"probs": ((HEADS, length, length), b16, spec)}

    def plain(arrays):
        return {name: (array, None) for name, array in arrays.items()}

    def body(first, last, base, steps):
        def run(r):
            step = pl.program_id(0)
            if first:
                pl.when(step == 0)(lambda: attn_open(r))
            else:

                @pl.when(step == 0)
                def _():
                    r["att_t"][: base * 128, :] = r["att_in"][: base * 128, :]

            attn_heads(r, step + base)
            if last:
                pl.when(step == steps - 1)(lambda: attn_close(r))

        return run

    if cut == groups:
        return call(
            body(True, True, 0, groups), "attn_fwd", (groups,),
            plain({**opening, **tables}), {**made, **att_t, **closing, **probs_out(0)}, work,
            20_000_000_000, 25_000_000,
        )
    shared = {name: (shape, dtype, None) for name, (shape, dtype) in work.items()}
    one = call(
        body(True, False, 0, cut), "attn_fwd_one", (cut,),
        plain({**opening, **tables}), {**made, **att_t, **shared, **probs_out(0)}, {},
        10_000_000_000, 15_000_000,
    )
    att_in = between(one["att_t"])
    ins = plain(
        {
            "x": x, "sg": spreads["sa"], "vec": vec, "mask": mask, "wabs": one["wabs"], "att_in": att_in,
            "qt": one["qt"], "k": one["k"], "vt": one["vt"],
        }
    )
    ins["probs_in"] = (one["probs"], pl.BlockSpec(memory_space=pl.ANY))
    two = call(
        body(False, True, cut, groups - cut), "attn_fwd_two", (groups - cut,),
        ins, {**att_t, **closing, **probs_out(cut)}, {},
        10_000_000_000, 15_000_000, aliases={"probs_in": "probs"},
    )
    return {**one, **two}


def ffn_specs(kind, arrays, base, hidden, lines, width):
    specs = {}
    if kind == "own":
        shape = (lines * hidden, width)
        for y in range(2):
            specs[f"up{y}"] = (arrays[0], pl.BlockSpec(shape, lambda i, own, y=y: (2 * i + y, 0)))
            specs[f"down{y}"] = (arrays[1], pl.BlockSpec(shape, lambda i, own, y=y: (2 * y + i, 0)))
        return specs
    shape = (1, lines, 1, 1, hidden, width)
    for which, name in enumerate(("up", "down")):
        for y in range(2):

            def index(i, own, y=y, which=which):
                return (i ^ own[0], 0, y ^ own[1], base ^ own[2], which, 0)

            specs[f"{name}{y}"] = (arrays[0], pl.BlockSpec(shape, index))
    return specs


def rows_of(ref):
    values = ref[...]
    return values.reshape(-1, values.shape[-1])


def ffn_forward(own, mid, vec, kind, arrays, bias, lines, hidden, base, before):
    length, width = mid.shape
    block = lines * hidden
    b16 = jnp.bfloat16
    kept = pl.BlockSpec((2, length, block), lambda i, own: (i, 0, 0))

    def body(r):
        h_two = r["h_two"] if before is None else r["h_in"]

        @pl.when(pl.program_id(0) == 0)
        def _():
            if before is None:
                unit, _ = norm_parts(r["mid"][...])
                h_two[...] = (unit * r["vec"][6:7] + r["vec"][7:8]).astype(b16)
                r["out"][...] = r["mid"][...] + r["vec"][8:9]
            else:
                r["out"][...] = r["so_far"][...]

        for y in range(2):
            pre = dot_nt(h_two[...], rows_of(r[f"up{y}"])) + r["bias"][y]
            cdf = 0.5 * (1.0 + lax.erf(pre * (0.5**0.5)))
            act = (pre * cdf).astype(b16)
            r["act"][y] = act
            slope = cdf + pre * (jnp.exp(-0.5 * pre * pre) * (1.0 / math.sqrt(2.0 * math.pi)))
            r["slope"][y] = slope.astype(b16)
            r["out"][...] += dot_nn(act, rows_of(r[f"down{y}"]))

    ins = {
        **ffn_specs(kind, arrays, base, hidden, lines, width),
        "bias": (
            bias.reshape(4, 1, block),
            pl.BlockSpec((2, 1, block), lambda i, own: (i, 0, 0)),
        ),
    }
    outs = {
        "out": ((length, width), jnp.float32, None),
        "act": ((4, length, block), b16, kept),
        "slope": ((4, length, block), b16, kept),
    }
    if before is None:
        ins.update({"mid": (mid, None), "vec": (vec, None)})
        outs["h_two"] = ((length, width), b16, None)
    else:
        ins.update({"h_in": (before["h_two"], None), "so_far": (before["out"], None)})
    name = "ffn_fwd_one" if before is None else "ffn_fwd_two"
    return call(body, name, (2,), ins, outs, {}, 5_000_000_000, 10_000_000, prefetch=own)


def ffn_backward(own, grad, mid, vec, kept, h_two, kind, arrays, lines, hidden, base, gh_in):
    length, width = mid.shape
    block = lines * hidden
    b16, f32 = jnp.bfloat16, jnp.float32
    last = gh_in is not None
    wide = pl.BlockSpec((2, length, block), lambda i, own: (i, 0, 0))

    def body(r):
        @pl.when(pl.program_id(0) == 0)
        def _():
            r["gf"][...] = r["g"][...].astype(b16)
            r["gh"][...] = r["gh_in"][...] if last else jnp.zeros_like(r["gh"])

        gf = r["gf"][...]
        for y in range(2):
            g_down = dot_tn(r["act"][y], gf)
            g_act = dot_nt(gf, rows_of(r[f"down{y}"]))
            g_pre = (g_act * r["slope"][y].astype(f32)).astype(b16)
            g_up = dot_tn(g_pre, r["h_two"][...])
            for line in range(lines):
                rows = slice(line * hidden, (line + 1) * hidden)
                r["grads"][y, line, 0] = g_up[rows].astype(b16)
                r["grads"][y, line, 1] = g_down[rows].astype(b16)
            r["gbias"][y] = jnp.sum(g_pre.astype(f32), axis=0, keepdims=True)
            r["gh"][...] += dot_nn(g_pre, rows_of(r[f"up{y}"]))
        if last:

            @pl.when(pl.program_id(0) == 1)
            def _():
                into, grad_gain, grad_shift = norm_grad(
                    r["gh"][...], r["mid"][...], r["vec"][6:7]
                )
                r["gmid"][...] = r["g"][...] + into
                r["sums"][...] = jnp.zeros_like(r["sums"])
                r["sums"][0:1] = grad_gain
                r["sums"][1:2] = grad_shift
                r["sums"][2:3] = jnp.sum(r["gf"][...].astype(f32), axis=0, keepdims=True)

    ins = {
        "g": (grad, None),
        "h_two": (h_two, None),
        "act": (kept["act"], wide),
        "slope": (kept["slope"], wide),
        **ffn_specs(kind, arrays, base, hidden, lines, width),
    }
    outs = {
        "grads": (
            (4, lines, 2, hidden, width),
            b16,
            pl.BlockSpec((2, lines, 2, hidden, width), lambda i, own: (i, 0, 0, 0, 0)),
        ),
        "gbias": ((4, 1, block), f32, pl.BlockSpec((2, 1, block), lambda i, own: (i, 0, 0))),
    }
    scratch = {"gf": ((length, width), b16)}
    if last:
        ins.update({"gh_in": (gh_in, None), "mid": (mid, None), "vec": (vec, None)})
        outs["gmid"] = ((length, width), f32, None)
        outs["sums"] = ((8, width), f32, None)
        scratch["gh"] = ((length, width), f32)
    else:
        outs["gh"] = ((length, width), f32, None)
    name = "ffn_bwd_two" if last else "ffn_bwd_one"
    return call(body, name, (2,), ins, outs, scratch, 9_000_000_000, 15_000_000, prefetch=own)


def put_pieces(r, index, values):
    count, _, slots, _ = r["kept"].shape
    for piece in range(2 * count):
        ref = r["kept"] if piece < count else r["sent"]
        ref[piece % count, index] = values[piece * slots : (piece + 1) * slots].astype(ref.dtype)


def attn_grad_open(r):
    b16 = jnp.bfloat16
    r["ga"][...] = r["gmid"][...].astype(b16)
    put_pieces(r, 3, dot_tn(r["att_rel"][...], r["ga"][...]))
    gatt = dot_nt(r["ga"][...], r["wabs"][3]).astype(b16)
    for start in range(gatt.shape[1] // 128):
        lanes = slice(128 * start, 128 * start + 128)
        r["gatt"][start] = gatt[:, lanes]
        r["qs"][start] = r["q"][:, lanes]
        r["vs"][start] = r["v"][:, lanes]
    gatt_t = gatt.astype(jnp.float32).T
    r["gatt_t"][...] = gatt_t.astype(b16)
    for head in range(HEADS):
        rows = slice(head * HEAD_DIM, (head + 1) * HEAD_DIM)
        r["inner"][head] = jnp.sum(gatt_t[rows] * r["att_t"][rows], axis=0, keepdims=True)


def attn_grad_heads(r, group):
    gatt_block, q_block, v_block = r["gatt"][group], r["qs"][group], r["vs"][group]
    gatt_t = r["gatt_t"][pl.ds(pl.multiple_of(group * 128, 128), 128), :]
    dk = jnp.zeros(q_block.shape, jnp.float32)
    dv = jnp.zeros(q_block.shape, jnp.float32)
    for head in range(GROUP):
        probs = r["probs"][head]
        gprobs = dot_nn(head_lanes(v_block, head), gatt_t)
        inner = r["inner"][group * GROUP + head]
        gscores = (probs.astype(jnp.float32) * (gprobs - inner)).astype(jnp.bfloat16)
        dv += dot_nn(probs, head_lanes(gatt_block, head))
        dk += dot_nn(gscores, head_lanes(q_block, head))
        rows = pl.ds(pl.multiple_of(group * 128 + head * HEAD_DIM, HEAD_DIM), HEAD_DIM)
        r["dqt"][rows, :] = dot_nn(r["kt"][rows, :], gscores)
    r["dk"][group] = dk
    r["dv"][group] = dv


def attn_grad_close(r):
    b16, f32 = jnp.bfloat16, jnp.float32

    def joined(ref):
        return jnp.concatenate([ref[i] for i in range(ref.shape[0])], axis=1)

    def rounded(values):
        return values.astype(b16).astype(f32)

    gq = rounded(r["dqt"][...].T) * HEAD_DIM ** (-0.5)
    gproj = [
        turn(gq, r["cos"], r["sin"], -1.0).astype(b16),
        turn(rounded(joined(r["dk"])), r["cos"], r["sin"], -1.0).astype(b16),
        joined(r["dv"]).astype(b16),
    ]
    r["sums"][...] = jnp.zeros_like(r["sums"])
    gh = jnp.zeros(r["gx"].shape, f32)
    for j in range(3):
        put_pieces(r, j, dot_tn(r["h_rel"][...], gproj[j]))
        r["sums"][j : j + 1] = jnp.sum(gproj[j].astype(f32), axis=0, keepdims=True)
        gh += dot_nt(gproj[j], r["wabs"][j])
    into, grad_gain, grad_shift = norm_grad(gh, r["x"][...], r["vec"][4:5])
    r["gx"][...] = r["gmid"][...] + into
    r["sums"][3:4] = jnp.sum(r["ga"][...].astype(f32), axis=0, keepdims=True)
    r["sums"][4:5] = grad_gain
    r["sums"][5:6] = grad_shift


def attn_backward(slots, gmid, x, vec, cos, sin, saved):
    length, width = x.shape
    spots = saved["h_rel"].shape[1]
    half = spots // slots // 2
    groups = width // 128
    b16, f32 = jnp.bfloat16, jnp.float32

    def body(r):
        step = pl.program_id(0)
        pl.when(step == 0)(lambda: attn_grad_open(r))
        attn_grad_heads(r, step)
        pl.when(step == groups - 1)(lambda: attn_grad_close(r))

    ins = {"gmid": gmid, "x": x, "vec": vec, "cos": cos, "sin": sin}
    for name in ("wabs", "h_rel", "q", "kt", "v", "att_t", "att_rel"):
        ins[name] = saved[name]
    ins = {name: (array, None) for name, array in ins.items()}
    ins["probs"] = (
        saved["probs"],
        pl.BlockSpec((GROUP, length, length), lambda i: (i, 0, 0)),
    )
    split = ((groups, length, 128), b16)
    return call(
        body, "attn_bwd", (groups,), ins,
        {
            "gx": ((length, width), f32, None),
            "kept": ((half, 4, slots, width), b16, None),
            "sent": ((half, 4, slots, width), b16, None),
            "sums": ((8, width), f32, None),
        },
        {
            "ga": ((length, width), b16),
            "gatt": split,
            "qs": split,
            "vs": split,
            "gatt_t": ((width, length), b16),
            "inner": ((HEADS, 1, length), f32),
            "dqt": ((width, length), f32),
            "dk": ((groups, length, 128), f32),
            "dv": ((groups, length, 128), f32),
        },
        30_000_000_000, 30_000_000,
    )


def add_halves(kept, came):
    _, total, width = kept.shape
    steps = 4 if total % 32 == 0 else 1
    rows = total // steps
    both = pl.BlockSpec((4, rows, width), lambda i: (0, i, 0))
    one = pl.BlockSpec((rows, width), lambda i: (i, 0))

    def body(r):
        for part in range(4):
            total_part = r["kept"][part].astype(jnp.float32) + r["came"][part].astype(jnp.float32)
            r[f"h{part}"][...] = total_part.astype(jnp.bfloat16)

    made = call(
        body, "add_halves", (steps,), {"kept": (kept, both), "came": (came, both)},
        {f"h{part}": ((total, width), jnp.bfloat16, one) for part in range(4)}, {},
        10_000_000, 10_000_000,
    )
    return [made[f"h{part}"] for part in range(4)]


def add_plane(own, parts, lines):
    total, width = parts[0].shape
    rows = total // lines
    picked = pl.BlockSpec((1, rows, width), lambda i, own: (i ^ own[3], 0, 0))
    ins = {f"p{n}": (part.reshape(lines, rows, width), picked) for n, part in enumerate(parts)}
    outs = {"own": ((rows, width), jnp.float32, None)}
    for line in range(1, lines):
        outs[f"s{line}"] = ((rows, width), jnp.bfloat16, None)

    def body(r):
        total_part = sum(r[f"p{n}"][0].astype(jnp.float32) for n in range(4))
        step = pl.program_id(0)

        @pl.when(step == 0)
        def _():
            r["own"][...] = total_part

        for line in range(1, lines):

            @pl.when(step == line)
            def _():
                r[f"s{line}"][...] = total_part.astype(jnp.bfloat16)

    made = call(
        body, "add_plane", (lines,), ins, outs, {}, 10_000_000, 5_000_000, prefetch=own
    )
    return (made["own"], [made[f"s{line}"] for line in range(1, lines)])


def shards(
    sizes,
    tokens,
    qkv_weight,
    out_weight,
    proj_bias,
    norm_gain,
    norm_shift,
    up_weight,
    down_weight,
    up_bias,
    seq_order,
    seq_length,
    mlm_mask,
    cotangent,
):
    _, length, width = tokens.shape
    layer_count = qkv_weight.shape[0]
    _, ffn_size, core_size = sizes
    lines = ffn_size // 2
    count = 2 * ffn_size * core_size
    x_bit, y_bit, core_bit, line_unit = ffn_size * core_size, core_size, 1, 2 * core_size
    own_id = lax.axis_index(AXES)
    own_x = (own_id // x_bit) % 2
    own_y = (own_id // y_bit) % 2
    own_core = own_id % 2
    own_line = (own_id // line_unit) % lines
    own = jnp.stack([own_x, own_y, own_core, own_line]).astype(jnp.int32)
    rows = qkv_weight.shape[2]
    slots = pad_rows(rows)
    hidden = up_weight.shape[1]
    b16, f32 = jnp.bfloat16, jnp.float32

    def device(x, y, line, core):
        return (x * ffn_size + line * 2 + y) * core_size + core

    def swap(values, bits):
        return lax.ppermute(values, AXES, [(i, i ^ bits) for i in range(count)])

    def grow(values, bits, axis):
        return jnp.concatenate([values, swap(values, bits)], axis=axis)

    def line_gather(values, axis):
        bit = lines // 2
        while bit:
            came = swap(values, bit * line_unit)
            high = (own_line & bit) > 0
            values = jnp.stack(
                [jnp.where(high, came, values), jnp.where(high, values, came)], axis=axis + 1
            )
            shape = values.shape
            values = values.reshape(shape[:axis] + (shape[axis] * 2,) + shape[axis + 2 :])
            bit //= 2
        return values

    order_ids = jnp.arange(seq_length.shape[0], dtype=jnp.int32)
    slot_length = jnp.sum(jnp.where(seq_order[0] == order_ids, seq_length, 0))
    key_ok = jnp.arange(length, dtype=jnp.int32) < slot_length
    loss_weight = jnp.where(key_ok & (mlm_mask[0] > 0), 1.0, 0.0).astype(f32)
    local_count = jnp.sum(loss_weight)
    count_high = jnp.floor(local_count / 256.0)
    count_low = local_count - 256.0 * count_high
    small_len = 9 * rows + hidden
    def small_row(layer, extra):
        parts = (proj_bias[layer], norm_gain[layer], norm_shift[layer], up_bias[layer])
        row = jnp.concatenate([part.reshape(-1) for part in parts] + extra).astype(b16)
        return jnp.pad(row, (0, width - row.shape[0]))

    def attn_piece(layer, row):
        piece = jnp.concatenate([qkv_weight[layer], out_weight[layer][None]], axis=0)
        spare = jnp.zeros((4, slots - rows, width), b16)
        first = jnp.arange(4 * (slots - rows)).reshape(4, slots - rows, 1) == 0
        spare = jnp.where(first, row[None, None], spare)
        return jnp.concatenate([piece.astype(b16), spare], axis=1)

    def ffn_piece(layer):
        return jnp.stack([up_weight[layer], down_weight[layer]]).astype(b16)

    attn = attn_piece(0, small_row(0, []))
    attn = line_gather(attn[:, None], 1).reshape(4, lines * slots, width)
    part_a = grow(attn[:2], y_bit, 1)
    part_b = grow(attn[2:], x_bit, 1)
    part_a = grow(part_a, x_bit, 1)
    part_b = grow(part_b, y_bit, 1)
    ffn = line_gather(after(ffn_piece(0), attn)[None], 0)
    ffn = after(ffn, part_a, part_b)
    half_a, half_b = (swap(part_a, core_bit), swap(part_b, core_bit))
    up_all = grow(ffn[:, 0].reshape(lines * hidden, width), y_bit, 0)
    down_all = grow(ffn[:, 1].reshape(lines * hidden, width), x_bit, 0)

    late = jnp.concatenate(
        [
            ffn_piece(1).reshape(2 * hidden, width),
            attn_piece(1, small_row(1, [count_high[None], count_low[None]])).reshape(
                4 * slots, width
            ),
        ]
    )
    late = lax.all_gather(after(late, attn), AXES, axis=0, tiled=False)
    late_attn = late[:, 2 * hidden :].reshape(count, 4, slots, width).transpose(1, 0, 2, 3)
    late_attn = late_attn.reshape(4, count * slots, width)
    late = late.reshape(2, lines, 2, 2, late.shape[1], width)
    late_kind = "own" if hidden % 16 else "late"
    late_weights = [(late,), (late,)]
    if late_kind == "own":
        turned = late[:, :, :, :, : 2 * hidden].reshape(2, lines, 2, 2, 2, hidden, width)
        for axis, odd in ((0, own_x), (2, own_y), (3, own_core)):
            turned = jnp.where(odd > 0, jnp.flip(turned, axis), turned)
        late_up = turned[:, :, :, :, 0].transpose(3, 0, 2, 1, 4, 5)
        late_down = turned[:, :, :, :, 1].transpose(3, 2, 0, 1, 4, 5)
        late_weights = [
            (late_up[n].reshape(-1, width), late_down[n].reshape(-1, width)) for n in range(2)
        ]

    index = jnp.arange(count, dtype=jnp.int32)
    line_at = index % lines
    low_at = index // lines % 2
    high_at = index // (2 * lines) % 2
    core_at = (index // (4 * lines)) ^ own_core
    owners_a = device(high_at ^ own_x, low_at ^ own_y, line_at, core_at)
    owners_b = device(low_at ^ own_x, high_at ^ own_y, line_at, core_at)
    slot_ids = jnp.arange(slots, dtype=jnp.int32)

    def spread_of(owners):
        source_row = jnp.where(
            slot_ids[None, :] < rows, owners[:, None] * rows + slot_ids[None, :], -1
        ).reshape(count * slots)
        return (jnp.arange(width, dtype=jnp.int32)[:, None] == source_row[None, :]).astype(b16)

    spread_a, spread_b, spread_d = [spread_of(o) for o in (owners_a, owners_b, index)]
    hot = owners_a[:, None] == index[None, :]
    cos_half, sin_half = rope_tables(length, HEAD_DIM)
    cos = jnp.tile(jnp.concatenate([cos_half, cos_half], axis=1), (1, GROUP))
    sin = jnp.tile(jnp.concatenate([-sin_half, sin_half], axis=1), (1, GROUP))
    mask = jnp.where(key_ok, 0.0, mask_value).astype(f32)[:, None]

    small_own = jnp.concatenate(
        [part[0].reshape(-1, slots, width)[:, rows, :] for part in (part_a, half_a)]
    )
    hot_b16 = hot.astype(b16)
    small_all = dot_tn(hot_b16, small_own)
    late_small = late_attn[0].reshape(count, slots, width)[:, rows, :]
    late_all = late_small.astype(f32)
    late_own = dot_nn(hot_b16, late_small)
    masked_total = jnp.sum(late_all[:, small_len] * 256.0 + late_all[:, small_len + 1])
    factor = seq_length.shape[0] * length / jnp.maximum(masked_total, 1.0)

    vecs, biases = [], []
    for small, spots in ((small_all, small_own), (late_all, late_own)):
        vec = small[:, : 9 * rows].reshape(count, 9, rows).transpose(1, 0, 2).reshape(9, width)
        vec = jnp.concatenate([vec[:4], vec[5:6], vec[7:8], vec[6:7], vec[8:9], vec[4:5]])
        vecs.append(jnp.pad(vec, ((0, 7), (0, 0))))
        bias = spots[:, 9 * rows : small_len]
        biases.append(bias.reshape(count * hidden).astype(f32))

    kinds = ("own", late_kind)
    groups = width // 128
    streams, attns, ffns = [tokens[0]], [], []

    def between(value):
        nonlocal up_all, down_all
        value, up_all, down_all = lax.optimization_barrier((value, up_all, down_all))
        up_all = grow(up_all, x_bit, 0)
        down_all = grow(down_all, y_bit, 0)
        return value

    attns.append(
        attn_forward(
            streams[0],
            {"wa": part_a, "wa2": half_a, "wb": part_b, "wb2": half_b},
            {"sa": spread_a, "sb": spread_b},
            vecs[0], cos, sin, mask, CUT, between,
        )
    )
    attns[0]["mid"], up_all, down_all = lax.optimization_barrier(
        (attns[0]["mid"], up_all, down_all)
    )
    up_came, down_came = (swap(up_all, core_bit), swap(down_all, core_bit))
    weights = [[(up_all, down_all), (up_came, down_came)], late_weights]

    def ffn_front(layer):
        parts = []
        for base in range(2):
            bias = biases[layer][base * 4 * lines * hidden : (base + 1) * 4 * lines * hidden]
            parts.append(
                ffn_forward(
                    own, attns[layer]["mid"], vecs[layer], kinds[layer], weights[layer][base],
                    bias, lines, hidden, base, parts[0] if base else None,
                )
            )
        return parts

    ffns.append(ffn_front(0))
    streams.append(ffns[0][1]["out"])
    half = late_attn.shape[1] // 2
    attns.append(
        attn_forward(
            streams[1],
            {
                "wa": late_attn[:2, :half],
                "wa2": late_attn[:2, half:],
                "wb": late_attn[2:, :half],
                "wb2": late_attn[2:, half:],
            },
            {"sa": spread_d, "sg": spread_a},
            vecs[1], cos, sin, mask, groups, None,
        )
    )
    ffns.append(ffn_front(1))
    result = ffns[1][1]["out"]

    def plane_swap(parts):
        return [parts[0]] + [
            swap(parts[n], n // 2 * x_bit + n % 2 * y_bit) for n in range(1, 4)
        ]

    def line_swap(sends):
        return [swap(send, (n + 1) * line_unit) for n, send in enumerate(sends)]

    def line_sum(own_part, came):
        return own_part + sum(part.astype(f32) for part in came)

    def ffn_back(layer, grad, base, gh_in):
        return ffn_backward(
            own, grad, attns[layer]["mid"], vecs[layer], ffns[layer][base], ffns[layer][0]["h_two"],
            kinds[layer], weights[layer][base], lines, hidden, base, gh_in,
        )

    def attn_back(layer, grad_mid):
        return attn_backward(slots, grad_mid, streams[layer], vecs[layer], cos, sin, attns[layer])

    def flat(values):
        return values.reshape(4, -1, width)

    grad = cotangent[0] * (loss_weight[:, None] * factor)
    one1 = ffn_back(1, grad, 1, None)
    came_f1 = swap(one1["grads"], core_bit)
    two1 = ffn_back(1, grad, 0, one1["gh"])
    halves_f1 = add_halves(flat(two1["grads"]), flat(came_f1))
    plane_f1 = plane_swap(halves_f1)
    attn_g1 = attn_back(1, after(two1["gmid"], *halves_f1))
    came_a1 = swap(attn_g1["sent"], core_bit)
    own_f1, sends_f1 = add_plane(own, plane_f1, lines)
    line_f1 = line_swap(sends_f1)
    grad = after(attn_g1["gx"], own_f1, *sends_f1)
    one0 = ffn_back(0, grad, 1, None)
    came_f0 = swap(one0["grads"], core_bit)
    halves_a1 = add_halves(flat(after(attn_g1["kept"], one0["gh"])), flat(came_a1))
    plane_a1 = plane_swap(halves_a1)
    two0 = ffn_back(0, grad, 0, after(one0["gh"], *halves_a1))
    halves_f0 = add_halves(flat(two0["grads"]), flat(came_f0))
    plane_f0 = plane_swap(halves_f0)
    attn_g0 = attn_back(0, after(two0["gmid"], *halves_f0, *line_f1))
    attn_g0, plane_a1, plane_f0 = lax.optimization_barrier((attn_g0, plane_a1, plane_f0))
    came_a0 = swap(attn_g0["sent"], core_bit)
    own_f0, sends_f0 = add_plane(own, plane_f0, lines)
    line_f0 = line_swap(sends_f0)
    own_a1, sends_a1 = add_plane(own, plane_a1, lines)
    line_a1 = line_swap(sends_a1)
    halves_a0 = add_halves(flat(attn_g0["kept"]), flat(came_a0))
    plane_a0 = plane_swap(halves_a0)
    own_a0, sends_a0 = add_plane(own, plane_a0, lines)
    line_a0 = line_swap(sends_a0)
    ffn_grads = [(two0, one0), (two1, one1)]

    small = []
    for layer, attn_g in ((0, attn_g0), (1, attn_g1)):
        two, one = ffn_grads[layer]
        a, f = attn_g["sums"], two["sums"]
        sums = jnp.concatenate([a[:4], f[2:3], a[4:5], f[0:1], a[5:6], f[1:2]])
        sums = sums.reshape(9, count, rows).transpose(1, 0, 2).reshape(count, 9 * rows)
        sums = jnp.dot(hot.astype(f32), sums, precision=lax.Precision.HIGHEST)
        bias = jnp.concatenate([two["gbias"], one["gbias"]]).reshape(count, hidden)
        small += [sums, bias]
    small = jnp.concatenate(small, axis=1)
    small = small[: count // 2] + swap(small[count // 2 :], core_bit)
    small = small.reshape(4, lines, -1)
    small = sum(plane_swap([small[n] for n in range(4)]))
    picked = [lax.dynamic_index_in_dim(small, own_line ^ n, 0) for n in range(lines)]
    small = (picked[0] + sum(line_swap(picked[1:])))[0].reshape(layer_count, small_len)

    own_attn = jnp.stack([line_sum(own_a0, line_a0), line_sum(own_a1, line_a1)])
    own_attn = own_attn.reshape(layer_count, 4, slots, width)
    own_ffn = jnp.stack([line_sum(own_f0, line_f0), line_sum(own_f1, line_f1)])
    own_ffn = own_ffn.reshape(layer_count, 2, hidden, width)
    return (
        result[None],
        attn_g0["gx"][None],
        own_attn[:, :3, :rows],
        own_attn[:, 3, :rows],
        small[:, : 5 * rows].reshape(layer_count, 5, rows),
        small[:, 5 * rows : 7 * rows].reshape(layer_count, 2, rows),
        small[:, 7 * rows : 9 * rows].reshape(layer_count, 2, rows),
        own_ffn[:, 0],
        own_ffn[:, 1],
        small[:, 9 * rows :],
    )


def solution(mesh):
    in_specs = (
        P(("batch", "ffn", "mp"), None, None),
        P(None, None, ("batch", "ffn", "mp"), None),
        P(None, ("batch", "ffn", "mp"), None),
        P(None, None, ("batch", "ffn", "mp")),
        P(None, None, ("batch", "ffn", "mp")),
        P(None, None, ("batch", "ffn", "mp")),
        P(None, ("batch", "ffn", "mp"), None),
        P(None, ("batch", "ffn", "mp"), None),
        P(None, ("batch", "ffn", "mp")),
        P(("batch", "ffn", "mp")),
        P(),
        P(("batch", "ffn", "mp"), None),
        P(("batch", "ffn", "mp"), None, None),
    )
    out_specs = (
        P(("batch", "ffn", "mp"), None, None),
        P(("batch", "ffn", "mp"), None, None),
        P(None, None, ("batch", "ffn", "mp"), None),
        P(None, ("batch", "ffn", "mp"), None),
        P(None, None, ("batch", "ffn", "mp")),
        P(None, None, ("batch", "ffn", "mp")),
        P(None, None, ("batch", "ffn", "mp")),
        P(None, ("batch", "ffn", "mp"), None),
        P(None, ("batch", "ffn", "mp"), None),
        P(None, ("batch", "ffn", "mp")),
    )
    sizes = tuple(mesh.shape[name] for name in AXES)
    return jax.shard_map(partial(shards, sizes), mesh=mesh, in_specs=in_specs, out_specs=out_specs, check_vma=False)
```

```python
from functools import partial
import math
from types import SimpleNamespace

import jax
import jax.numpy as jnp
from jax import lax
from jax.experimental import pallas as pl
from jax.experimental.pallas import tpu as pltpu
from jax.sharding import PartitionSpec as P

HEADS = 20
HEAD_DIM = 32


norm_eps = 1e-05
mask_value = -1e30


def rope_tables(length, head_width):
    half_width = head_width // 2
    freqs = jnp.exp(
        jnp.arange(half_width, dtype=jnp.float32) * (-2.0 * math.log(10000.0) / head_width)
    )
    angles = jnp.arange(length, dtype=jnp.float32)[:, None] * freqs[None, :]
    return (jnp.cos(angles), jnp.sin(angles))


AXES = ("batch", "ffn", "mp")
CUT = 2


def after(value, *others):
    return lax.optimization_barrier((value, *others))[0]


def pad_rows(rows):
    return -(-(rows + 1) // 8) * 8


GROUP = 128 // HEAD_DIM
VMEM_LIMIT = 56 * 1024 * 1024


def dot_nn(left, right):
    return lax.dot_general(
        left, right, (((1,), (0,)), ((), ())), preferred_element_type=jnp.float32
    )


def dot_nt(left, right):
    return lax.dot_general(
        left, right, (((1,), (1,)), ((), ())), preferred_element_type=jnp.float32
    )


def dot_tn(left, right):
    return lax.dot_general(
        left, right, (((0,), (0,)), ((), ())), preferred_element_type=jnp.float32
    )


def norm_parts(values):
    centred = values - jnp.mean(values, axis=-1, keepdims=True)
    variance = jnp.mean(centred * centred, axis=-1, keepdims=True)
    inverse = lax.rsqrt(variance + norm_eps)
    return (centred * inverse, inverse)


def norm_grad(grad, values, gain_row):
    unit, inverse = norm_parts(values)
    scaled = grad * gain_row
    mean_one = jnp.mean(scaled, axis=-1, keepdims=True)
    mean_two = jnp.mean(scaled * unit, axis=-1, keepdims=True)
    into = inverse * (scaled - mean_one - unit * mean_two)
    grad_gain = jnp.sum(grad * unit, axis=0, keepdims=True)
    grad_shift = jnp.sum(grad, axis=0, keepdims=True)
    return (into, grad_gain, grad_shift)


def turn(values, cos_ref, sin_ref, sign):
    half = HEAD_DIM // 2
    lanes = lax.broadcasted_iota(jnp.int32, (values.shape[0], 128), 1)
    low_half = lanes % HEAD_DIM < half
    parts = []
    for start in range(0, values.shape[1], 128):
        part = values[:, start : start + 128]
        partner = jnp.where(
            low_half, pltpu.roll(part, 128 - half, 1), pltpu.roll(part, half, 1)
        )
        parts.append(part * cos_ref[...] + sign * (partner * sin_ref[...]))
    return jnp.concatenate(parts, axis=1)


def head_lanes(block, head):
    lanes = lax.broadcasted_iota(jnp.int32, block.shape, 1)
    return jnp.where(lanes // HEAD_DIM == head, block, jnp.zeros_like(block))


def sds(shape, dtype):
    return jax.ShapeDtypeStruct(shape, dtype)


def whole(shape):
    return pl.BlockSpec(shape, lambda *_: (0,) * len(shape))


def call(body, name, grid, ins, outs, scratch, flops, moved, prefetch=None, aliases=None):
    names = list(ins) + list(outs) + list(scratch)
    lead = 0 if prefetch is None else 1

    def kernel(*refs):
        body(SimpleNamespace(**dict(zip(names, refs[lead:]))))

    in_specs = [spec or whole(array.shape) for array, spec in ins.values()]
    out_specs = [spec or whole(shape) for shape, _, spec in outs.values()]
    out_shape = [sds(shape, dtype) for shape, dtype, _ in outs.values()]
    scratch_shapes = [pltpu.VMEM(shape, dtype) for shape, dtype in scratch.values()]
    operands = ([] if prefetch is None else [prefetch]) + [array for array, _ in ins.values()]
    in_names, out_names = list(ins), list(outs)
    pairs = {
        in_names.index(a) + lead: out_names.index(b) for a, b in (aliases or {}).items()
    }
    results = pl.pallas_call(
        kernel,
        grid_spec=pltpu.PrefetchScalarGridSpec(
            num_scalar_prefetch=lead,
            grid=grid,
            in_specs=in_specs,
            out_specs=out_specs,
            scratch_shapes=scratch_shapes,
        ),
        out_shape=out_shape,
        input_output_aliases=pairs,
        compiler_params=pltpu.CompilerParams(vmem_limit_bytes=VMEM_LIMIT),
        cost_estimate=pl.CostEstimate(flops=flops, bytes_accessed=moved, transcendentals=0),
        name=name,
    )(*operands)
    return SimpleNamespace(**dict(zip(out_names, results)))


def attn_open(r):
    unit, _ = norm_parts(r.x[...])
    h_one = (unit * r.vec[4:5] + r.vec[5:6]).astype(jnp.bfloat16)
    r.h_rel[...] = dot_nn(h_one, (r.sg if hasattr(r, "sg") else r.sa)[...]).astype(jnp.bfloat16)
    wabs = r.wabs
    half = r.wa.shape[1]
    for j in range(4):
        spread = r.sa if j < 2 or not hasattr(r, "sb") else r.sb
        own, came = (r.wa, r.wa2) if j < 2 else (r.wb, r.wb2)
        placed = dot_nn(spread[:, :half], own[j % 2])
        placed += dot_nn(spread[:, half:], came[j % 2])
        wabs[j] = placed.astype(jnp.bfloat16)
    query = dot_nn(h_one, wabs[0]) + r.vec[0:1]
    query = turn(query, r.cos, r.sin, 1.0) * HEAD_DIM ** (-0.5)
    r.q[...] = query.astype(jnp.bfloat16)
    r.qt[...] = query.T.astype(jnp.bfloat16)
    key = turn(dot_nn(h_one, wabs[1]) + r.vec[1:2], r.cos, r.sin, 1.0)
    key_bf = key.astype(jnp.bfloat16)
    for start in range(key.shape[1] // 128):
        r.k[start] = key_bf[:, 128 * start : 128 * start + 128]
    r.kt[...] = key.T.astype(jnp.bfloat16)
    value = dot_nn(h_one, wabs[2]) + r.vec[2:3]
    r.v[...] = value.astype(jnp.bfloat16)
    r.vt[...] = value.T.astype(jnp.bfloat16)


def attn_heads(r, group):
    key_block = r.k[group]
    query_t = r.qt[pl.ds(pl.multiple_of(group * 128, 128), 128), :]
    for head in range(GROUP):
        scores = dot_nn(head_lanes(key_block, head), query_t) + r.mask[...]
        top = jnp.max(scores, axis=0, keepdims=True)
        shifted = jnp.exp(scores - top)
        total = jnp.sum(shifted, axis=0, keepdims=True)
        probs = (shifted * (1.0 / total)).astype(jnp.bfloat16)
        r.probs[head] = probs
        rows = pl.ds(pl.multiple_of(group * 128 + head * HEAD_DIM, HEAD_DIM), HEAD_DIM)
        r.att_t[rows, :] = dot_nn(r.vt[rows, :], probs)


def attn_close(r):
    att = r.att_t[...].T.astype(jnp.bfloat16)
    r.att_rel[...] = dot_nn(att, (r.sg if hasattr(r, "sg") else r.sa)[...]).astype(jnp.bfloat16)
    r.mid[...] = r.x[...] + (dot_nn(att, r.wabs[3]) + r.vec[3:4])


def attn_forward(x, parts, spreads, vec, cos, sin, mask, cut, between):
    length, width = x.shape
    spots = spreads["sa"].shape[1]
    groups = width // 128
    b16, f32 = jnp.bfloat16, jnp.float32
    opening = dict(x=x, **parts, **spreads)
    tables = dict(vec=vec, cos=cos, sin=sin, mask=mask)
    made = dict(
        wabs=((4, width, width), b16, None),
        h_rel=((length, spots), b16, None),
        q=((length, width), b16, None),
        kt=((width, length), b16, None),
        v=((length, width), b16, None),
    )
    work = dict(
        qt=((width, length), b16),
        k=((groups, length, 128), b16),
        vt=((width, length), b16),
    )
    att_t = dict(att_t=((width, length), f32, None))
    closing = dict(att_rel=((length, spots), b16, None), mid=((length, width), f32, None))

    def probs_out(base):
        spec = pl.BlockSpec((GROUP, length, length), lambda i: (i + base, 0, 0))
        return dict(probs=((HEADS, length, length), b16, spec))

    def plain(arrays):
        return {name: (array, None) for name, array in arrays.items()}

    def body(first, last, base, steps):
        def run(r):
            step = pl.program_id(0)
            if first:
                pl.when(step == 0)(lambda: attn_open(r))
            else:

                @pl.when(step == 0)
                def _():
                    r.att_t[: base * 128, :] = r.att_in[: base * 128, :]

            attn_heads(r, step + base)
            if last:
                pl.when(step == steps - 1)(lambda: attn_close(r))

        return run

    if cut == groups:
        return call(
            body(True, True, 0, groups), "attn_fwd", (groups,),
            plain({**opening, **tables}), {**made, **att_t, **closing, **probs_out(0)}, work,
            20_000_000_000, 25_000_000,
        )
    shared = {name: (shape, dtype, None) for name, (shape, dtype) in work.items()}
    one = call(
        body(True, False, 0, cut), "attn_fwd_one", (cut,),
        plain({**opening, **tables}), {**made, **att_t, **shared, **probs_out(0)}, {},
        10_000_000_000, 15_000_000,
    )
    att_in = between(one.att_t)
    ins = plain(
        dict(
            x=x, sa=spreads["sa"], vec=vec, mask=mask, wabs=one.wabs, att_in=att_in,
            qt=one.qt, k=one.k, vt=one.vt,
        )
    )
    ins.update(probs_in=(one.probs, pl.BlockSpec(memory_space=pl.ANY)))
    two = call(
        body(False, True, cut, groups - cut), "attn_fwd_two", (groups - cut,),
        ins, {**att_t, **closing, **probs_out(cut)}, {},
        10_000_000_000, 15_000_000, aliases=dict(probs_in="probs"),
    )
    return SimpleNamespace(**{**vars(one), **vars(two)})


def ffn_specs(kind, arrays, base, hidden, lines, width):
    specs = {}
    if kind == "own":
        shape = (lines * hidden, width)
        for y in range(2):
            specs["up" + str(y)] = (arrays[0], pl.BlockSpec(shape, lambda i, own, y=y: (2 * i + y, 0)))
            specs["down" + str(y)] = (arrays[1], pl.BlockSpec(shape, lambda i, own, y=y: (2 * y + i, 0)))
        return specs
    shape = (1, lines, 1, 1, hidden, width)
    for which, name in enumerate(("up", "down")):
        for y in range(2):

            def index(i, own, y=y, which=which):
                return (i ^ own[0], 0, y ^ own[1], base ^ own[2], which, 0)

            specs[name + str(y)] = (arrays[0], pl.BlockSpec(shape, index))
    return specs


def rows_of(ref):
    values = ref[...]
    return values.reshape(-1, values.shape[-1])


def ffn_forward(own, mid, vec, kind, arrays, bias, lines, hidden, base, before):
    length, width = mid.shape
    block = lines * hidden
    b16 = jnp.bfloat16
    kept = pl.BlockSpec((2, length, block), lambda i, own: (i, 0, 0))

    def body(r):
        h_two = r.h_two if before is None else r.h_in

        @pl.when(pl.program_id(0) == 0)
        def _():
            if before is None:
                unit, _ = norm_parts(r.mid[...])
                h_two[...] = (unit * r.vec[6:7] + r.vec[7:8]).astype(b16)
                r.out[...] = r.mid[...] + r.vec[8:9]
            else:
                r.out[...] = r.so_far[...]

        for y in range(2):
            pre = dot_nt(h_two[...], rows_of((r.up0, r.up1)[y])) + r.bias[y]
            cdf = 0.5 * (1.0 + lax.erf(pre * (0.5**0.5)))
            act = (pre * cdf).astype(b16)
            r.act[y] = act
            slope = cdf + pre * (jnp.exp(-0.5 * pre * pre) * (1.0 / math.sqrt(2.0 * math.pi)))
            r.slope[y] = slope.astype(b16)
            r.out[...] += dot_nn(act, rows_of((r.down0, r.down1)[y]))

    ins = {
        **ffn_specs(kind, arrays, base, hidden, lines, width),
    }
    ins.update(
        bias=(
            bias.reshape(4, 1, block),
            pl.BlockSpec((2, 1, block), lambda i, own: (i, 0, 0)),
        ),
    )
    outs = dict(
        out=((length, width), jnp.float32, None),
        act=((4, length, block), b16, kept),
        slope=((4, length, block), b16, kept),
    )
    if before is None:
        ins.update(mid=(mid, None), vec=(vec, None))
        outs.update(h_two=((length, width), b16, None))
    else:
        ins.update(h_in=(before.h_two, None), so_far=(before.out, None))
    name = "ffn_fwd_one" if before is None else "ffn_fwd_two"
    return call(body, name, (2,), ins, outs, {}, 5_000_000_000, 10_000_000, prefetch=own)


def ffn_backward(own, grad, mid, vec, kept, h_two, kind, arrays, lines, hidden, base, gh_in):
    length, width = mid.shape
    block = lines * hidden
    b16, f32 = jnp.bfloat16, jnp.float32
    last = gh_in is not None
    wide = pl.BlockSpec((2, length, block), lambda i, own: (i, 0, 0))

    def body(r):
        @pl.when(pl.program_id(0) == 0)
        def _():
            r.gf[...] = r.g[...].astype(b16)
            r.gh[...] = r.gh_in[...] if last else jnp.zeros_like(r.gh)

        gf = r.gf[...]
        for y in range(2):
            g_down = dot_tn(r.act[y], gf)
            g_act = dot_nt(gf, rows_of((r.down0, r.down1)[y]))
            g_pre = (g_act * r.slope[y].astype(f32)).astype(b16)
            g_up = dot_tn(g_pre, r.h_two[...])
            for line in range(lines):
                rows = slice(line * hidden, (line + 1) * hidden)
                r.grads[0, y, line, 0] = g_up[rows].astype(b16)
                r.grads[0, y, line, 1] = g_down[rows].astype(b16)
            r.gbias[y] = jnp.sum(g_pre.astype(f32), axis=0, keepdims=True)
            r.gh[...] += dot_nn(g_pre, rows_of((r.up0, r.up1)[y]))
        if last:

            @pl.when(pl.program_id(0) == 1)
            def _():
                into, grad_gain, grad_shift = norm_grad(
                    r.gh[...], r.mid[...], r.vec[6:7]
                )
                r.gmid[...] = r.g[...] + into
                r.sums[...] = jnp.zeros_like(r.sums)
                r.sums[0:1] = grad_gain
                r.sums[1:2] = grad_shift
                r.sums[2:3] = jnp.sum(r.gf[...].astype(f32), axis=0, keepdims=True)

    ins = dict(
        g=(grad, None),
        h_two=(h_two, None),
        act=(kept.act, wide),
        slope=(kept.slope, wide),
        **ffn_specs(kind, arrays, base, hidden, lines, width),
    )
    outs = dict(
        grads=(
            (2, 2, lines, 2, hidden, width),
            b16,
            pl.BlockSpec((1, 2, lines, 2, hidden, width), lambda i, own: (i, 0, 0, 0, 0, 0)),
        ),
        gbias=((4, 1, block), f32, pl.BlockSpec((2, 1, block), lambda i, own: (i, 0, 0))),
    )
    scratch = dict(gf=((length, width), b16))
    if last:
        ins.update(gh_in=(gh_in, None), mid=(mid, None), vec=(vec, None))
        outs.update(gmid=((length, width), f32, None), sums=((8, width), f32, None))
        scratch.update(gh=((length, width), f32))
    else:
        outs.update(gh=((length, width), f32, None))
    name = "ffn_bwd_two" if last else "ffn_bwd_one"
    return call(body, name, (2,), ins, outs, scratch, 9_000_000_000, 15_000_000, prefetch=own)


def put_pieces(r, index, values):
    count, _, slots, _ = r.kept.shape
    for piece in range(2 * count):
        ref = r.kept if piece < count else r.sent
        ref[piece % count, index] = values[piece * slots : (piece + 1) * slots].astype(ref.dtype)


def attn_grad_open(r):
    b16 = jnp.bfloat16
    r.ga[...] = r.gmid[...].astype(b16)
    put_pieces(r, 3, dot_tn(r.att_rel[...], r.ga[...]))
    gatt = dot_nt(r.ga[...], r.wabs[3]).astype(b16)
    for start in range(gatt.shape[1] // 128):
        lanes = slice(128 * start, 128 * start + 128)
        r.gatt[start] = gatt[:, lanes]
        r.qs[start] = r.q[:, lanes]
        r.vs[start] = r.v[:, lanes]
    gatt_t = gatt.astype(jnp.float32).T
    r.gatt_t[...] = gatt_t.astype(b16)
    for head in range(HEADS):
        rows = slice(head * HEAD_DIM, (head + 1) * HEAD_DIM)
        r.inner[head] = jnp.sum(gatt_t[rows] * r.att_t[rows], axis=0, keepdims=True)


def attn_grad_heads(r, group):
    gatt_block, q_block, v_block = r.gatt[group], r.qs[group], r.vs[group]
    gatt_t = r.gatt_t[pl.ds(pl.multiple_of(group * 128, 128), 128), :]
    dk = jnp.zeros(q_block.shape, jnp.float32)
    dv = jnp.zeros(q_block.shape, jnp.float32)
    for head in range(GROUP):
        probs = r.probs[head]
        gprobs = dot_nn(head_lanes(v_block, head), gatt_t)
        inner = r.inner[group * GROUP + head]
        gscores = (probs.astype(jnp.float32) * (gprobs - inner)).astype(jnp.bfloat16)
        dv += dot_nn(probs, head_lanes(gatt_block, head))
        dk += dot_nn(gscores, head_lanes(q_block, head))
        rows = pl.ds(pl.multiple_of(group * 128 + head * HEAD_DIM, HEAD_DIM), HEAD_DIM)
        r.dqt[rows, :] = dot_nn(r.kt[rows, :], gscores)
    r.dk[group] = dk
    r.dv[group] = dv


def attn_grad_close(r):
    b16, f32 = jnp.bfloat16, jnp.float32

    def joined(ref):
        return jnp.concatenate([ref[i] for i in range(ref.shape[0])], axis=1)

    def rounded(values):
        return values.astype(b16).astype(f32)

    gq = rounded(r.dqt[...].T) * HEAD_DIM ** (-0.5)
    gproj = [
        turn(gq, r.cos, r.sin, -1.0).astype(b16),
        turn(rounded(joined(r.dk)), r.cos, r.sin, -1.0).astype(b16),
        joined(r.dv).astype(b16),
    ]
    r.sums[...] = jnp.zeros_like(r.sums)
    gh = jnp.zeros(r.gx.shape, f32)
    for j in range(3):
        put_pieces(r, j, dot_tn(r.h_rel[...], gproj[j]))
        r.sums[j : j + 1] = jnp.sum(gproj[j].astype(f32), axis=0, keepdims=True)
        gh += dot_nt(gproj[j], r.wabs[j])
    into, grad_gain, grad_shift = norm_grad(gh, r.x[...], r.vec[4:5])
    r.gx[...] = r.gmid[...] + into
    r.sums[3:4] = jnp.sum(r.ga[...].astype(f32), axis=0, keepdims=True)
    r.sums[4:5] = grad_gain
    r.sums[5:6] = grad_shift


def attn_backward(slots, gmid, x, vec, cos, sin, saved):
    length, width = x.shape
    spots = saved.h_rel.shape[1]
    half = spots // slots // 2
    groups = width // 128
    b16, f32 = jnp.bfloat16, jnp.float32

    def body(r):
        step = pl.program_id(0)
        pl.when(step == 0)(lambda: attn_grad_open(r))
        attn_grad_heads(r, step)
        pl.when(step == groups - 1)(lambda: attn_grad_close(r))

    full = dict(
        gmid=gmid, x=x, vec=vec, cos=cos, sin=sin, wabs=saved.wabs, h_rel=saved.h_rel,
        q=saved.q, kt=saved.kt, v=saved.v, att_t=saved.att_t, att_rel=saved.att_rel,
    )
    ins = {name: (array, None) for name, array in full.items()}
    ins.update(
        probs=(saved.probs, pl.BlockSpec((GROUP, length, length), lambda i: (i, 0, 0)))
    )
    split = ((groups, length, 128), b16)
    sums = ((groups, length, 128), f32)
    return call(
        body, "attn_bwd", (groups,), ins,
        dict(
            gx=((length, width), f32, None),
            kept=((half, 4, slots, width), b16, None),
            sent=((half, 4, slots, width), b16, None),
            sums=((8, width), f32, None),
        ),
        dict(
            ga=((length, width), b16),
            gatt=split,
            qs=split,
            vs=split,
            gatt_t=((width, length), b16),
            inner=((HEADS, 1, length), f32),
            dqt=((width, length), f32),
            dk=sums,
            dv=sums,
        ),
        30_000_000_000, 30_000_000,
    )


def total_of(one, two):
    return one.astype(jnp.float32) + two.astype(jnp.float32)


def add_core(kept, came):
    _, _, lines, _, rows, width = kept.shape
    b16 = jnp.bfloat16
    both = pl.BlockSpec((2, 2, 1, 2, rows, width), lambda i: (0, 0, i, 0, 0, 0))
    one = ((2, lines, rows, width), b16, pl.BlockSpec((2, 1, rows, width), lambda i: (0, i, 0, 0)))

    def body(r):
        for n in range(2):
            r.ak[n, 0] = total_of(r.kept[0, n, 0, 0], r.came[0, n, 0, 0]).astype(b16)
            r.at[n, 0] = total_of(r.kept[1, n, 0, 0], r.came[1, n, 0, 0]).astype(b16)
            r.bk[n, 0] = total_of(r.kept[n, 0, 0, 1], r.came[n, 0, 0, 1]).astype(b16)
            r.bt[n, 0] = total_of(r.kept[n, 1, 0, 1], r.came[n, 1, 0, 1]).astype(b16)

    made = call(
        body, "add_core", (lines,), dict(kept=(kept, both), came=(came, both)),
        dict(ak=one, at=one, bk=one, bt=one), {}, 10_000_000, 10_000_000,
    )
    return (made.ak, made.at, made.bk, made.bt)


def add_first(ak, ac, bk, bc):
    _, lines, rows, width = ak.shape
    b16 = jnp.bfloat16
    steps = max(1, lines // 2)
    block = lines // steps
    both = pl.BlockSpec((2, block, rows, width), lambda i: (0, i, 0, 0))
    one = ((lines, rows, width), b16, pl.BlockSpec((block, rows, width), lambda i: (i, 0, 0)))

    def body(r):
        r.a0[...] = total_of(r.ak[0], r.ac[0]).astype(b16)
        r.a1[...] = total_of(r.ak[1], r.ac[1]).astype(b16)
        r.b0[...] = total_of(r.bk[0], r.bc[0]).astype(b16)
        r.b1[...] = total_of(r.bk[1], r.bc[1]).astype(b16)

    made = call(
        body, "add_first", (steps,),
        dict(ak=(ak, both), ac=(ac, both), bk=(bk, both), bc=(bc, both)),
        dict(a0=one, a1=one, b0=one, b1=one), {}, 10_000_000, 10_000_000,
    )
    return (made.a0, made.a1, made.b0, made.b1)


def add_second(own, ak, ac, bk, bc):
    lines, rows, width = ak.shape
    b16 = jnp.bfloat16
    half = lines // 2

    def place(i):
        order, unit, left = 0, 1, half
        while left:
            order += (i // left % 2) * unit
            unit, left = unit * 2, left // 2
        return order

    picked = pl.BlockSpec((1, rows, width), lambda i, own: (place(i) ^ own[3], 0, 0))
    shape = (half, 2, rows, width)
    low = pl.BlockSpec((1, 2, rows, width), lambda i, own: (jnp.minimum(i, half - 1), 0, 0, 0))
    high = pl.BlockSpec((1, 2, rows, width), lambda i, own: (jnp.maximum(i - half, 0), 0, 0, 0))

    def body(r):
        part_a = total_of(r.ak[0], r.ac[0]).astype(b16)
        part_b = total_of(r.bk[0], r.bc[0]).astype(b16)

        @pl.when(pl.program_id(0) < half)
        def _():
            r.kept[0, 0] = part_a
            r.kept[0, 1] = part_b

        @pl.when(pl.program_id(0) >= half)
        def _():
            r.sent[0, 0] = part_a
            r.sent[0, 1] = part_b

    made = call(
        body, "add_second", (lines,),
        dict(ak=(ak, picked), ac=(ac, picked), bk=(bk, picked), bc=(bc, picked)),
        dict(kept=(shape, b16, low), sent=(shape, b16, high)), {},
        10_000_000, 5_000_000, prefetch=own,
    )
    return (made.kept, made.sent)


def add_line(kept, came):
    half, _, rows, width = kept.shape
    shape = (half // 2, 2, rows, width)

    def body(r):
        total = total_of(r.kept[...], r.came[...])
        r.low[...] = total[: half // 2]
        r.high[...] = total[half // 2 :].astype(jnp.bfloat16)

    made = call(
        body, "add_line", (1,), dict(kept=(kept, None), came=(came, None)),
        dict(low=(shape, jnp.float32, None), high=(shape, jnp.bfloat16, None)), {},
        10_000_000, 2_000_000,
    )
    return (made.low, made.high)


def shards(
    sizes,
    tokens,
    qkv_weight,
    out_weight,
    proj_bias,
    norm_gain,
    norm_shift,
    up_weight,
    down_weight,
    up_bias,
    seq_order,
    seq_length,
    mlm_mask,
    cotangent,
):
    _, length, width = tokens.shape
    layer_count = qkv_weight.shape[0]
    _, ffn_size, core_size = sizes
    lines = ffn_size // 2
    count = 2 * ffn_size * core_size
    x_bit, y_bit, core_bit, line_unit = ffn_size * core_size, core_size, 1, 2 * core_size
    own_id = lax.axis_index(AXES)
    own_x = (own_id // x_bit) % 2
    own_y = (own_id // y_bit) % 2
    own_core = own_id % 2
    own_line = (own_id // line_unit) % lines
    own = jnp.stack([own_x, own_y, own_core, own_line]).astype(jnp.int32)
    rows = qkv_weight.shape[2]
    slots = pad_rows(rows)
    hidden = up_weight.shape[1]
    b16, f32 = jnp.bfloat16, jnp.float32

    def device(x, y, line, core):
        return (x * ffn_size + line * 2 + y) * core_size + core

    def swap(values, bits):
        return lax.ppermute(values, AXES, [(i, i ^ bits) for i in range(count)])

    def grow(values, bits, axis):
        return jnp.concatenate([values, swap(values, bits)], axis=axis)

    def line_gather(values, axis):
        bit = lines // 2
        while bit:
            came = swap(values, bit * line_unit)
            high = (own_line & bit) > 0
            values = jnp.stack(
                [jnp.where(high, came, values), jnp.where(high, values, came)], axis=axis + 1
            )
            shape = values.shape
            values = values.reshape(shape[:axis] + (shape[axis] * 2,) + shape[axis + 2 :])
            bit //= 2
        return values

    order_ids = jnp.arange(seq_length.shape[0], dtype=jnp.int32)
    slot_length = jnp.sum(jnp.where(seq_order[0] == order_ids, seq_length, 0))
    key_ok = jnp.arange(length, dtype=jnp.int32) < slot_length
    loss_weight = jnp.where(key_ok & (mlm_mask[0] > 0), 1.0, 0.0).astype(f32)
    local_count = jnp.sum(loss_weight)
    count_high = jnp.floor(local_count / 256.0)
    count_low = local_count - 256.0 * count_high
    small_len = 9 * rows + hidden
    def small_row(layer, extra):
        parts = (proj_bias[layer], norm_gain[layer], norm_shift[layer], up_bias[layer])
        row = jnp.concatenate([part.reshape(-1) for part in parts] + extra).astype(b16)
        return jnp.pad(row, (0, width - row.shape[0]))

    def attn_piece(layer, row):
        piece = jnp.concatenate([qkv_weight[layer], out_weight[layer][None]], axis=0)
        spare = jnp.zeros((4, slots - rows, width), b16)
        first = jnp.arange(4 * (slots - rows)).reshape(4, slots - rows, 1) == 0
        spare = jnp.where(first, row[None, None], spare)
        return jnp.concatenate([piece.astype(b16), spare], axis=1)

    def ffn_piece(layer):
        return jnp.stack([up_weight[layer], down_weight[layer]]).astype(b16)

    attn = attn_piece(0, small_row(0, []))
    attn = line_gather(attn[:, None], 1).reshape(4, lines * slots, width)
    part_a = grow(attn[:2], y_bit, 1)
    part_b = grow(attn[2:], x_bit, 1)
    part_a = grow(part_a, x_bit, 1)
    part_b = grow(part_b, y_bit, 1)
    ffn = line_gather(after(ffn_piece(0), attn)[None], 0)
    ffn = after(ffn, part_a, part_b)
    half_a, half_b = (swap(part_a, core_bit), swap(part_b, core_bit))
    up_all = ffn[:, 0].reshape(lines * hidden, width)
    down_all = ffn[:, 1].reshape(lines * hidden, width)
    up_came, down_came = (swap(up_all, y_bit), swap(down_all, x_bit))

    late = jnp.concatenate(
        [
            ffn_piece(1).reshape(2 * hidden, width),
            attn_piece(1, small_row(1, [count_high[None], count_low[None]])).reshape(
                4 * slots, width
            ),
        ]
    )
    late = lax.all_gather(after(late, attn), AXES, axis=0, tiled=False)
    late_attn = late[:, 2 * hidden :].reshape(count, 4, slots, width).transpose(1, 0, 2, 3)
    late_attn = late_attn.reshape(4, count * slots, width)
    late = late.reshape(2, lines, 2, 2, late.shape[1], width)
    late_kind = "own" if hidden % 16 else "late"
    late_weights = [(late,), (late,)]
    if late_kind == "own":
        turned = late[:, :, :, :, : 2 * hidden].reshape(2, lines, 2, 2, 2, hidden, width)
        for axis, odd in ((0, own_x), (2, own_y), (3, own_core)):
            turned = jnp.where(odd > 0, jnp.flip(turned, axis), turned)
        late_up = turned[:, :, :, :, 0].transpose(3, 0, 2, 1, 4, 5)
        late_down = turned[:, :, :, :, 1].transpose(3, 2, 0, 1, 4, 5)
        late_weights = [
            (late_up[n].reshape(-1, width), late_down[n].reshape(-1, width)) for n in range(2)
        ]

    index = jnp.arange(count, dtype=jnp.int32)
    line_at = index % lines
    low_at = index // lines % 2
    high_at = index // (2 * lines) % 2
    core_at = (index // (4 * lines)) ^ own_core
    owners_a = device(high_at ^ own_x, low_at ^ own_y, line_at, core_at)
    owners_b = device(low_at ^ own_x, high_at ^ own_y, line_at, core_at)
    slot_ids = jnp.arange(slots, dtype=jnp.int32)

    def spread_of(owners):
        source_row = jnp.where(
            slot_ids[None, :] < rows, owners[:, None] * rows + slot_ids[None, :], -1
        ).reshape(count * slots)
        return (jnp.arange(width, dtype=jnp.int32)[:, None] == source_row[None, :]).astype(b16)

    spread_a, spread_b, spread_d = [spread_of(o) for o in (owners_a, owners_b, index)]
    hot = owners_a[:, None] == index[None, :]
    cos_half, sin_half = rope_tables(length, HEAD_DIM)
    cos = jnp.tile(jnp.concatenate([cos_half, cos_half], axis=1), (1, GROUP))
    sin = jnp.tile(jnp.concatenate([-sin_half, sin_half], axis=1), (1, GROUP))
    mask = jnp.where(key_ok, 0.0, mask_value).astype(f32)[:, None]

    small_own = jnp.concatenate(
        [part[0].reshape(-1, slots, width)[:, rows, :] for part in (part_a, half_a)]
    )
    hot_b16 = hot.astype(b16)
    small_all = dot_tn(hot_b16, small_own)
    late_small = late_attn[0].reshape(count, slots, width)[:, rows, :]
    late_all = late_small.astype(f32)
    late_own = dot_nn(hot_b16, late_small)
    masked_total = jnp.sum(late_all[:, small_len] * 256.0 + late_all[:, small_len + 1])
    factor = seq_length.shape[0] * length / jnp.maximum(masked_total, 1.0)

    vecs, biases = [], []
    for small, spots in ((small_all, small_own), (late_all, late_own)):
        vec = small[:, : 9 * rows].reshape(count, 9, rows).transpose(1, 0, 2).reshape(9, width)
        vec = jnp.concatenate([vec[:4], vec[5:6], vec[7:8], vec[6:7], vec[8:9], vec[4:5]])
        vecs.append(jnp.pad(vec, ((0, 7), (0, 0))))
        bias = spots[:, 9 * rows : small_len]
        biases.append(bias.reshape(count * hidden).astype(f32))

    kinds = ("own", late_kind)
    groups = width // 128
    streams, attns, ffns = [tokens[0]], [], []

    def between(value):
        nonlocal up_all, down_all, up_came, down_came
        value, up_came, down_came = lax.optimization_barrier((value, up_came, down_came))
        up_all = jnp.concatenate([up_all, up_came])
        down_all = jnp.concatenate([down_all, down_came])
        up_came, down_came = (swap(up_all, x_bit), swap(down_all, y_bit))
        return value

    attns.append(
        attn_forward(
            streams[0],
            dict(wa=part_a, wa2=half_a, wb=part_b, wb2=half_b),
            dict(sa=spread_a, sb=spread_b),
            vecs[0], cos, sin, mask, CUT, between,
        )
    )
    attns[0].mid, up_came, down_came = lax.optimization_barrier(
        (attns[0].mid, up_came, down_came)
    )
    up_all = jnp.concatenate([up_all, up_came])
    down_all = jnp.concatenate([down_all, down_came])
    up_came, down_came = (swap(up_all, core_bit), swap(down_all, core_bit))
    weights = [[(up_all, down_all), (up_came, down_came)], late_weights]

    def ffn_front(layer):
        parts = []
        for base in range(2):
            bias = biases[layer][base * 4 * lines * hidden : (base + 1) * 4 * lines * hidden]
            parts.append(
                ffn_forward(
                    own, attns[layer].mid, vecs[layer], kinds[layer], weights[layer][base],
                    bias, lines, hidden, base, parts[0] if base else None,
                )
            )
        return parts

    ffns.append(ffn_front(0))
    streams.append(ffns[0][1].out)
    half = late_attn.shape[1] // 2
    attns.append(
        attn_forward(
            streams[1],
            dict(
                wa=late_attn[:2, :half],
                wa2=late_attn[:2, half:],
                wb=late_attn[2:, :half],
                wb2=late_attn[2:, half:],
            ),
            dict(sa=spread_d, sg=spread_a),
            vecs[1], cos, sin, mask, groups, None,
        )
    )
    ffns.append(ffn_front(1))
    result = ffns[1][1].out

    def ffn_back(layer, grad, base, gh_in):
        return ffn_backward(
            own, grad, attns[layer].mid, vecs[layer], ffns[layer][base], ffns[layer][0].h_two,
            kinds[layer], weights[layer][base], lines, hidden, base, gh_in,
        )

    def attn_back(layer, grad_mid):
        return attn_backward(slots, grad_mid, streams[layer], vecs[layer], cos, sin, attns[layer])

    def hold(value, *others):
        return lax.optimization_barrier((value, *others))

    def core_step(kept, sent):
        return (kept, swap(sent, core_bit))

    def first_step(kept, came):
        ak, at, bk, bt = add_core(kept, came)
        return (ak, swap(at, x_bit), bk, swap(bt, y_bit))

    def second_step(*parts):
        a0, a1, b0, b1 = add_first(*parts)
        return (a0, swap(a1, y_bit), b0, swap(b1, x_bit))

    def third_step(*parts):
        kept, sent = add_second(own, *parts)
        return (kept, swap(sent, line_unit))

    def line_step(unit, kept, came):
        kept, sent = add_line(kept, came)
        return (kept, swap(sent, unit))

    def split_attn(values):
        return values.reshape(2, 2, lines, 2, 2 * slots, width)

    grad = cotangent[0] * (loss_weight[:, None] * factor)
    one1 = ffn_back(1, grad, 1, None)
    came = swap(one1.grads, core_bit)
    two1 = ffn_back(1, grad, 0, one1.gh)
    f1 = first_step(two1.grads, came)
    attn_g1 = attn_back(1, after(two1.gmid, f1[0]))
    a1 = core_step(split_attn(attn_g1.kept), split_attn(attn_g1.sent))
    grad, *f1 = hold(attn_g1.gx, *f1)
    f1 = second_step(*f1)
    one0 = ffn_back(0, after(grad, f1[0]), 1, None)
    f0 = swap(one0.grads, core_bit)
    gh, a1k, a1c, *f1 = hold(one0.gh, *a1, *f1)
    a1 = first_step(a1k, a1c)
    f1 = third_step(*f1)
    two0 = ffn_back(0, grad, 0, after(gh, a1[0], f1[0]))
    gmid, f0k, f0c, f1k, f1c, *a1 = hold(two0.gmid, two0.grads, f0, *f1, *a1)
    f0 = first_step(f0k, f0c)
    a1 = second_step(*a1)
    unit = 2 * line_unit
    f1 = line_step(unit, f1k, f1c)
    attn_g0 = attn_back(0, after(gmid, f0[0], a1[0], f1[0]))
    parts = (attn_g0.kept, attn_g0.sent, attn_g0.sums)
    kept, sent, sums, f1k, f1c, a1k, a1kc, a1b, a1bc, *f0 = hold(*parts, *f1, *a1, *f0)
    attn_g0.sums = sums
    a0 = core_step(split_attn(kept), split_attn(sent))
    f0 = second_step(*f0)
    a1 = third_step(a1k, a1kc, a1b, a1bc)
    f1 = (f1k, f1c)
    a0 = first_step(*a0)
    f0 = third_step(*f0)
    a1 = line_step(unit, *a1)
    a0 = second_step(*a0)
    f0 = line_step(unit, *f0)
    a0 = third_step(*a0)
    a0 = line_step(unit, *a0)
    while unit * 2 < lines * line_unit:
        unit *= 2
        f1, a1, f0, a0 = [line_step(unit, *parts) for parts in (f1, a1, f0, a0)]
    ffn_grads = [(two0, one0), (two1, one1)]

    small = []
    for layer, attn_g in ((0, attn_g0), (1, attn_g1)):
        two, one = ffn_grads[layer]
        a, f = attn_g.sums, two.sums
        sums = jnp.concatenate([a[:4], f[2:3], a[4:5], f[0:1], a[5:6], f[1:2]])
        sums = sums.reshape(9, count, rows).transpose(1, 0, 2).reshape(count, 9 * rows)
        sums = jnp.dot(hot.astype(f32), sums, precision=lax.Precision.HIGHEST)
        bias = jnp.concatenate([two.gbias, one.gbias]).reshape(count, hidden)
        small += [sums, bias]
    small = jnp.concatenate(small, axis=1)
    for bits, size in ((core_bit, 2), (x_bit, 4), (y_bit, 8)):
        kept = small[: count // size]
        small = kept + swap(small[count // size :], bits)
    bit = 1
    relative = [lax.dynamic_index_in_dim(small, own_line ^ n, 0) for n in range(lines)]
    while bit < lines:
        sent = jnp.concatenate(relative[bit :: 2 * bit])
        came = swap(sent, bit * line_unit)
        for n, place in enumerate(range(0, lines, 2 * bit)):
            relative[place] = relative[place] + came[n : n + 1]
        bit *= 2
    small = relative[0][0].reshape(layer_count, small_len)

    own_attn = jnp.stack([total_of(*a0), total_of(*a1)]).reshape(layer_count, 4, slots, width)
    own_ffn = jnp.stack([total_of(*f0), total_of(*f1)]).reshape(layer_count, 2, hidden, width)
    return (
        result[None],
        attn_g0.gx[None],
        own_attn[:, :3, :rows],
        own_attn[:, 3, :rows],
        small[:, : 5 * rows].reshape(layer_count, 5, rows),
        small[:, 5 * rows : 7 * rows].reshape(layer_count, 2, rows),
        small[:, 7 * rows : 9 * rows].reshape(layer_count, 2, rows),
        own_ffn[:, 0],
        own_ffn[:, 1],
        small[:, 9 * rows :],
    )


def solution(mesh):
    in_specs = (
        P(("batch", "ffn", "mp"), None, None),
        P(None, None, ("batch", "ffn", "mp"), None),
        P(None, ("batch", "ffn", "mp"), None),
        P(None, None, ("batch", "ffn", "mp")),
        P(None, None, ("batch", "ffn", "mp")),
        P(None, None, ("batch", "ffn", "mp")),
        P(None, ("batch", "ffn", "mp"), None),
        P(None, ("batch", "ffn", "mp"), None),
        P(None, ("batch", "ffn", "mp")),
        P(("batch", "ffn", "mp")),
        P(),
        P(("batch", "ffn", "mp"), None),
        P(("batch", "ffn", "mp"), None, None),
    )
    out_specs = (
        P(("batch", "ffn", "mp"), None, None),
        P(("batch", "ffn", "mp"), None, None),
        P(None, None, ("batch", "ffn", "mp"), None),
        P(None, ("batch", "ffn", "mp"), None),
        P(None, None, ("batch", "ffn", "mp")),
        P(None, None, ("batch", "ffn", "mp")),
        P(None, None, ("batch", "ffn", "mp")),
        P(None, ("batch", "ffn", "mp"), None),
        P(None, ("batch", "ffn", "mp"), None),
        P(None, ("batch", "ffn", "mp")),
    )
    sizes = tuple(mesh.shape[name] for name in AXES)
    return jax.shard_map(partial(shards, sizes), mesh=mesh, in_specs=in_specs, out_specs=out_specs, check_vma=False)
```

```python
from functools import partial
import math
from types import SimpleNamespace

import jax
import jax.numpy as jnp
from jax import lax
from jax.experimental import pallas as pl
from jax.experimental.pallas import tpu as pltpu
from jax.sharding import PartitionSpec as P

HEADS = 20
HEAD_DIM = 32


norm_eps = 1e-05
mask_value = -1e30


def rope_tables(length, head_width):
    half_width = head_width // 2
    freqs = jnp.exp(
        jnp.arange(half_width, dtype=jnp.float32) * (-2.0 * math.log(10000.0) / head_width)
    )
    angles = jnp.arange(length, dtype=jnp.float32)[:, None] * freqs[None, :]
    return (jnp.cos(angles), jnp.sin(angles))


AXES = ("batch", "ffn", "mp")
CUT = 2


def after(value, *others):
    return lax.optimization_barrier((value, *others))[0]


def pad_rows(rows):
    return -(-(rows + 1) // 8) * 8


GROUP = 128 // HEAD_DIM
VMEM_LIMIT = 56 * 1024 * 1024
SMALL_LIMIT = 24 * 1024 * 1024


def dot_nn(left, right):
    return lax.dot_general(
        left, right, (((1,), (0,)), ((), ())), preferred_element_type=jnp.float32
    )


def dot_nt(left, right):
    return lax.dot_general(
        left, right, (((1,), (1,)), ((), ())), preferred_element_type=jnp.float32
    )


def dot_tn(left, right):
    return lax.dot_general(
        left, right, (((0,), (0,)), ((), ())), preferred_element_type=jnp.float32
    )


def norm_parts(values):
    centred = values - jnp.mean(values, axis=-1, keepdims=True)
    variance = jnp.mean(centred * centred, axis=-1, keepdims=True)
    inverse = lax.rsqrt(variance + norm_eps)
    return (centred * inverse, inverse)


def norm_grad(grad, values, gain_row):
    unit, inverse = norm_parts(values)
    scaled = grad * gain_row
    mean_one = jnp.mean(scaled, axis=-1, keepdims=True)
    mean_two = jnp.mean(scaled * unit, axis=-1, keepdims=True)
    into = inverse * (scaled - mean_one - unit * mean_two)
    grad_gain = jnp.sum(grad * unit, axis=0, keepdims=True)
    grad_shift = jnp.sum(grad, axis=0, keepdims=True)
    return (into, grad_gain, grad_shift)


def turn(values, cos_ref, sin_ref, sign):
    half = HEAD_DIM // 2
    lanes = lax.broadcasted_iota(jnp.int32, (values.shape[0], 128), 1)
    low_half = lanes % HEAD_DIM < half
    parts = []
    for start in range(0, values.shape[1], 128):
        part = values[:, start : start + 128]
        partner = jnp.where(
            low_half, pltpu.roll(part, 128 - half, 1), pltpu.roll(part, half, 1)
        )
        parts.append(part * cos_ref[...] + sign * (partner * sin_ref[...]))
    return jnp.concatenate(parts, axis=1)


def head_lanes(block, head):
    lanes = lax.broadcasted_iota(jnp.int32, block.shape, 1)
    return jnp.where(lanes // HEAD_DIM == head, block, jnp.zeros_like(block))


def sds(shape, dtype):
    return jax.ShapeDtypeStruct(shape, dtype)


def whole(shape):
    return pl.BlockSpec(shape, lambda *_: (0,) * len(shape))


def call(body, name, grid, ins, outs, scratch, flops, moved, prefetch=None, aliases=None, limit=None):
    names = list(ins) + list(outs) + list(scratch)
    lead = 0 if prefetch is None else 1

    def kernel(*refs):
        named = dict(zip(names, refs[lead:]))
        if lead:
            named.update(own=refs[0])
        body(SimpleNamespace(**named))

    in_specs = [spec or whole(array.shape) for array, spec in ins.values()]
    out_specs = [spec or whole(shape) for shape, _, spec in outs.values()]
    out_shape = [sds(shape, dtype) for shape, dtype, _ in outs.values()]
    scratch_shapes = [pltpu.VMEM(shape, dtype) for shape, dtype in scratch.values()]
    operands = ([] if prefetch is None else [prefetch]) + [array for array, _ in ins.values()]
    in_names, out_names = list(ins), list(outs)
    pairs = {
        in_names.index(a) + lead: out_names.index(b) for a, b in (aliases or {}).items()
    }
    results = pl.pallas_call(
        kernel,
        grid_spec=pltpu.PrefetchScalarGridSpec(
            num_scalar_prefetch=lead,
            grid=grid,
            in_specs=in_specs,
            out_specs=out_specs,
            scratch_shapes=scratch_shapes,
        ),
        out_shape=out_shape,
        input_output_aliases=pairs,
        compiler_params=pltpu.CompilerParams(vmem_limit_bytes=limit or VMEM_LIMIT),
        cost_estimate=pl.CostEstimate(flops=flops, bytes_accessed=moved, transcendentals=0),
        name=name,
    )(*operands)
    return SimpleNamespace(**dict(zip(out_names, results)))


def attn_open(r):
    unit, _ = norm_parts(r.x[...])
    h_one = (unit * r.vec[4:5] + r.vec[5:6]).astype(jnp.bfloat16)
    r.h_rel[...] = dot_nn(h_one, (r.sg if hasattr(r, "sg") else r.sa)[...]).astype(jnp.bfloat16)
    wabs = r.wabs
    for j, ref in enumerate((r.w0, r.w1, r.w2, r.w3) if hasattr(r, "w0") else ()):
        wabs[j] = dot_nn(r.sa[...], rows_of(ref)).astype(jnp.bfloat16)
    for j in () if hasattr(r, "w0") else range(4):
        half = r.wa.shape[1]
        spread = r.sa if j < 2 or not hasattr(r, "sb") else r.sb
        own, came = (r.wa, r.wa2) if j < 2 else (r.wb, r.wb2)
        placed = dot_nn(spread[:, :half], own[j % 2])
        placed += dot_nn(spread[:, half:], came[j % 2])
        wabs[j] = placed.astype(jnp.bfloat16)
    query = dot_nn(h_one, wabs[0]) + r.vec[0:1]
    query = turn(query, r.cos, r.sin, 1.0) * HEAD_DIM ** (-0.5)
    r.q[...] = query.astype(jnp.bfloat16)
    r.qt[...] = query.T.astype(jnp.bfloat16)
    key = turn(dot_nn(h_one, wabs[1]) + r.vec[1:2], r.cos, r.sin, 1.0)
    key_bf = key.astype(jnp.bfloat16)
    for start in range(key.shape[1] // 128):
        r.k[start] = key_bf[:, 128 * start : 128 * start + 128]
    r.kt[...] = key.T.astype(jnp.bfloat16)
    value = dot_nn(h_one, wabs[2]) + r.vec[2:3]
    r.v[...] = value.astype(jnp.bfloat16)
    r.vt[...] = value.T.astype(jnp.bfloat16)


def attn_heads(r, group):
    key_block = r.k[group]
    query_t = r.qt[pl.ds(pl.multiple_of(group * 128, 128), 128), :]
    for head in range(GROUP):
        scores = dot_nn(head_lanes(key_block, head), query_t) + r.mask[...]
        top = jnp.max(scores, axis=0, keepdims=True)
        shifted = jnp.exp(scores - top)
        total = jnp.sum(shifted, axis=0, keepdims=True)
        probs = (shifted * (1.0 / total)).astype(jnp.bfloat16)
        r.probs[head] = probs
        rows = pl.ds(pl.multiple_of(group * 128 + head * HEAD_DIM, HEAD_DIM), HEAD_DIM)
        r.att_t[rows, :] = dot_nn(r.vt[rows, :], probs)


def attn_close(r):
    att = r.att_t[...].T.astype(jnp.bfloat16)
    r.att_rel[...] = dot_nn(att, (r.sg if hasattr(r, "sg") else r.sa)[...]).astype(jnp.bfloat16)
    r.mid[...] = r.x[...] + (dot_nn(att, r.wabs[3]) + r.vec[3:4])


def attn_forward(x, parts, spreads, vec, cos, sin, mask, cut, between):
    length, width = x.shape
    spots = (spreads["sg"] if "sg" in spreads else spreads["sa"]).shape[1]
    groups = width // 128
    b16, f32 = jnp.bfloat16, jnp.float32
    opening = dict(x=x, **parts, **spreads)
    tables = dict(vec=vec, cos=cos, sin=sin, mask=mask)
    made = dict(
        wabs=((4, width, width), b16, None),
        h_rel=((length, spots), b16, None),
        q=((length, width), b16, None),
        kt=((width, length), b16, None),
        v=((length, width), b16, None),
    )
    work = dict(
        qt=((width, length), b16),
        k=((groups, length, 128), b16),
        vt=((width, length), b16),
    )
    att_t = dict(att_t=((width, length), f32, None))
    closing = dict(att_rel=((length, spots), b16, None), mid=((length, width), f32, None))

    def probs_out(base):
        spec = pl.BlockSpec((GROUP, length, length), lambda i: (i + base, 0, 0))
        return dict(probs=((HEADS, length, length), b16, spec))

    def plain(arrays):
        return {
            name: array if isinstance(array, tuple) else (array, None)
            for name, array in arrays.items()
        }

    def body(first, last, base, steps):
        def run(r):
            step = pl.program_id(0)
            if first:
                pl.when(step == 0)(lambda: attn_open(r))
            else:

                @pl.when(step == 0)
                def _():
                    r.att_t[: base * 128, :] = r.att_in[: base * 128, :]

            attn_heads(r, step + base)
            if last:
                pl.when(step == steps - 1)(lambda: attn_close(r))

        return run

    if cut == groups:
        return call(
            body(True, True, 0, groups), "attn_fwd", (groups,),
            plain({**opening, **tables}), {**made, **att_t, **closing, **probs_out(0)}, work,
            20_000_000_000, 25_000_000,
        )
    shared = {name: (shape, dtype, None) for name, (shape, dtype) in work.items()}
    one = call(
        body(True, False, 0, cut), "attn_fwd_one", (cut,),
        plain({**opening, **tables}), {**made, **att_t, **shared, **probs_out(0)}, {},
        10_000_000_000, 15_000_000,
    )
    att_in = between(one.att_t)
    ins = plain(
        dict(
            x=x, sa=spreads["sa"], vec=vec, mask=mask, wabs=one.wabs, att_in=att_in,
            qt=one.qt, k=one.k, vt=one.vt,
        )
    )
    ins.update(probs_in=(one.probs, pl.BlockSpec(memory_space=pl.ANY)))
    two = call(
        body(False, True, cut, groups - cut), "attn_fwd_two", (groups - cut,),
        ins, {**att_t, **closing, **probs_out(cut)}, {},
        10_000_000_000, 15_000_000, aliases=dict(probs_in="probs"),
    )
    return SimpleNamespace(**{**vars(one), **vars(two)})


def ffn_specs(kind, arrays, base, hidden, lines, width):
    specs = {}
    rows = lines * hidden
    if kind == "own":
        specs.update(up0=(arrays[0], pl.BlockSpec((2 * rows, width), lambda i, own: (i, 0))))
        for y in range(2):
            spec = pl.BlockSpec((rows, width), lambda i, own, y=y: (2 * y + i, 0))
            specs["down" + str(y)] = (arrays[1], spec)
        return specs
    shape = (1, lines, 1, 1, hidden, width)
    for which, name in enumerate(("up", "down")):
        for y in range(2):

            def index(i, own, y=y, which=which):
                core = base + i // 2
                return ((i % 2) ^ own[0], 0, y ^ own[1], core ^ own[2], which, 0)

            specs[name + str(y)] = (arrays[0], pl.BlockSpec(shape, index))
    return specs


def rows_of(*refs):
    parts = []
    for ref in refs:
        values = ref[...]
        parts.append(values.reshape(-1, values.shape[-1]))
    return jnp.concatenate(parts) if len(parts) > 1 else parts[0]


def up_rows(r):
    return rows_of(r.up0, r.up1) if hasattr(r, "up1") else rows_of(r.up0)


def ffn_forward(own, mid, vec, kind, arrays, bias, lines, hidden, base, steps, before):
    length, width = mid.shape
    block = 2 * lines * hidden
    b16 = jnp.bfloat16
    kept = pl.BlockSpec((1, length, block), lambda i, own: (i, 0, 0))

    def body(r):
        h_two = r.h_two if before is None else r.h_in

        @pl.when(pl.program_id(0) == 0)
        def _():
            if before is None:
                unit, _ = norm_parts(r.mid[...])
                h_two[...] = (unit * r.vec[6:7] + r.vec[7:8]).astype(b16)
                r.out[...] = r.mid[...] + r.vec[8:9]
            else:
                r.out[...] = r.so_far[...]

        pre = dot_nt(h_two[...], up_rows(r)) + r.bias[0]
        cdf = 0.5 * (1.0 + lax.erf(pre * (0.5**0.5)))
        act = (pre * cdf).astype(b16)
        r.act[0] = act
        slope = cdf + pre * (jnp.exp(-0.5 * pre * pre) * (1.0 / math.sqrt(2.0 * math.pi)))
        r.slope[0] = slope.astype(b16)
        r.out[...] += dot_nn(act, rows_of(r.down0, r.down1))

    ins = ffn_specs(kind, arrays, base, hidden, lines, width)
    ins.update(
        bias=(
            bias.reshape(steps, 1, block),
            pl.BlockSpec((1, 1, block), lambda i, own: (i, 0, 0)),
        ),
    )
    outs = dict(
        out=((length, width), jnp.float32, None),
        act=((steps, length, block), b16, kept),
        slope=((steps, length, block), b16, kept),
    )
    if before is None:
        ins.update(mid=(mid, None), vec=(vec, None))
        outs.update(h_two=((length, width), b16, None))
    else:
        ins.update(h_in=(before.h_two, None), so_far=(before.out, None))
    name = "ffn_fwd_one" if before is None else "ffn_fwd_two"
    return call(body, name, (steps,), ins, outs, {}, 5_000_000_000, 10_000_000, prefetch=own)


def ffn_backward(
    own, grad, mid, vec, kept, at, h_two, kind, arrays, lines, hidden, base, gh_in
):
    length, width = mid.shape
    block = 2 * lines * hidden
    b16, f32 = jnp.bfloat16, jnp.float32
    last = gh_in is not None
    wide = pl.BlockSpec((1, length, block), lambda i, own: (i + at, 0, 0))

    def body(r):
        @pl.when(pl.program_id(0) == 0)
        def _():
            r.gf[...] = r.g[...].astype(b16)
            r.gh[...] = r.gh_in[...] if last else jnp.zeros_like(r.gh)

        gf = r.gf[...]
        g_down = dot_tn(r.act[0], gf)
        g_act = dot_nt(gf, rows_of(r.down0, r.down1))
        g_pre = (g_act * r.slope[0].astype(f32)).astype(b16)
        g_up = dot_tn(g_pre, r.h_two[...])
        for n in range(2 * lines):
            rows = slice(n * hidden, (n + 1) * hidden)
            r.grads[0, n // lines, n % lines, 0] = g_up[rows].astype(b16)
            r.grads[0, n // lines, n % lines, 1] = g_down[rows].astype(b16)
        r.gbias[0] = jnp.sum(g_pre.astype(f32), axis=0, keepdims=True)
        r.gh[...] += dot_nn(g_pre, up_rows(r))
        if last:

            @pl.when(pl.program_id(0) == 1)
            def _():
                into, grad_gain, grad_shift = norm_grad(
                    r.gh[...], r.mid[...], r.vec[6:7]
                )
                r.gmid[...] = r.g[...] + into
                r.sums[...] = jnp.zeros_like(r.sums)
                r.sums[0:1] = grad_gain
                r.sums[1:2] = grad_shift
                r.sums[2:3] = jnp.sum(r.gf[...].astype(f32), axis=0, keepdims=True)

    ins = dict(
        g=(grad, None),
        h_two=(h_two, None),
        act=(kept.act, wide),
        slope=(kept.slope, wide),
        **ffn_specs(kind, arrays, base, hidden, lines, width),
    )
    outs = dict(
        grads=(
            (2, 2, lines, 2, hidden, width),
            b16,
            pl.BlockSpec((1, 2, lines, 2, hidden, width), lambda i, own: (i, 0, 0, 0, 0, 0)),
        ),
        gbias=((2, 1, block), f32, pl.BlockSpec((1, 1, block), lambda i, own: (i, 0, 0))),
    )
    scratch = dict(gf=((length, width), b16))
    if last:
        ins.update(gh_in=(gh_in, None), mid=(mid, None), vec=(vec, None))
        outs.update(gmid=((length, width), f32, None), sums=((8, width), f32, None))
        scratch.update(gh=((length, width), f32))
    else:
        outs.update(gh=((length, width), f32, None))
    name = "ffn_bwd_two" if last else "ffn_bwd_one"
    return call(body, name, (2,), ins, outs, scratch, 9_000_000_000, 15_000_000, prefetch=own)


def put_pieces(r, index, values):
    count, _, slots, _ = r.kept.shape
    for piece in range(2 * count):
        ref = r.kept if piece < count else r.sent
        ref[piece % count, index] = values[piece * slots : (piece + 1) * slots].astype(ref.dtype)


def attn_grad_open(r):
    b16 = jnp.bfloat16
    r.ga[...] = r.gmid[...].astype(b16)
    put_pieces(r, 3, dot_tn(r.att_rel[...], r.ga[...]))
    gatt = dot_nt(r.ga[...], r.wabs[3]).astype(b16)
    for start in range(gatt.shape[1] // 128):
        lanes = slice(128 * start, 128 * start + 128)
        r.gatt[start] = gatt[:, lanes]
        r.qs[start] = r.q[:, lanes]
        r.vs[start] = r.v[:, lanes]
    gatt_t = gatt.astype(jnp.float32).T
    r.gatt_t[...] = gatt_t.astype(b16)
    for head in range(HEADS):
        rows = slice(head * HEAD_DIM, (head + 1) * HEAD_DIM)
        r.inner[head] = jnp.sum(gatt_t[rows] * r.att_t[rows], axis=0, keepdims=True)


def attn_grad_heads(r, group):
    gatt_block, q_block, v_block = r.gatt[group], r.qs[group], r.vs[group]
    gatt_t = r.gatt_t[pl.ds(pl.multiple_of(group * 128, 128), 128), :]
    dk = jnp.zeros(q_block.shape, jnp.float32)
    dv = jnp.zeros(q_block.shape, jnp.float32)
    for head in range(GROUP):
        probs = r.probs[head]
        gprobs = dot_nn(head_lanes(v_block, head), gatt_t)
        inner = r.inner[group * GROUP + head]
        gscores = (probs.astype(jnp.float32) * (gprobs - inner)).astype(jnp.bfloat16)
        dv += dot_nn(probs, head_lanes(gatt_block, head))
        dk += dot_nn(gscores, head_lanes(q_block, head))
        rows = pl.ds(pl.multiple_of(group * 128 + head * HEAD_DIM, HEAD_DIM), HEAD_DIM)
        r.dqt[rows, :] = dot_nn(r.kt[rows, :], gscores)
    r.dk[group] = dk
    r.dv[group] = dv


def attn_grad_close(r):
    b16, f32 = jnp.bfloat16, jnp.float32

    def joined(ref):
        return jnp.concatenate([ref[i] for i in range(ref.shape[0])], axis=1)

    def rounded(values):
        return values.astype(b16).astype(f32)

    gq = rounded(r.dqt[...].T) * HEAD_DIM ** (-0.5)
    gproj = [
        turn(gq, r.cos, r.sin, -1.0).astype(b16),
        turn(rounded(joined(r.dk)), r.cos, r.sin, -1.0).astype(b16),
        joined(r.dv).astype(b16),
    ]
    r.sums[...] = jnp.zeros_like(r.sums)
    gh = jnp.zeros(r.gx.shape, f32)
    for j in range(3):
        put_pieces(r, j, dot_tn(r.h_rel[...], gproj[j]))
        r.sums[j : j + 1] = jnp.sum(gproj[j].astype(f32), axis=0, keepdims=True)
        gh += dot_nt(gproj[j], r.wabs[j])
    into, grad_gain, grad_shift = norm_grad(gh, r.x[...], r.vec[4:5])
    r.gx[...] = r.gmid[...] + into
    r.sums[3:4] = jnp.sum(r.ga[...].astype(f32), axis=0, keepdims=True)
    r.sums[4:5] = grad_gain
    r.sums[5:6] = grad_shift


def attn_backward(slots, gmid, x, vec, cos, sin, saved):
    length, width = x.shape
    spots = saved.h_rel.shape[1]
    half = spots // slots // 2
    groups = width // 128
    b16, f32 = jnp.bfloat16, jnp.float32

    def body(r):
        step = pl.program_id(0)
        pl.when(step == 0)(lambda: attn_grad_open(r))
        attn_grad_heads(r, step)
        pl.when(step == groups - 1)(lambda: attn_grad_close(r))

    full = dict(
        gmid=gmid, x=x, vec=vec, cos=cos, sin=sin, wabs=saved.wabs, h_rel=saved.h_rel,
        q=saved.q, kt=saved.kt, v=saved.v, att_t=saved.att_t, att_rel=saved.att_rel,
    )
    ins = {name: (array, None) for name, array in full.items()}
    ins.update(
        probs=(saved.probs, pl.BlockSpec((GROUP, length, length), lambda i: (i, 0, 0)))
    )
    split = ((groups, length, 128), b16)
    sums = ((groups, length, 128), f32)
    return call(
        body, "attn_bwd", (groups,), ins,
        dict(
            gx=((length, width), f32, None),
            kept=((half, 4, slots, width), b16, None),
            sent=((half, 4, slots, width), b16, None),
            sums=((8, width), f32, None),
        ),
        dict(
            ga=((length, width), b16),
            gatt=split,
            qs=split,
            vs=split,
            gatt_t=((width, length), b16),
            inner=((HEADS, 1, length), f32),
            dqt=((width, length), f32),
            dk=sums,
            dv=sums,
        ),
        30_000_000_000, 30_000_000,
    )


def total_of(one, two):
    return one.astype(jnp.float32) + two.astype(jnp.float32)


def add_core(kept, came):
    _, _, lines, _, rows, width = kept.shape
    b16 = jnp.bfloat16
    both = pl.BlockSpec((2, 2, 1, 2, rows, width), lambda i: (0, 0, i, 0, 0, 0))
    one = ((2, lines, rows, width), b16, pl.BlockSpec((2, 1, rows, width), lambda i: (0, i, 0, 0)))

    def body(r):
        for n in range(2):
            r.ak[n, 0] = total_of(r.kept[0, n, 0, 0], r.came[0, n, 0, 0]).astype(b16)
            r.at[n, 0] = total_of(r.kept[1, n, 0, 0], r.came[1, n, 0, 0]).astype(b16)
            r.bk[n, 0] = total_of(r.kept[n, 0, 0, 1], r.came[n, 0, 0, 1]).astype(b16)
            r.bt[n, 0] = total_of(r.kept[n, 1, 0, 1], r.came[n, 1, 0, 1]).astype(b16)

    made = call(
        body, "add_core", (lines,), dict(kept=(kept, both), came=(came, both)),
        dict(ak=one, at=one, bk=one, bt=one), {}, 10_000_000, 10_000_000, limit=SMALL_LIMIT,
    )
    return (made.ak, made.at, made.bk, made.bt)


def add_first(ak, ac, bk, bc):
    _, lines, rows, width = ak.shape
    b16 = jnp.bfloat16
    steps = max(1, lines // 2)
    block = lines // steps
    both = pl.BlockSpec((2, block, rows, width), lambda i: (0, i, 0, 0))
    one = ((lines, rows, width), b16, pl.BlockSpec((block, rows, width), lambda i: (i, 0, 0)))

    def body(r):
        r.a0[...] = total_of(r.ak[0], r.ac[0]).astype(b16)
        r.a1[...] = total_of(r.ak[1], r.ac[1]).astype(b16)
        r.b0[...] = total_of(r.bk[0], r.bc[0]).astype(b16)
        r.b1[...] = total_of(r.bk[1], r.bc[1]).astype(b16)

    made = call(
        body, "add_first", (steps,),
        dict(ak=(ak, both), ac=(ac, both), bk=(bk, both), bc=(bc, both)),
        dict(a0=one, a1=one, b0=one, b1=one), {}, 10_000_000, 10_000_000, limit=SMALL_LIMIT,
    )
    return (made.a0, made.a1, made.b0, made.b1)


def add_second(own, ak, ac, bk, bc):
    lines, rows, width = ak.shape
    b16 = jnp.bfloat16
    half = lines // 2

    def place(i):
        order, unit, left = 0, 1, half
        while left:
            order += (i // left % 2) * unit
            unit, left = unit * 2, left // 2
        return order

    shape = (half, 2, rows, width)

    def body(r):
        for n in range(lines):
            line = place(n) ^ r.own[3]
            ref = r.kept if n < half else r.sent
            ref[n % half, 0] = total_of(r.ak[line], r.ac[line]).astype(b16)
            ref[n % half, 1] = total_of(r.bk[line], r.bc[line]).astype(b16)

    made = call(
        body, "add_second", (1,),
        dict(ak=(ak, None), ac=(ac, None), bk=(bk, None), bc=(bc, None)),
        dict(kept=(shape, b16, None), sent=(shape, b16, None)), {},
        10_000_000, 5_000_000, prefetch=own, limit=SMALL_LIMIT,
    )
    return (made.kept, made.sent)


def add_line(kept, came):
    half, _, rows, width = kept.shape
    shape = (half // 2, 2, rows, width)

    def body(r):
        total = total_of(r.kept[...], r.came[...])
        r.low[...] = total[: half // 2]
        r.high[...] = total[half // 2 :].astype(jnp.bfloat16)

    made = call(
        body, "add_line", (1,), dict(kept=(kept, None), came=(came, None)),
        dict(low=(shape, jnp.float32, None), high=(shape, jnp.bfloat16, None)), {},
        10_000_000, 2_000_000, limit=SMALL_LIMIT,
    )
    return (made.low, made.high)


def shards(
    sizes,
    tokens,
    qkv_weight,
    out_weight,
    proj_bias,
    norm_gain,
    norm_shift,
    up_weight,
    down_weight,
    up_bias,
    seq_order,
    seq_length,
    mlm_mask,
    cotangent,
):
    _, length, width = tokens.shape
    layer_count = qkv_weight.shape[0]
    _, ffn_size, core_size = sizes
    lines = ffn_size // 2
    count = 2 * ffn_size * core_size
    x_bit, y_bit, core_bit, line_unit = ffn_size * core_size, core_size, 1, 2 * core_size
    own_id = lax.axis_index(AXES)
    own_x = (own_id // x_bit) % 2
    own_y = (own_id // y_bit) % 2
    own_core = own_id % 2
    own_line = (own_id // line_unit) % lines
    own = jnp.stack([own_x, own_y, own_core, own_line]).astype(jnp.int32)
    rows = qkv_weight.shape[2]
    slots = pad_rows(rows)
    hidden = up_weight.shape[1]
    b16, f32 = jnp.bfloat16, jnp.float32

    def device(x, y, line, core):
        return (x * ffn_size + line * 2 + y) * core_size + core

    def swap(values, bits):
        return lax.ppermute(values, AXES, [(i, i ^ bits) for i in range(count)])

    def grow(values, bits, axis):
        return jnp.concatenate([values, swap(values, bits)], axis=axis)

    def line_gather(values, axis):
        bit = lines // 2
        while bit:
            came = swap(values, bit * line_unit)
            high = (own_line & bit) > 0
            values = jnp.stack(
                [jnp.where(high, came, values), jnp.where(high, values, came)], axis=axis + 1
            )
            shape = values.shape
            values = values.reshape(shape[:axis] + (shape[axis] * 2,) + shape[axis + 2 :])
            bit //= 2
        return values

    order_ids = jnp.arange(seq_length.shape[0], dtype=jnp.int32)
    slot_length = jnp.sum(jnp.where(seq_order[0] == order_ids, seq_length, 0))
    key_ok = jnp.arange(length, dtype=jnp.int32) < slot_length
    loss_weight = jnp.where(key_ok & (mlm_mask[0] > 0), 1.0, 0.0).astype(f32)
    local_count = jnp.sum(loss_weight)
    count_high = jnp.floor(local_count / 256.0)
    count_low = local_count - 256.0 * count_high
    small_len = 9 * rows + hidden
    layers = range(layer_count)
    small_row = jnp.concatenate(
        [
            part.reshape(-1)
            for layer in layers
            for part in (proj_bias[layer], norm_gain[layer], norm_shift[layer], up_bias[layer])
        ]
        + [count_high[None], count_low[None]]
    ).astype(b16)
    small_row = jnp.pad(small_row, (0, width - small_row.shape[0]))
    spare = jnp.zeros((4, slots - rows, width), b16)
    spare_at = jnp.arange(4 * (slots - rows)).reshape(4, slots - rows, 1) == 0
    spare = jnp.where(spare_at, small_row[None, None], spare)
    attn = jnp.concatenate([qkv_weight[0], out_weight[0][None]]).astype(b16)
    attn = jnp.concatenate([attn, spare], axis=1)
    attn, up_weight, down_weight, qkv_late, out_late = lax.optimization_barrier(
        (attn, up_weight, down_weight, qkv_weight[1], out_weight[1])
    )

    def ffn_piece(layer):
        return jnp.stack([up_weight[layer], down_weight[layer]]).astype(b16)

    attn = line_gather(attn[:, None], 1).reshape(4, lines * slots, width)
    part_a = grow(attn[:2], y_bit, 1)
    part_b = grow(attn[2:], x_bit, 1)
    part_a = grow(part_a, x_bit, 1)
    part_b = grow(part_b, y_bit, 1)
    ffn = after(ffn_piece(0), attn)
    ffn = jnp.stack([ffn] + [swap(ffn, n * line_unit) for n in range(1, lines)])
    bit = lines // 2
    while bit:
        pairs = ffn.reshape(lines // (2 * bit), 2, bit, *ffn.shape[1:])
        ffn = jnp.where((own_line & bit) > 0, jnp.flip(pairs, 1), pairs).reshape(ffn.shape)
        bit //= 2
    half_a, half_b = (swap(part_a, core_bit), swap(part_b, core_bit))
    up_all = ffn[:, 0].reshape(lines * hidden, width)
    down_all = ffn[:, 1].reshape(lines * hidden, width)
    up_came, down_came = (swap(up_all, y_bit), swap(down_all, x_bit))

    late_slots = slots if hidden % 16 else 32
    late = jnp.concatenate([qkv_late, out_late[None]]).astype(b16)
    late = jnp.pad(late, ((0, 0), (0, late_slots - rows), (0, 0)))
    late = jnp.concatenate(
        [ffn_piece(1).reshape(2 * hidden, width), late.reshape(4 * late_slots, width)]
    )
    late = lax.all_gather(after(late, attn), AXES, axis=0, tiled=False)
    if hidden % 16:
        late_attn = late[:, 2 * hidden :].reshape(count, 4, slots, width).transpose(1, 0, 2, 3)
        late_attn = [(part.reshape(count * slots, width), None) for part in late_attn]
    else:
        first_block = 2 * hidden // late_slots
        late_attn = [
            (late, pl.BlockSpec((count, late_slots, width), lambda i, n=n: (0, first_block + n, 0)))
            for n in range(4)
        ]
    late = late.reshape(2, lines, 2, 2, late.shape[1], width)
    late_kind = "own" if hidden % 16 else "late"
    late_weights = [(late,), (late,)]
    if late_kind == "own":
        turned = late[:, :, :, :, : 2 * hidden].reshape(2, lines, 2, 2, 2, hidden, width)
        for axis, odd in ((0, own_x), (2, own_y), (3, own_core)):
            turned = jnp.where(odd > 0, jnp.flip(turned, axis), turned)
        late_up = turned[:, :, :, :, 0].transpose(3, 0, 2, 1, 4, 5)
        late_down = turned[:, :, :, :, 1].transpose(3, 2, 0, 1, 4, 5)
        late_weights = [
            (late_up[n].reshape(-1, width), late_down[n].reshape(-1, width)) for n in range(2)
        ]

    index = jnp.arange(count, dtype=jnp.int32)
    line_at = index % lines
    low_at = index // lines % 2
    high_at = index // (2 * lines) % 2
    core_at = (index // (4 * lines)) ^ own_core
    owners_a = device(high_at ^ own_x, low_at ^ own_y, line_at, core_at)
    owners_b = device(low_at ^ own_x, high_at ^ own_y, line_at, core_at)

    def spread_of(owners, size):
        slot_ids = jnp.arange(size, dtype=jnp.int32)
        source_row = jnp.where(
            slot_ids[None, :] < rows, owners[:, None] * rows + slot_ids[None, :], -1
        ).reshape(count * size)
        return (jnp.arange(width, dtype=jnp.int32)[:, None] == source_row[None, :]).astype(b16)

    spread_a, spread_b = spread_of(owners_a, slots), spread_of(owners_b, slots)
    spread_d = spread_of(index, late_slots)
    hot = owners_a[:, None] == index[None, :]
    cos_half, sin_half = rope_tables(length, HEAD_DIM)
    cos = jnp.tile(jnp.concatenate([cos_half, cos_half], axis=1), (1, GROUP))
    sin = jnp.tile(jnp.concatenate([-sin_half, sin_half], axis=1), (1, GROUP))
    mask = jnp.where(key_ok, 0.0, mask_value).astype(f32)[:, None]

    small_own = jnp.concatenate(
        [part[0].reshape(-1, slots, width)[:, rows, :] for part in (part_a, half_a)]
    )
    small_all = dot_tn(hot.astype(b16), small_own)
    spot = layer_count * small_len
    masked_total = jnp.sum(small_all[:, spot] * 256.0 + small_all[:, spot + 1])
    factor = seq_length.shape[0] * length / jnp.maximum(masked_total, 1.0)

    vecs, biases = [], []
    for layer in layers:
        start = layer * small_len
        vec = small_all[:, start : start + 9 * rows]
        vec = vec.reshape(count, 9, rows).transpose(1, 0, 2).reshape(9, width)
        vec = jnp.concatenate([vec[:4], vec[5:6], vec[7:8], vec[6:7], vec[8:9], vec[4:5]])
        vecs.append(jnp.pad(vec, ((0, 7), (0, 0))))
        bias = small_own[:, start + 9 * rows : start + small_len]
        biases.append(bias.reshape(count * hidden).astype(f32))

    kinds = ("own", late_kind)
    groups = width // 128
    streams, attns, ffns = [tokens[0]], [], []

    def between(value):
        nonlocal up_all, down_all, up_came, down_came
        value, up_came, down_came = lax.optimization_barrier((value, up_came, down_came))
        up_all = jnp.concatenate([up_all, up_came])
        down_all = jnp.concatenate([down_all, down_came])
        up_came, down_came = (swap(up_all, x_bit), swap(down_all, y_bit))
        return value

    attns.append(
        attn_forward(
            streams[0],
            dict(wa=part_a, wa2=half_a, wb=part_b, wb2=half_b),
            dict(sa=spread_a, sb=spread_b),
            vecs[0], cos, sin, mask, CUT, between,
        )
    )
    attns[0].mid, up_came, down_came = lax.optimization_barrier(
        (attns[0].mid, up_came, down_came)
    )
    up_all = jnp.concatenate([up_all, up_came])
    down_all = jnp.concatenate([down_all, down_came])
    up_came, down_came = (swap(up_all, core_bit), swap(down_all, core_bit))
    weights = [[(up_all, down_all), (up_came, down_came)], late_weights]

    def ffn_front(layer):
        halves = 1 if kinds[layer] == "late" else 2
        bias = biases[layer].reshape(halves, -1)
        parts = []
        for base in range(halves):
            parts.append(
                ffn_forward(
                    own, attns[layer].mid, vecs[layer], kinds[layer], weights[layer][base],
                    bias[base], lines, hidden, base, 4 // halves, parts[0] if base else None,
                )
            )
        return parts

    ffns.append(ffn_front(0))
    streams.append(ffns[0][-1].out)
    attns.append(
        attn_forward(
            streams[1],
            dict(w0=late_attn[0], w1=late_attn[1], w2=late_attn[2], w3=late_attn[3]),
            dict(sa=spread_d, sg=spread_a),
            vecs[1], cos, sin, mask, groups, None,
        )
    )
    ffns.append(ffn_front(1))
    result = ffns[1][-1].out

    def ffn_back(layer, grad, base, gh_in):
        joint = len(ffns[layer]) == 1
        return ffn_backward(
            own, grad, attns[layer].mid, vecs[layer], ffns[layer][0 if joint else base],
            2 * base if joint else 0, ffns[layer][0].h_two, kinds[layer], weights[layer][base],
            lines, hidden, base, gh_in,
        )

    def attn_back(layer, grad_mid):
        return attn_backward(slots, grad_mid, streams[layer], vecs[layer], cos, sin, attns[layer])

    def hold(value, *others):
        return lax.optimization_barrier((value, *others))

    def core_step(kept, sent):
        return (kept, swap(sent, core_bit))

    def first_step(kept, came):
        ak, at, bk, bt = add_core(kept, came)
        return (ak, swap(at, x_bit), bk, swap(bt, y_bit))

    def second_step(*parts):
        a0, a1, b0, b1 = add_first(*parts)
        return (a0, swap(a1, y_bit), b0, swap(b1, x_bit))

    def third_step(*parts):
        kept, sent = add_second(own, *parts)
        return (kept, swap(sent, line_unit))

    def line_step(unit, kept, came):
        kept, sent = add_line(kept, came)
        return (kept, swap(sent, unit))

    def split_attn(values):
        return values.reshape(2, 2, lines, 2, 2 * slots, width)

    grad = cotangent[0] * (loss_weight[:, None] * factor)
    one1 = ffn_back(1, grad, 1, None)
    came = swap(one1.grads, core_bit)
    two1 = ffn_back(1, grad, 0, one1.gh)
    gmid, f1k, f1c = hold(two1.gmid, two1.grads, came)
    f1 = first_step(f1k, f1c)
    attn_g1 = attn_back(1, after(gmid, f1[0]))
    grad, kept, sent, sums, *f1 = hold(
        attn_g1.gx, attn_g1.kept, attn_g1.sent, attn_g1.sums, *f1
    )
    attn_g1.sums = sums
    a1k, a1c = core_step(split_attn(kept), split_attn(sent))
    f1 = second_step(*f1)
    a1k, a1c, *_ = hold(a1k, a1c, f1[0])
    a1 = first_step(a1k, a1c)
    one0 = ffn_back(0, after(grad, f1[0], a1[0]), 1, None)
    gh, sent, *parts = hold(one0.gh, one0.grads, *f1, *a1)
    f0 = swap(sent, core_bit)
    f1 = third_step(*parts[:4])
    a1 = second_step(*parts[4:])
    two0 = ffn_back(0, grad, 0, after(gh, f1[0], a1[0]))
    gmid, f0k, f0c, *parts = hold(two0.gmid, two0.grads, f0, *f1, *a1)
    f0 = first_step(f0k, f0c)
    unit = 2 * line_unit
    f1 = line_step(unit, *parts[:2])
    a1 = third_step(*parts[2:])
    attn_g0 = attn_back(0, after(gmid, f0[0], a1[0], f1[0]))
    kept, sent, sums, *parts = hold(attn_g0.kept, attn_g0.sent, attn_g0.sums, *f1, *a1, *f0)
    a0k, a0c = core_step(split_attn(kept), split_attn(sent))
    f1 = parts[:2]
    f0 = second_step(*parts[4:])
    a0k, a0c, *_ = hold(a0k, a0c, f0[0])
    a0 = first_step(a0k, a0c)
    attn_g0.sums, a1k, a1c, *f0 = hold(sums, *parts[2:4], *f0, a0[0])[:-1]
    a1 = line_step(unit, a1k, a1c)
    f0 = third_step(*f0)
    a0 = second_step(*a0)
    f0 = line_step(unit, *f0)
    a0 = third_step(*a0)
    a0 = line_step(unit, *a0)
    while unit * 2 < lines * line_unit:
        unit *= 2
        f1, a1, f0, a0 = [line_step(unit, *parts) for parts in (f1, a1, f0, a0)]
    ffn_grads = [(two0, one0), (two1, one1)]

    small = []
    for layer, attn_g in ((0, attn_g0), (1, attn_g1)):
        two, one = ffn_grads[layer]
        a, f = attn_g.sums, two.sums
        sums = jnp.concatenate([a[:4], f[2:3], a[4:5], f[0:1], a[5:6], f[1:2]])
        sums = sums.reshape(9, count, rows).transpose(1, 0, 2).reshape(count, 9 * rows)
        sums = jnp.dot(hot.astype(f32), sums, precision=lax.Precision.HIGHEST)
        bias = jnp.concatenate([two.gbias, one.gbias]).reshape(count, hidden)
        small += [sums, bias]
    small = jnp.concatenate(small, axis=1)
    for bits, size in ((core_bit, 2), (x_bit, 4), (y_bit, 8)):
        kept = small[: count // size]
        small = kept + swap(small[count // size :], bits)
    bit = 1
    relative = [lax.dynamic_index_in_dim(small, own_line ^ n, 0) for n in range(lines)]
    while bit < lines:
        sent = jnp.concatenate(relative[bit :: 2 * bit])
        came = swap(sent, bit * line_unit)
        for n, place in enumerate(range(0, lines, 2 * bit)):
            relative[place] = relative[place] + came[n : n + 1]
        bit *= 2
    small = relative[0][0].reshape(layer_count, small_len)

    own_attn = jnp.stack([total_of(*a0), total_of(*a1)]).reshape(layer_count, 4, slots, width)
    own_ffn = jnp.stack([total_of(*f0), total_of(*f1)]).reshape(layer_count, 2, hidden, width)
    return (
        result[None],
        attn_g0.gx[None],
        own_attn[:, :3, :rows],
        own_attn[:, 3, :rows],
        small[:, : 5 * rows].reshape(layer_count, 5, rows),
        small[:, 5 * rows : 7 * rows].reshape(layer_count, 2, rows),
        small[:, 7 * rows : 9 * rows].reshape(layer_count, 2, rows),
        own_ffn[:, 0],
        own_ffn[:, 1],
        small[:, 9 * rows :],
    )


def solution(mesh):
    in_specs = (
        P(("batch", "ffn", "mp"), None, None),
        P(None, None, ("batch", "ffn", "mp"), None),
        P(None, ("batch", "ffn", "mp"), None),
        P(None, None, ("batch", "ffn", "mp")),
        P(None, None, ("batch", "ffn", "mp")),
        P(None, None, ("batch", "ffn", "mp")),
        P(None, ("batch", "ffn", "mp"), None),
        P(None, ("batch", "ffn", "mp"), None),
        P(None, ("batch", "ffn", "mp")),
        P(("batch", "ffn", "mp")),
        P(),
        P(("batch", "ffn", "mp"), None),
        P(("batch", "ffn", "mp"), None, None),
    )
    out_specs = (
        P(("batch", "ffn", "mp"), None, None),
        P(("batch", "ffn", "mp"), None, None),
        P(None, None, ("batch", "ffn", "mp"), None),
        P(None, ("batch", "ffn", "mp"), None),
        P(None, None, ("batch", "ffn", "mp")),
        P(None, None, ("batch", "ffn", "mp")),
        P(None, None, ("batch", "ffn", "mp")),
        P(None, ("batch", "ffn", "mp"), None),
        P(None, ("batch", "ffn", "mp"), None),
        P(None, ("batch", "ffn", "mp")),
    )
    sizes = tuple(mesh.shape[name] for name in AXES)
    return jax.shard_map(partial(shards, sizes), mesh=mesh, in_specs=in_specs, out_specs=out_specs, check_vma=False)
```

```python
from functools import partial
import math
from types import SimpleNamespace

import jax
import jax.numpy as jnp
from jax import lax
from jax.experimental import pallas as pl
from jax.experimental.pallas import tpu as pltpu
from jax.sharding import PartitionSpec as P

HEADS = 20
HEAD_DIM = 32


norm_eps = 1e-05
mask_value = -1e30


def rope_tables(length, head_width):
    half_width = head_width // 2
    freqs = jnp.exp(
        jnp.arange(half_width, dtype=jnp.float32) * (-2.0 * math.log(10000.0) / head_width)
    )
    angles = jnp.arange(length, dtype=jnp.float32)[:, None] * freqs[None, :]
    return (jnp.cos(angles), jnp.sin(angles))


AXES = ("batch", "ffn", "mp")
CUT = 2


def after(value, *others):
    return lax.optimization_barrier((value, *others))[0]


def pad_rows(rows):
    return -(-(rows + 1) // 8) * 8


GROUP = 128 // HEAD_DIM
VMEM_LIMIT = 56 * 1024 * 1024
SMALL_LIMIT = 24 * 1024 * 1024


def dot_nn(left, right):
    return lax.dot_general(
        left, right, (((1,), (0,)), ((), ())), preferred_element_type=jnp.float32
    )


def dot_nt(left, right):
    return lax.dot_general(
        left, right, (((1,), (1,)), ((), ())), preferred_element_type=jnp.float32
    )


def dot_tn(left, right):
    return lax.dot_general(
        left, right, (((0,), (0,)), ((), ())), preferred_element_type=jnp.float32
    )


def norm_parts(values):
    centred = values - jnp.mean(values, axis=-1, keepdims=True)
    variance = jnp.mean(centred * centred, axis=-1, keepdims=True)
    inverse = lax.rsqrt(variance + norm_eps)
    return (centred * inverse, inverse)


def norm_grad(grad, values, gain_row):
    unit, inverse = norm_parts(values)
    scaled = grad * gain_row
    mean_one = jnp.mean(scaled, axis=-1, keepdims=True)
    mean_two = jnp.mean(scaled * unit, axis=-1, keepdims=True)
    into = inverse * (scaled - mean_one - unit * mean_two)
    grad_gain = jnp.sum(grad * unit, axis=0, keepdims=True)
    grad_shift = jnp.sum(grad, axis=0, keepdims=True)
    return (into, grad_gain, grad_shift)


def turn(values, cos_ref, sin_ref, sign):
    half = HEAD_DIM // 2
    lanes = lax.broadcasted_iota(jnp.int32, (values.shape[0], 128), 1)
    low_half = lanes % HEAD_DIM < half
    parts = []
    for start in range(0, values.shape[1], 128):
        part = values[:, start : start + 128]
        partner = jnp.where(
            low_half, pltpu.roll(part, 128 - half, 1), pltpu.roll(part, half, 1)
        )
        parts.append(part * cos_ref[...] + sign * (partner * sin_ref[...]))
    return jnp.concatenate(parts, axis=1)


def head_lanes(block, head):
    lanes = lax.broadcasted_iota(jnp.int32, block.shape, 1)
    return jnp.where(lanes // HEAD_DIM == head, block, jnp.zeros_like(block))


def sds(shape, dtype):
    return jax.ShapeDtypeStruct(shape, dtype)


def whole(shape):
    return pl.BlockSpec(shape, lambda *_: (0,) * len(shape))


def call(body, name, grid, ins, outs, scratch, flops, moved, prefetch=None, aliases=None, limit=None):
    names = list(ins) + list(outs) + list(scratch)
    lead = 0 if prefetch is None else 1

    def kernel(*refs):
        named = dict(zip(names, refs[lead:]))
        if lead:
            named.update(own=refs[0])
        body(SimpleNamespace(**named))

    in_specs = [spec or whole(array.shape) for array, spec in ins.values()]
    out_specs = [spec or whole(shape) for shape, _, spec in outs.values()]
    out_shape = [sds(shape, dtype) for shape, dtype, _ in outs.values()]
    scratch_shapes = [pltpu.VMEM(shape, dtype) for shape, dtype in scratch.values()]
    operands = ([] if prefetch is None else [prefetch]) + [array for array, _ in ins.values()]
    in_names, out_names = list(ins), list(outs)
    pairs = {
        in_names.index(a) + lead: out_names.index(b) for a, b in (aliases or {}).items()
    }
    results = pl.pallas_call(
        kernel,
        grid_spec=pltpu.PrefetchScalarGridSpec(
            num_scalar_prefetch=lead,
            grid=grid,
            in_specs=in_specs,
            out_specs=out_specs,
            scratch_shapes=scratch_shapes,
        ),
        out_shape=out_shape,
        input_output_aliases=pairs,
        compiler_params=pltpu.CompilerParams(vmem_limit_bytes=limit or VMEM_LIMIT),
        cost_estimate=pl.CostEstimate(flops=flops, bytes_accessed=moved, transcendentals=0),
        name=name,
    )(*operands)
    return SimpleNamespace(**dict(zip(out_names, results)))


def attn_open(r):
    unit, _ = norm_parts(r.x[...])
    h_one = (unit * r.vec[4:5] + r.vec[5:6]).astype(jnp.bfloat16)
    r.h_rel[...] = dot_nn(h_one, (r.sg if hasattr(r, "sg") else r.sa)[...]).astype(jnp.bfloat16)
    wabs = r.wabs
    for j, ref in enumerate((r.w0, r.w1, r.w2, r.w3) if hasattr(r, "w0") else ()):
        wabs[j] = dot_nn(r.sa[...], rows_of(ref)).astype(jnp.bfloat16)
    for j in () if hasattr(r, "w0") else range(4):
        half = r.wa.shape[1]
        spread = r.sa if j < 2 or not hasattr(r, "sb") else r.sb
        own, came = (r.wa, r.wa2) if j < 2 else (r.wb, r.wb2)
        placed = dot_nn(spread[:, :half], own[j % 2])
        placed += dot_nn(spread[:, half:], came[j % 2])
        wabs[j] = placed.astype(jnp.bfloat16)
    query = dot_nn(h_one, wabs[0]) + r.vec[0:1]
    query = turn(query, r.cos, r.sin, 1.0) * HEAD_DIM ** (-0.5)
    r.q[...] = query.astype(jnp.bfloat16)
    r.qt[...] = query.T.astype(jnp.bfloat16)
    key = turn(dot_nn(h_one, wabs[1]) + r.vec[1:2], r.cos, r.sin, 1.0)
    key_bf = key.astype(jnp.bfloat16)
    for start in range(key.shape[1] // 128):
        r.k[start] = key_bf[:, 128 * start : 128 * start + 128]
    r.kt[...] = key.T.astype(jnp.bfloat16)
    value = dot_nn(h_one, wabs[2]) + r.vec[2:3]
    r.v[...] = value.astype(jnp.bfloat16)
    r.vt[...] = value.T.astype(jnp.bfloat16)


def attn_heads(r, group):
    key_block = r.k[group]
    query_t = r.qt[pl.ds(pl.multiple_of(group * 128, 128), 128), :]
    for head in range(GROUP):
        scores = dot_nn(head_lanes(key_block, head), query_t) + r.mask[...]
        top = jnp.max(scores, axis=0, keepdims=True)
        shifted = jnp.exp(scores - top)
        total = jnp.sum(shifted, axis=0, keepdims=True)
        probs = (shifted * (1.0 / total)).astype(jnp.bfloat16)
        r.probs[head] = probs
        rows = pl.ds(pl.multiple_of(group * 128 + head * HEAD_DIM, HEAD_DIM), HEAD_DIM)
        r.att_t[rows, :] = dot_nn(r.vt[rows, :], probs)


def attn_close(r):
    att = r.att_t[...].T.astype(jnp.bfloat16)
    r.att_rel[...] = dot_nn(att, (r.sg if hasattr(r, "sg") else r.sa)[...]).astype(jnp.bfloat16)
    r.mid[...] = r.x[...] + (dot_nn(att, r.wabs[3]) + r.vec[3:4])


def attn_forward(x, parts, spreads, vec, cos, sin, mask, cut, between):
    length, width = x.shape
    spots = (spreads["sg"] if "sg" in spreads else spreads["sa"]).shape[1]
    groups = width // 128
    b16, f32 = jnp.bfloat16, jnp.float32
    opening = dict(x=x, **parts, **spreads)
    tables = dict(vec=vec, cos=cos, sin=sin, mask=mask)
    made = dict(
        wabs=((4, width, width), b16, None),
        h_rel=((length, spots), b16, None),
        q=((length, width), b16, None),
        kt=((width, length), b16, None),
        v=((length, width), b16, None),
    )
    work = dict(
        qt=((width, length), b16),
        k=((groups, length, 128), b16),
        vt=((width, length), b16),
    )
    att_t = dict(att_t=((width, length), f32, None))
    closing = dict(att_rel=((length, spots), b16, None), mid=((length, width), f32, None))

    def probs_out(base):
        spec = pl.BlockSpec((GROUP, length, length), lambda i: (i + base, 0, 0))
        return dict(probs=((HEADS, length, length), b16, spec))

    def plain(arrays):
        return {
            name: array if isinstance(array, tuple) else (array, None)
            for name, array in arrays.items()
        }

    def body(first, last, base, steps):
        def run(r):
            step = pl.program_id(0)
            if first:
                pl.when(step == 0)(lambda: attn_open(r))
            else:

                @pl.when(step == 0)
                def _():
                    r.att_t[: base * 128, :] = r.att_in[: base * 128, :]

            attn_heads(r, step + base)
            if last:
                pl.when(step == steps - 1)(lambda: attn_close(r))

        return run

    if cut == groups:
        return call(
            body(True, True, 0, groups), "attn_fwd", (groups,),
            plain({**opening, **tables}), {**made, **att_t, **closing, **probs_out(0)}, work,
            20_000_000_000, 25_000_000,
        )
    shared = {name: (shape, dtype, None) for name, (shape, dtype) in work.items()}
    one = call(
        body(True, False, 0, cut), "attn_fwd_one", (cut,),
        plain({**opening, **tables}), {**made, **att_t, **shared, **probs_out(0)}, {},
        10_000_000_000, 15_000_000,
    )
    att_in = between(one.att_t)
    ins = plain(
        dict(
            x=x, sa=spreads["sa"], vec=vec, mask=mask, wabs=one.wabs, att_in=att_in,
            qt=one.qt, k=one.k, vt=one.vt,
        )
    )
    ins.update(probs_in=(one.probs, pl.BlockSpec(memory_space=pl.ANY)))
    two = call(
        body(False, True, cut, groups - cut), "attn_fwd_two", (groups - cut,),
        ins, {**att_t, **closing, **probs_out(cut)}, {},
        10_000_000_000, 15_000_000, aliases=dict(probs_in="probs"),
    )
    return SimpleNamespace(**{**vars(one), **vars(two)})


def ffn_specs(kind, arrays, base, hidden, lines, width):
    specs = {}
    rows = lines * hidden
    if kind == "own":
        specs.update(up0=(arrays[0], pl.BlockSpec((2 * rows, width), lambda i, own: (i, 0))))
        for y in range(2):
            spec = pl.BlockSpec((rows, width), lambda i, own, y=y: (2 * y + i, 0))
            specs["down" + str(y)] = (arrays[1], spec)
        return specs
    shape = (1, lines, 1, 1, hidden, width)
    for which, name in enumerate(("up", "down")):
        for y in range(2):

            def index(i, own, y=y, which=which):
                core = base + i // 2
                return ((i % 2) ^ own[0], 0, y ^ own[1], core ^ own[2], which, 0)

            specs[name + str(y)] = (arrays[0], pl.BlockSpec(shape, index))
    return specs


def rows_of(*refs):
    parts = []
    for ref in refs:
        values = ref[...]
        parts.append(values.reshape(-1, values.shape[-1]))
    return jnp.concatenate(parts) if len(parts) > 1 else parts[0]


def up_rows(r):
    return rows_of(r.up0, r.up1) if hasattr(r, "up1") else rows_of(r.up0)


def ffn_forward(own, mid, vec, kind, arrays, bias, lines, hidden, base, steps, before):
    length, width = mid.shape
    block = 2 * lines * hidden
    b16 = jnp.bfloat16
    kept = pl.BlockSpec((1, length, block), lambda i, own: (i, 0, 0))

    def body(r):
        h_two = r.h_two if before is None else r.h_in

        @pl.when(pl.program_id(0) == 0)
        def _():
            if before is None:
                unit, _ = norm_parts(r.mid[...])
                h_two[...] = (unit * r.vec[6:7] + r.vec[7:8]).astype(b16)
                r.out[...] = r.mid[...] + r.vec[8:9]
            else:
                r.out[...] = r.so_far[...]

        pre = dot_nt(h_two[...], up_rows(r)) + r.bias[0]
        cdf = 0.5 * (1.0 + lax.erf(pre * (0.5**0.5)))
        act = (pre * cdf).astype(b16)
        r.act[0] = act
        slope = cdf + pre * (jnp.exp(-0.5 * pre * pre) * (1.0 / math.sqrt(2.0 * math.pi)))
        r.slope[0] = slope.astype(b16)
        r.out[...] += dot_nn(act, rows_of(r.down0, r.down1))

    ins = ffn_specs(kind, arrays, base, hidden, lines, width)
    ins.update(
        bias=(
            bias.reshape(steps, 1, block),
            pl.BlockSpec((1, 1, block), lambda i, own: (i, 0, 0)),
        ),
    )
    outs = dict(
        out=((length, width), jnp.float32, None),
        act=((steps, length, block), b16, kept),
        slope=((steps, length, block), b16, kept),
    )
    if before is None:
        ins.update(mid=(mid, None), vec=(vec, None))
        outs.update(h_two=((length, width), b16, None))
    else:
        ins.update(h_in=(before.h_two, None), so_far=(before.out, None))
    name = "ffn_fwd_one" if before is None else "ffn_fwd_two"
    return call(body, name, (steps,), ins, outs, {}, 5_000_000_000, 10_000_000, prefetch=own)


def ffn_backward(
    own, grad, mid, vec, kept, at, h_two, kind, arrays, lines, hidden, base, gh_in
):
    length, width = mid.shape
    block = 2 * lines * hidden
    b16, f32 = jnp.bfloat16, jnp.float32
    last = gh_in is not None
    wide = pl.BlockSpec((1, length, block), lambda i, own: (i + at, 0, 0))

    def body(r):
        @pl.when(pl.program_id(0) == 0)
        def _():
            r.gf[...] = r.g[...].astype(b16)
            r.gh[...] = r.gh_in[...] if last else jnp.zeros_like(r.gh)

        gf = r.gf[...]
        g_down = dot_tn(r.act[0], gf)
        g_act = dot_nt(gf, rows_of(r.down0, r.down1))
        g_pre = (g_act * r.slope[0].astype(f32)).astype(b16)
        g_up = dot_tn(g_pre, r.h_two[...])
        for n in range(2 * lines):
            rows = slice(n * hidden, (n + 1) * hidden)
            r.grads[0, n // lines, n % lines, 0] = g_up[rows].astype(b16)
            r.grads[0, n // lines, n % lines, 1] = g_down[rows].astype(b16)
        r.gbias[0] = jnp.sum(g_pre.astype(f32), axis=0, keepdims=True)
        r.gh[...] += dot_nn(g_pre, up_rows(r))
        if last:

            @pl.when(pl.program_id(0) == 1)
            def _():
                into, grad_gain, grad_shift = norm_grad(
                    r.gh[...], r.mid[...], r.vec[6:7]
                )
                r.gmid[...] = r.g[...] + into
                r.sums[...] = jnp.zeros_like(r.sums)
                r.sums[0:1] = grad_gain
                r.sums[1:2] = grad_shift
                r.sums[2:3] = jnp.sum(r.gf[...].astype(f32), axis=0, keepdims=True)

    ins = dict(
        g=(grad, None),
        h_two=(h_two, None),
        act=(kept.act, wide),
        slope=(kept.slope, wide),
        **ffn_specs(kind, arrays, base, hidden, lines, width),
    )
    outs = dict(
        grads=(
            (2, 2, lines, 2, hidden, width),
            b16,
            pl.BlockSpec((1, 2, lines, 2, hidden, width), lambda i, own: (i, 0, 0, 0, 0, 0)),
        ),
        gbias=((2, 1, block), f32, pl.BlockSpec((1, 1, block), lambda i, own: (i, 0, 0))),
    )
    scratch = dict(gf=((length, width), b16))
    if last:
        ins.update(gh_in=(gh_in, None), mid=(mid, None), vec=(vec, None))
        outs.update(gmid=((length, width), f32, None), sums=((8, width), f32, None))
        scratch.update(gh=((length, width), f32))
    else:
        outs.update(gh=((length, width), f32, None))
    name = "ffn_bwd_two" if last else "ffn_bwd_one"
    return call(body, name, (2,), ins, outs, scratch, 9_000_000_000, 15_000_000, prefetch=own)


def put_pieces(r, index, values):
    count, _, slots, _ = r.kept.shape
    for piece in range(2 * count):
        ref = r.kept if piece < count else r.sent
        ref[piece % count, index] = values[piece * slots : (piece + 1) * slots].astype(ref.dtype)


def attn_grad_open(r):
    b16 = jnp.bfloat16
    r.ga[...] = r.gmid[...].astype(b16)
    put_pieces(r, 3, dot_tn(r.att_rel[...], r.ga[...]))
    gatt = dot_nt(r.ga[...], r.wabs[3]).astype(b16)
    for start in range(gatt.shape[1] // 128):
        lanes = slice(128 * start, 128 * start + 128)
        r.gatt[start] = gatt[:, lanes]
        r.qs[start] = r.q[:, lanes]
        r.vs[start] = r.v[:, lanes]
    gatt_t = gatt.astype(jnp.float32).T
    r.gatt_t[...] = gatt_t.astype(b16)
    for head in range(HEADS):
        rows = slice(head * HEAD_DIM, (head + 1) * HEAD_DIM)
        r.inner[head] = jnp.sum(gatt_t[rows] * r.att_t[rows], axis=0, keepdims=True)


def attn_grad_heads(r, group):
    gatt_block, q_block, v_block = r.gatt[group], r.qs[group], r.vs[group]
    gatt_t = r.gatt_t[pl.ds(pl.multiple_of(group * 128, 128), 128), :]
    dk = jnp.zeros(q_block.shape, jnp.float32)
    dv = jnp.zeros(q_block.shape, jnp.float32)
    for head in range(GROUP):
        probs = r.probs[head]
        gprobs = dot_nn(head_lanes(v_block, head), gatt_t)
        inner = r.inner[group * GROUP + head]
        gscores = (probs.astype(jnp.float32) * (gprobs - inner)).astype(jnp.bfloat16)
        dv += dot_nn(probs, head_lanes(gatt_block, head))
        dk += dot_nn(gscores, head_lanes(q_block, head))
        rows = pl.ds(pl.multiple_of(group * 128 + head * HEAD_DIM, HEAD_DIM), HEAD_DIM)
        r.dqt[rows, :] = dot_nn(r.kt[rows, :], gscores)
    r.dk[group] = dk
    r.dv[group] = dv


def attn_grad_close(r):
    b16, f32 = jnp.bfloat16, jnp.float32

    def joined(ref):
        return jnp.concatenate([ref[i] for i in range(ref.shape[0])], axis=1)

    def rounded(values):
        return values.astype(b16).astype(f32)

    gq = rounded(r.dqt[...].T) * HEAD_DIM ** (-0.5)
    gproj = [
        turn(gq, r.cos, r.sin, -1.0).astype(b16),
        turn(rounded(joined(r.dk)), r.cos, r.sin, -1.0).astype(b16),
        joined(r.dv).astype(b16),
    ]
    r.sums[...] = jnp.zeros_like(r.sums)
    gh = jnp.zeros(r.gx.shape, f32)
    for j in range(3):
        put_pieces(r, j, dot_tn(r.h_rel[...], gproj[j]))
        r.sums[j : j + 1] = jnp.sum(gproj[j].astype(f32), axis=0, keepdims=True)
        gh += dot_nt(gproj[j], r.wabs[j])
    into, grad_gain, grad_shift = norm_grad(gh, r.x[...], r.vec[4:5])
    r.gx[...] = r.gmid[...] + into
    r.sums[3:4] = jnp.sum(r.ga[...].astype(f32), axis=0, keepdims=True)
    r.sums[4:5] = grad_gain
    r.sums[5:6] = grad_shift


def attn_backward(slots, gmid, x, vec, cos, sin, saved):
    length, width = x.shape
    spots = saved.h_rel.shape[1]
    half = spots // slots // 2
    groups = width // 128
    b16, f32 = jnp.bfloat16, jnp.float32

    def body(r):
        step = pl.program_id(0)
        pl.when(step == 0)(lambda: attn_grad_open(r))
        attn_grad_heads(r, step)
        pl.when(step == groups - 1)(lambda: attn_grad_close(r))

    full = dict(
        gmid=gmid, x=x, vec=vec, cos=cos, sin=sin, wabs=saved.wabs, h_rel=saved.h_rel,
        q=saved.q, kt=saved.kt, v=saved.v, att_t=saved.att_t, att_rel=saved.att_rel,
    )
    ins = {name: (array, None) for name, array in full.items()}
    ins.update(
        probs=(saved.probs, pl.BlockSpec((GROUP, length, length), lambda i: (i, 0, 0)))
    )
    split = ((groups, length, 128), b16)
    sums = ((groups, length, 128), f32)
    return call(
        body, "attn_bwd", (groups,), ins,
        dict(
            gx=((length, width), f32, None),
            kept=((half, 4, slots, width), b16, None),
            sent=((half, 4, slots, width), b16, None),
            sums=((8, width), f32, None),
        ),
        dict(
            ga=((length, width), b16),
            gatt=split,
            qs=split,
            vs=split,
            gatt_t=((width, length), b16),
            inner=((HEADS, 1, length), f32),
            dqt=((width, length), f32),
            dk=sums,
            dv=sums,
        ),
        30_000_000_000, 30_000_000,
    )


def total_of(one, two):
    return one.astype(jnp.float32) + two.astype(jnp.float32)


def add_core(kept, came):
    _, _, lines, _, rows, width = kept.shape
    b16 = jnp.bfloat16
    both = pl.BlockSpec((2, 2, 1, 2, rows, width), lambda i: (0, 0, i, 0, 0, 0))
    one = ((2, lines, rows, width), b16, pl.BlockSpec((2, 1, rows, width), lambda i: (0, i, 0, 0)))

    def body(r):
        for n in range(2):
            r.ak[n, 0] = total_of(r.kept[0, n, 0, 0], r.came[0, n, 0, 0]).astype(b16)
            r.at[n, 0] = total_of(r.kept[1, n, 0, 0], r.came[1, n, 0, 0]).astype(b16)
            r.bk[n, 0] = total_of(r.kept[n, 0, 0, 1], r.came[n, 0, 0, 1]).astype(b16)
            r.bt[n, 0] = total_of(r.kept[n, 1, 0, 1], r.came[n, 1, 0, 1]).astype(b16)

    made = call(
        body, "add_core", (lines,), dict(kept=(kept, both), came=(came, both)),
        dict(ak=one, at=one, bk=one, bt=one), {}, 10_000_000, 10_000_000, limit=SMALL_LIMIT,
    )
    return (made.ak, made.at, made.bk, made.bt)


def add_first(ak, ac, bk, bc):
    _, lines, rows, width = ak.shape
    b16 = jnp.bfloat16
    steps = max(1, lines // 2)
    block = lines // steps
    both = pl.BlockSpec((2, block, rows, width), lambda i: (0, i, 0, 0))
    one = ((lines, rows, width), b16, pl.BlockSpec((block, rows, width), lambda i: (i, 0, 0)))

    def body(r):
        r.a0[...] = total_of(r.ak[0], r.ac[0]).astype(b16)
        r.a1[...] = total_of(r.ak[1], r.ac[1]).astype(b16)
        r.b0[...] = total_of(r.bk[0], r.bc[0]).astype(b16)
        r.b1[...] = total_of(r.bk[1], r.bc[1]).astype(b16)

    made = call(
        body, "add_first", (steps,),
        dict(ak=(ak, both), ac=(ac, both), bk=(bk, both), bc=(bc, both)),
        dict(a0=one, a1=one, b0=one, b1=one), {}, 10_000_000, 10_000_000, limit=SMALL_LIMIT,
    )
    return (made.a0, made.a1, made.b0, made.b1)


def add_second(own, ak, ac, bk, bc):
    lines, rows, width = ak.shape
    b16 = jnp.bfloat16
    half = lines // 2

    def place(i):
        order, unit, left = 0, 1, half
        while left:
            order += (i // left % 2) * unit
            unit, left = unit * 2, left // 2
        return order

    shape = (half, 2, rows, width)

    def body(r):
        for n in range(lines):
            line = place(n) ^ r.own[3]
            ref = r.kept if n < half else r.sent
            ref[n % half, 0] = total_of(r.ak[line], r.ac[line]).astype(b16)
            ref[n % half, 1] = total_of(r.bk[line], r.bc[line]).astype(b16)

    made = call(
        body, "add_second", (1,),
        dict(ak=(ak, None), ac=(ac, None), bk=(bk, None), bc=(bc, None)),
        dict(kept=(shape, b16, None), sent=(shape, b16, None)), {},
        10_000_000, 5_000_000, prefetch=own, limit=SMALL_LIMIT,
    )
    return (made.kept, made.sent)


def add_line(kept, came):
    half, _, rows, width = kept.shape
    shape = (half // 2, 2, rows, width)

    def body(r):
        total = total_of(r.kept[...], r.came[...])
        r.low[...] = total[: half // 2]
        r.high[...] = total[half // 2 :].astype(jnp.bfloat16)

    made = call(
        body, "add_line", (1,), dict(kept=(kept, None), came=(came, None)),
        dict(low=(shape, jnp.float32, None), high=(shape, jnp.bfloat16, None)), {},
        10_000_000, 2_000_000, limit=SMALL_LIMIT,
    )
    return (made.low, made.high)


def shards(
    sizes,
    tokens,
    qkv_weight,
    out_weight,
    proj_bias,
    norm_gain,
    norm_shift,
    up_weight,
    down_weight,
    up_bias,
    seq_order,
    seq_length,
    mlm_mask,
    cotangent,
):
    _, length, width = tokens.shape
    layer_count = qkv_weight.shape[0]
    _, ffn_size, core_size = sizes
    lines = ffn_size // 2
    count = 2 * ffn_size * core_size
    x_bit, y_bit, core_bit, line_unit = ffn_size * core_size, core_size, 1, 2 * core_size
    own_id = lax.axis_index(AXES)
    own_x = (own_id // x_bit) % 2
    own_y = (own_id // y_bit) % 2
    own_core = own_id % 2
    own_line = (own_id // line_unit) % lines
    own = jnp.stack([own_x, own_y, own_core, own_line]).astype(jnp.int32)
    rows = qkv_weight.shape[2]
    slots = pad_rows(rows)
    hidden = up_weight.shape[1]
    b16, f32 = jnp.bfloat16, jnp.float32

    def device(x, y, line, core):
        return (x * ffn_size + line * 2 + y) * core_size + core

    def swap(values, bits):
        return lax.ppermute(values, AXES, [(i, i ^ bits) for i in range(count)])

    def grow(values, bits, axis):
        return jnp.concatenate([values, swap(values, bits)], axis=axis)

    def line_swaps(values):
        return [swap(values, n * line_unit) for n in range(1, lines)]

    def line_join(values, came):
        joined = jnp.stack([values] + list(came))
        bit = lines // 2
        while bit:
            pairs = joined.reshape(lines // (2 * bit), 2, bit, *values.shape)
            joined = jnp.where((own_line & bit) > 0, jnp.flip(pairs, 1), pairs)
            joined = joined.reshape(lines, *values.shape)
            bit //= 2
        return joined

    def attn_lines(values, came):
        joined = line_join(values, came).transpose(1, 0, 2, 3)
        joined = joined.reshape(4, lines * slots, width)
        return (joined[:2], joined[2:])

    def hold(value, *others):
        return lax.optimization_barrier((value, *others))

    def along(values, came):
        return jnp.concatenate([values, came], axis=1)

    order_ids = jnp.arange(seq_length.shape[0], dtype=jnp.int32)
    slot_length = jnp.sum(jnp.where(seq_order[0] == order_ids, seq_length, 0))
    key_ok = jnp.arange(length, dtype=jnp.int32) < slot_length
    loss_weight = jnp.where(key_ok & (mlm_mask[0] > 0), 1.0, 0.0).astype(f32)
    local_count = jnp.sum(loss_weight)
    count_high = jnp.floor(local_count / 256.0)
    count_low = local_count - 256.0 * count_high
    small_len = 9 * rows + hidden
    layers = range(layer_count)
    small_row = jnp.concatenate(
        [
            part.reshape(-1)
            for layer in layers
            for part in (proj_bias[layer], norm_gain[layer], norm_shift[layer], up_bias[layer])
        ]
        + [count_high[None], count_low[None]]
    ).astype(b16)
    small_row = jnp.pad(small_row, (0, width - small_row.shape[0]))
    spare = jnp.zeros((4, slots - rows, width), b16)
    spare_at = jnp.arange(4 * (slots - rows)).reshape(4, slots - rows, 1) == 0
    spare = jnp.where(spare_at, small_row[None, None], spare)
    attn = jnp.concatenate([qkv_weight[0], out_weight[0][None]]).astype(b16)
    attn = jnp.concatenate([attn, spare], axis=1)
    attn, up_weight, down_weight, qkv_late, out_late = lax.optimization_barrier(
        (attn, up_weight, down_weight, qkv_weight[1], out_weight[1])
    )

    def ffn_piece(layer):
        return jnp.stack([up_weight[layer], down_weight[layer]]).astype(b16)

    def pair(values, came, bit):
        high = (own_line & bit) > 0
        return jnp.stack(
            [jnp.where(high, came, values), jnp.where(high, values, came)], axis=1
        ).reshape(-1, *values.shape[1:])

    part_a, part_b = attn_lines(attn, line_swaps(attn))
    ffn = after(ffn_piece(0), part_a)[None]
    bit = lines // 2
    came_a, came_b, came = (swap(part_a, y_bit), swap(part_b, x_bit), swap(ffn, bit * line_unit))
    came_a, came_b, came = hold(came_a, came_b, came)
    part_a, part_b = along(part_a, came_a), along(part_b, came_b)
    ffn = pair(ffn, came, bit)
    bit //= 2
    came_a, came_b, came = (swap(part_a, x_bit), swap(part_b, y_bit), swap(ffn, bit * line_unit))
    came_a, came_b, came = hold(came_a, came_b, came)
    part_a, part_b = along(part_a, came_a), along(part_b, came_b)
    ffn = pair(ffn, came, bit)
    while bit > 1:
        bit //= 2
        ffn = pair(ffn, swap(ffn, bit * line_unit), bit)
    half_a, half_b = (swap(part_a, core_bit), swap(part_b, core_bit))
    up_all = ffn[:, 0].reshape(lines * hidden, width)
    down_all = ffn[:, 1].reshape(lines * hidden, width)
    up_came, down_came = (swap(up_all, y_bit), swap(down_all, x_bit))

    next_attn = jnp.concatenate([qkv_late, out_late[None]]).astype(b16)
    next_attn = jnp.pad(next_attn, ((0, 0), (0, slots - rows), (0, 0)))
    next_attn = after(next_attn, ffn)
    next_came = line_swaps(next_attn)
    late = after(ffn_piece(1).reshape(2 * hidden, width), part_a, part_b)
    late = lax.all_gather(late, AXES, axis=0, tiled=False)
    late = late.reshape(2, lines, 2, 2, late.shape[1], width)
    late_kind = "own" if hidden % 16 else "late"
    late_weights = [(late,), (late,)]
    if late_kind == "own":
        turned = late[:, :, :, :, : 2 * hidden].reshape(2, lines, 2, 2, 2, hidden, width)
        for axis, odd in ((0, own_x), (2, own_y), (3, own_core)):
            turned = jnp.where(odd > 0, jnp.flip(turned, axis), turned)
        late_up = turned[:, :, :, :, 0].transpose(3, 0, 2, 1, 4, 5)
        late_down = turned[:, :, :, :, 1].transpose(3, 2, 0, 1, 4, 5)
        late_weights = [
            (late_up[n].reshape(-1, width), late_down[n].reshape(-1, width)) for n in range(2)
        ]

    index = jnp.arange(count, dtype=jnp.int32)
    line_at = index % lines
    low_at = index // lines % 2
    high_at = index // (2 * lines) % 2
    core_at = (index // (4 * lines)) ^ own_core
    owners_a = device(high_at ^ own_x, low_at ^ own_y, line_at, core_at)
    owners_b = device(low_at ^ own_x, high_at ^ own_y, line_at, core_at)

    def spread_of(owners, size):
        slot_ids = jnp.arange(size, dtype=jnp.int32)
        source_row = jnp.where(
            slot_ids[None, :] < rows, owners[:, None] * rows + slot_ids[None, :], -1
        ).reshape(count * size)
        return (jnp.arange(width, dtype=jnp.int32)[:, None] == source_row[None, :]).astype(b16)

    spread_a, spread_b = spread_of(owners_a, slots), spread_of(owners_b, slots)
    hot = owners_a[:, None] == index[None, :]
    cos_half, sin_half = rope_tables(length, HEAD_DIM)
    cos = jnp.tile(jnp.concatenate([cos_half, cos_half], axis=1), (1, GROUP))
    sin = jnp.tile(jnp.concatenate([-sin_half, sin_half], axis=1), (1, GROUP))
    mask = jnp.where(key_ok, 0.0, mask_value).astype(f32)[:, None]

    small_own = jnp.concatenate(
        [part[0].reshape(-1, slots, width)[:, rows, :] for part in (part_a, half_a)]
    )
    small_all = dot_tn(hot.astype(b16), small_own)
    spot = layer_count * small_len
    masked_total = jnp.sum(small_all[:, spot] * 256.0 + small_all[:, spot + 1])
    factor = seq_length.shape[0] * length / jnp.maximum(masked_total, 1.0)

    vecs, biases = [], []
    for layer in layers:
        start = layer * small_len
        vec = small_all[:, start : start + 9 * rows]
        vec = vec.reshape(count, 9, rows).transpose(1, 0, 2).reshape(9, width)
        vec = jnp.concatenate([vec[:4], vec[5:6], vec[7:8], vec[6:7], vec[8:9], vec[4:5]])
        vecs.append(jnp.pad(vec, ((0, 7), (0, 0))))
        bias = small_own[:, start + 9 * rows : start + small_len]
        biases.append(bias.reshape(count * hidden).astype(f32))

    kinds = ("own", late_kind)
    groups = width // 128
    streams, attns, ffns = [tokens[0]], [], []

    def between(value):
        nonlocal up_all, down_all, up_came, down_came, next_came
        value, up_came, down_came, *next_came = hold(value, up_came, down_came, *next_came)
        up_all = jnp.concatenate([up_all, up_came])
        down_all = jnp.concatenate([down_all, down_came])
        up_came, down_came = (swap(up_all, x_bit), swap(down_all, y_bit))
        return value

    attns.append(
        attn_forward(
            streams[0],
            dict(wa=part_a, wa2=half_a, wb=part_b, wb2=half_b),
            dict(sa=spread_a, sb=spread_b),
            vecs[0], cos, sin, mask, CUT, between,
        )
    )
    next_a, next_b = attn_lines(next_attn, next_came)
    attns[0].mid, up_came, down_came, next_a, next_b = hold(
        attns[0].mid, up_came, down_came, next_a, next_b
    )
    up_all = jnp.concatenate([up_all, up_came])
    down_all = jnp.concatenate([down_all, down_came])
    up_came, down_came = (swap(up_all, core_bit), swap(down_all, core_bit))
    came_a, came_b = (swap(next_a, y_bit), swap(next_b, x_bit))
    weights = [[(up_all, down_all), (up_came, down_came)], late_weights]

    def ffn_front(layer, base, before):
        halves = 1 if kinds[layer] == "late" else 2
        bias = biases[layer].reshape(halves, -1)[base]
        return ffn_forward(
            own, attns[layer].mid, vecs[layer], kinds[layer], weights[layer][base], bias, lines,
            hidden, base, 4 // halves, before,
        )

    first = ffn_front(0, 0, None)
    first.out, came_a, came_b, up_came, down_came = hold(
        first.out, came_a, came_b, up_came, down_came
    )
    weights[0][1] = (up_came, down_came)
    next_a, next_b = (along(next_a, came_a), along(next_b, came_b))
    came_a, came_b = (swap(next_a, x_bit), swap(next_b, y_bit))
    ffns.append([first, ffn_front(0, 1, first)])
    stream, came_a, came_b = hold(ffns[0][1].out, came_a, came_b)
    streams.append(stream)
    next_a, next_b = (along(next_a, came_a), along(next_b, came_b))
    attns.append(
        attn_forward(
            stream,
            dict(
                wa=next_a, wa2=swap(next_a, core_bit), wb=next_b, wb2=swap(next_b, core_bit),
            ),
            dict(sa=spread_a, sb=spread_b),
            vecs[1], cos, sin, mask, groups, None,
        )
    )
    ffns.append([ffn_front(1, 0, None)])
    if kinds[1] == "own":
        ffns[1].append(ffn_front(1, 1, ffns[1][0]))
    result = ffns[1][-1].out

    def ffn_back(layer, grad, base, gh_in):
        joint = len(ffns[layer]) == 1
        return ffn_backward(
            own, grad, attns[layer].mid, vecs[layer], ffns[layer][0 if joint else base],
            2 * base if joint else 0, ffns[layer][0].h_two, kinds[layer], weights[layer][base],
            lines, hidden, base, gh_in,
        )

    def attn_back(layer, grad_mid):
        return attn_backward(slots, grad_mid, streams[layer], vecs[layer], cos, sin, attns[layer])

    def core_step(kept, sent):
        return (kept, swap(sent, core_bit))

    def first_step(kept, came):
        ak, at, bk, bt = add_core(kept, came)
        return (ak, swap(at, x_bit), bk, swap(bt, y_bit))

    def second_step(*parts):
        a0, a1, b0, b1 = add_first(*parts)
        return (a0, swap(a1, y_bit), b0, swap(b1, x_bit))

    def third_step(*parts):
        kept, sent = add_second(own, *parts)
        return (kept, swap(sent, line_unit))

    def line_step(unit, kept, came):
        kept, sent = add_line(kept, came)
        return (kept, swap(sent, unit))

    def split_attn(values):
        return values.reshape(2, 2, lines, 2, 2 * slots, width)

    grad = cotangent[0] * (loss_weight[:, None] * factor)
    one1 = ffn_back(1, grad, 1, None)
    came = swap(one1.grads, core_bit)
    two1 = ffn_back(1, grad, 0, one1.gh)
    gmid, f1k, f1c = hold(two1.gmid, two1.grads, came)
    f1 = first_step(f1k, f1c)
    attn_g1 = attn_back(1, after(gmid, f1[0]))
    grad, kept, sent, sums, *f1 = hold(
        attn_g1.gx, attn_g1.kept, attn_g1.sent, attn_g1.sums, *f1
    )
    attn_g1.sums = sums
    a1k, a1c = core_step(split_attn(kept), split_attn(sent))
    f1 = second_step(*f1)
    a1k, a1c, *_ = hold(a1k, a1c, f1[0])
    a1 = first_step(a1k, a1c)
    one0 = ffn_back(0, after(grad, f1[0], a1[0]), 1, None)
    gh, sent, *parts = hold(one0.gh, one0.grads, *f1, *a1)
    f0 = swap(sent, core_bit)
    f1 = third_step(*parts[:4])
    a1 = second_step(*parts[4:])
    two0 = ffn_back(0, grad, 0, after(gh, f1[0], a1[0]))
    gmid, f0k, f0c, *parts = hold(two0.gmid, two0.grads, f0, *f1, *a1)
    f0 = first_step(f0k, f0c)
    unit = 2 * line_unit
    f1 = line_step(unit, *parts[:2])
    a1 = third_step(*parts[2:])
    attn_g0 = attn_back(0, after(gmid, f0[0], a1[0], f1[0]))
    kept, sent, sums, *parts = hold(attn_g0.kept, attn_g0.sent, attn_g0.sums, *f1, *a1, *f0)
    a0k, a0c = core_step(split_attn(kept), split_attn(sent))
    f1 = parts[:2]
    f0 = second_step(*parts[4:])
    a0k, a0c, *_ = hold(a0k, a0c, f0[0])
    a0 = first_step(a0k, a0c)
    attn_g0.sums, a1k, a1c, *f0 = hold(sums, *parts[2:4], *f0, a0[0])[:-1]
    a1 = line_step(unit, a1k, a1c)
    f0 = third_step(*f0)
    a0 = second_step(*a0)
    f0 = line_step(unit, *f0)
    a0 = third_step(*a0)
    a0 = line_step(unit, *a0)
    while unit * 2 < lines * line_unit:
        unit *= 2
        f1, a1, f0, a0 = [line_step(unit, *parts) for parts in (f1, a1, f0, a0)]
    ffn_grads = [(two0, one0), (two1, one1)]

    small = []
    for layer, attn_g in ((0, attn_g0), (1, attn_g1)):
        two, one = ffn_grads[layer]
        a, f = attn_g.sums, two.sums
        sums = jnp.concatenate([a[:4], f[2:3], a[4:5], f[0:1], a[5:6], f[1:2]])
        sums = sums.reshape(9, count, rows).transpose(1, 0, 2).reshape(count, 9 * rows)
        bias = jnp.concatenate([two.gbias, one.gbias]).reshape(count, hidden)
        bias = lax.dot_general(
            hot.astype(f32), bias, (((0,), (0,)), ((), ())), precision=lax.Precision.HIGHEST
        )
        small += [sums, bias]
    small = lax.all_to_all(jnp.concatenate(small, axis=1), AXES, 0, 0, tiled=True)
    small = jnp.sum(small, axis=0).reshape(layer_count, small_len)

    own_attn = jnp.stack([total_of(*a0), total_of(*a1)]).reshape(layer_count, 4, slots, width)
    own_ffn = jnp.stack([total_of(*f0), total_of(*f1)]).reshape(layer_count, 2, hidden, width)
    return (
        result[None],
        attn_g0.gx[None],
        own_attn[:, :3, :rows],
        own_attn[:, 3, :rows],
        small[:, : 5 * rows].reshape(layer_count, 5, rows),
        small[:, 5 * rows : 7 * rows].reshape(layer_count, 2, rows),
        small[:, 7 * rows : 9 * rows].reshape(layer_count, 2, rows),
        own_ffn[:, 0],
        own_ffn[:, 1],
        small[:, 9 * rows :],
    )


def solution(mesh):
    in_specs = (
        P(("batch", "ffn", "mp"), None, None),
        P(None, None, ("batch", "ffn", "mp"), None),
        P(None, ("batch", "ffn", "mp"), None),
        P(None, None, ("batch", "ffn", "mp")),
        P(None, None, ("batch", "ffn", "mp")),
        P(None, None, ("batch", "ffn", "mp")),
        P(None, ("batch", "ffn", "mp"), None),
        P(None, ("batch", "ffn", "mp"), None),
        P(None, ("batch", "ffn", "mp")),
        P(("batch", "ffn", "mp")),
        P(),
        P(("batch", "ffn", "mp"), None),
        P(("batch", "ffn", "mp"), None, None),
    )
    out_specs = (
        P(("batch", "ffn", "mp"), None, None),
        P(("batch", "ffn", "mp"), None, None),
        P(None, None, ("batch", "ffn", "mp"), None),
        P(None, ("batch", "ffn", "mp"), None),
        P(None, None, ("batch", "ffn", "mp")),
        P(None, None, ("batch", "ffn", "mp")),
        P(None, None, ("batch", "ffn", "mp")),
        P(None, ("batch", "ffn", "mp"), None),
        P(None, ("batch", "ffn", "mp"), None),
        P(None, ("batch", "ffn", "mp")),
    )
    sizes = tuple(mesh.shape[name] for name in AXES)
    return jax.shard_map(partial(shards, sizes), mesh=mesh, in_specs=in_specs, out_specs=out_specs, check_vma=False)
```

```python
from functools import partial
import math
from types import SimpleNamespace

import jax
import jax.numpy as jnp
from jax import lax
from jax.experimental import pallas as pl
from jax.experimental.pallas import tpu as pltpu
from jax.sharding import PartitionSpec as P

HEADS = 20
HEAD_DIM = 32


norm_eps = 1e-05
mask_value = -1e30


def rope_tables(length, head_width):
    half_width = head_width // 2
    freqs = jnp.exp(
        jnp.arange(half_width, dtype=jnp.float32) * (-2.0 * math.log(10000.0) / head_width)
    )
    angles = jnp.arange(length, dtype=jnp.float32)[:, None] * freqs[None, :]
    return (jnp.cos(angles), jnp.sin(angles))


AXES = ("batch", "ffn", "mp")
CUT = 2


def after(value, *others):
    return lax.optimization_barrier((value, *others))[0]


def pad_rows(rows):
    return -(-(rows + 1) // 8) * 8


GROUP = 128 // HEAD_DIM
VMEM_LIMIT = 56 * 1024 * 1024
SMALL_LIMIT = 24 * 1024 * 1024


def dot_nn(left, right):
    return lax.dot_general(
        left, right, (((1,), (0,)), ((), ())), preferred_element_type=jnp.float32
    )


def dot_nt(left, right):
    return lax.dot_general(
        left, right, (((1,), (1,)), ((), ())), preferred_element_type=jnp.float32
    )


def dot_tn(left, right):
    return lax.dot_general(
        left, right, (((0,), (0,)), ((), ())), preferred_element_type=jnp.float32
    )


def norm_parts(values):
    centred = values - jnp.mean(values, axis=-1, keepdims=True)
    variance = jnp.mean(centred * centred, axis=-1, keepdims=True)
    inverse = lax.rsqrt(variance + norm_eps)
    return (centred * inverse, inverse)


def norm_grad(grad, values, gain_row):
    unit, inverse = norm_parts(values)
    scaled = grad * gain_row
    mean_one = jnp.mean(scaled, axis=-1, keepdims=True)
    mean_two = jnp.mean(scaled * unit, axis=-1, keepdims=True)
    into = inverse * (scaled - mean_one - unit * mean_two)
    grad_gain = jnp.sum(grad * unit, axis=0, keepdims=True)
    grad_shift = jnp.sum(grad, axis=0, keepdims=True)
    return (into, grad_gain, grad_shift)


def turn(values, cos_ref, sin_ref, sign):
    half = HEAD_DIM // 2
    lanes = lax.broadcasted_iota(jnp.int32, (values.shape[0], 128), 1)
    low_half = lanes % HEAD_DIM < half
    parts = []
    for start in range(0, values.shape[1], 128):
        part = values[:, start : start + 128]
        partner = jnp.where(
            low_half, pltpu.roll(part, 128 - half, 1), pltpu.roll(part, half, 1)
        )
        parts.append(part * cos_ref[...] + sign * (partner * sin_ref[...]))
    return jnp.concatenate(parts, axis=1)


def head_lanes(block, head):
    lanes = lax.broadcasted_iota(jnp.int32, block.shape, 1)
    return jnp.where(lanes // HEAD_DIM == head, block, jnp.zeros_like(block))


def sds(shape, dtype):
    return jax.ShapeDtypeStruct(shape, dtype)


def whole(shape):
    return pl.BlockSpec(shape, lambda *_: (0,) * len(shape))


EAGER = object()


def call(
    body, name, grid, ins, outs, scratch, flops, moved, prefetch=None, aliases=None, limit=None,
    lazy=None,
):
    lazy = {n: a if isinstance(a, tuple) else (a, None) for n, a in (lazy or {}).items()}
    eager = {n: (shape, dtype) for n, (shape, dtype, spec) in outs.items() if spec is EAGER}
    names = list(ins) + list(lazy) + list(outs) + list(scratch) + list(lazy) + list(eager)
    lead = 0 if prefetch is None else 1

    def picked(array, index):
        return array.shape if index is None else array.shape[1:]

    def kernel(*refs):
        named = dict(zip(names, refs[lead:]))
        if lead:
            named.update(own=refs[0])
        if lazy:
            sources = refs[lead + len(ins) : lead + len(ins) + len(lazy)]
            copies = {}
            for n, (name, (_, index)) in enumerate(lazy.items()):
                source = sources[n] if index is None else sources[n].at[index]
                copies[name] = pltpu.make_async_copy(source, named[name], refs[-1].at[n])

            @pl.when(pl.program_id(0) == 0)
            def _():
                for copy in copies.values():
                    copy.start()

            def need(*wanted):
                for name in lazy:
                    if any(named[name] is ref for ref in wanted):
                        copies[name].wait()

            named.update(need=need)
        flushed = []
        if eager:
            out_at = lead + len(ins) + len(lazy)
            targets = dict(zip(outs, refs[out_at : out_at + len(outs)]))
            sems = refs[-2] if lazy else refs[-1]

            def copy_out(name, index, n):
                source, target = named[name], targets[name]
                if index is not None:
                    source, target = source.at[:, index], target.at[:, index]
                return pltpu.make_async_copy(source, target, sems.at[n])

            def flush(ref, index=None):
                for name in eager:
                    if named[name] is ref:
                        flushed.append((name, index, len(flushed)))
                        copy_out(*flushed[-1]).start()

            named.update(flush=flush)
        body(SimpleNamespace(**named))
        if eager:

            @pl.when(pl.program_id(0) == grid[0] - 1)
            def _():
                for entry in flushed:
                    copy_out(*entry).wait()

    raw = pl.BlockSpec(memory_space=pl.ANY)
    in_specs = [spec or whole(array.shape) for array, spec in ins.values()] + [raw] * len(lazy)
    out_specs = [
        raw if spec is EAGER else spec or whole(shape) for shape, _, spec in outs.values()
    ]
    out_shape = [sds(shape, dtype) for shape, dtype, _ in outs.values()]
    scratch_shapes = [pltpu.VMEM(shape, dtype) for shape, dtype in scratch.values()]
    scratch_shapes += [pltpu.VMEM(picked(a, index), a.dtype) for a, index in lazy.values()]
    scratch_shapes += [pltpu.VMEM(shape, dtype) for shape, dtype in eager.values()]
    if eager:
        scratch_shapes.append(pltpu.SemaphoreType.DMA((16,)))
    if lazy:
        scratch_shapes.append(pltpu.SemaphoreType.DMA((len(lazy),)))
    operands = ([] if prefetch is None else [prefetch]) + [array for array, _ in ins.values()]
    operands += [array for array, _ in lazy.values()]
    in_names, out_names = list(ins), list(outs)
    pairs = {
        in_names.index(a) + lead: out_names.index(b) for a, b in (aliases or {}).items()
    }
    results = pl.pallas_call(
        kernel,
        grid_spec=pltpu.PrefetchScalarGridSpec(
            num_scalar_prefetch=lead,
            grid=grid,
            in_specs=in_specs,
            out_specs=out_specs,
            scratch_shapes=scratch_shapes,
        ),
        out_shape=out_shape,
        input_output_aliases=pairs,
        compiler_params=pltpu.CompilerParams(vmem_limit_bytes=limit or VMEM_LIMIT),
        cost_estimate=pl.CostEstimate(flops=flops, bytes_accessed=moved, transcendentals=0),
        name=name,
    )(*operands)
    return SimpleNamespace(**dict(zip(out_names, results)))


def attn_open(r, shared):
    r.need(r.x)
    unit, _ = norm_parts(r.x[...])
    h_one = (unit * r.vec[4:5] + r.vec[5:6]).astype(jnp.bfloat16)
    r.need(r.sa)
    r.h_rel[...] = dot_nn(h_one, r.sa[...]).astype(jnp.bfloat16)
    r.flush(r.h_rel)

    def place(j, spread, own, came):
        half = own.shape[1]
        placed = dot_nn(spread[:, :half], own[j % 2])
        placed += dot_nn(spread[:, half:], came[j % 2])
        r.wabs[j] = placed.astype(jnp.bfloat16)

    r.need(r.wa, r.wa2)
    place(0, r.sa, r.wa, r.wa2)
    place(1, r.sa, r.wa, r.wa2)
    r.need(r.cos, r.sin)
    query = dot_nn(h_one, r.wabs[0]) + r.vec[0:1]
    query = turn(query, r.cos, r.sin, 1.0) * HEAD_DIM ** (-0.5)
    r.q[...] = query.astype(jnp.bfloat16)
    r.flush(r.q)
    r.qt[...] = query.T.astype(jnp.bfloat16)
    key = turn(dot_nn(h_one, r.wabs[1]) + r.vec[1:2], r.cos, r.sin, 1.0)
    key_bf = key.astype(jnp.bfloat16)
    for start in range(key.shape[1] // 128):
        r.k[start] = key_bf[:, 128 * start : 128 * start + 128]
    r.kt[...] = key.T.astype(jnp.bfloat16)
    r.flush(r.kt)
    r.need(r.sb, r.wb, r.wb2)
    place(2, r.sb, r.wb, r.wb2)
    place(3, r.sb, r.wb, r.wb2)
    r.flush(r.wabs)
    value = dot_nn(h_one, r.wabs[2]) + r.vec[2:3]
    r.v[...] = value.astype(jnp.bfloat16)
    r.flush(r.v)
    r.vt[...] = value.T.astype(jnp.bfloat16)
    if shared:
        for ref in (r.qt, r.k, r.vt):
            r.flush(ref)


def attn_heads(r, group):
    key_block = r.k[group]
    query_t = r.qt[pl.ds(pl.multiple_of(group * 128, 128), 128), :]
    for head in range(GROUP):
        scores = dot_nn(head_lanes(key_block, head), query_t) + r.mask[...]
        top = jnp.max(scores, axis=0, keepdims=True)
        shifted = jnp.exp(scores - top)
        total = jnp.sum(shifted, axis=0, keepdims=True)
        probs = (shifted * (1.0 / total)).astype(jnp.bfloat16)
        r.probs[head] = probs
        rows = pl.ds(pl.multiple_of(group * 128 + head * HEAD_DIM, HEAD_DIM), HEAD_DIM)
        r.att_t[rows, :] = dot_nn(r.vt[rows, :], probs)


def attn_close(r, wo):
    att = r.att_t[...].T.astype(jnp.bfloat16)
    r.att_rel[...] = dot_nn(att, r.sa[...]).astype(jnp.bfloat16)
    r.mid[...] = r.x[...] + (dot_nn(att, wo) + r.vec[3:4])


def attn_forward(x, parts, spreads, vec, cos, sin, mask, cut, between):
    length, width = x.shape
    spots = spreads["sa"].shape[1]
    groups = width // 128
    b16, f32 = jnp.bfloat16, jnp.float32
    opening = dict(
        x=x, sa=spreads["sa"], wa=parts["wa"], wa2=parts["wa2"], cos=cos, sin=sin,
        sb=spreads["sb"], wb=parts["wb"], wb2=parts["wb2"],
    )
    tables = dict(vec=vec, mask=mask)
    made = dict(
        wabs=((4, width, width), b16, EAGER),
        h_rel=((length, spots), b16, EAGER),
        q=((length, width), b16, EAGER),
        kt=((width, length), b16, EAGER),
        v=((length, width), b16, EAGER),
    )
    work = dict(
        qt=((width, length), b16),
        k=((groups, length, 128), b16),
        vt=((width, length), b16),
    )
    att_t = dict(att_t=((width, length), f32, None))
    closing = dict(att_rel=((length, spots), b16, None), mid=((length, width), f32, None))

    def probs_out(base):
        spec = pl.BlockSpec((GROUP, length, length), lambda i: (i + base, 0, 0))
        return dict(probs=((HEADS, length, length), b16, spec))

    def plain(arrays):
        return {
            name: array if isinstance(array, tuple) else (array, None)
            for name, array in arrays.items()
        }

    def body(first, last, base, steps):
        def run(r):
            step = pl.program_id(0)
            if first:
                pl.when(step == 0)(lambda: attn_open(r, not last))

            attn_heads(r, step + base)
            if last:

                @pl.when(step == steps - 1)
                def _():
                    if not first:
                        r.need(r.att_in, r.sa, r.wo, r.x)
                        r.att_t[: base * 128, :] = r.att_in[: base * 128, :]
                    attn_close(r, r.wabs[3] if first else r.wo[...])

        return run

    if cut == groups:
        return call(
            body(True, True, 0, groups), "attn_fwd", (groups,),
            plain(tables), {**made, **att_t, **closing, **probs_out(0)}, work,
            20_000_000_000, 25_000_000, lazy=opening,
        )
    shared = {name: (shape, dtype, EAGER) for name, (shape, dtype) in work.items()}
    one = call(
        body(True, False, 0, cut), "attn_fwd_one", (cut,),
        plain(tables), {**made, **att_t, **shared, **probs_out(0)}, {},
        10_000_000_000, 15_000_000, lazy=opening,
    )
    att_in = between(one.att_t)
    ins = plain(
        dict(
            vec=vec, mask=mask, k=one.k, qt=one.qt, vt=one.vt,
        )
    )
    ins.update(probs_in=(one.probs, pl.BlockSpec(memory_space=pl.ANY)))
    two = call(
        body(False, True, cut, groups - cut), "attn_fwd_two", (groups - cut,),
        ins, {**att_t, **closing, **probs_out(cut)}, {},
        10_000_000_000, 15_000_000, aliases=dict(probs_in="probs"),
        lazy=dict(att_in=att_in, sa=spreads["sa"], wo=(one.wabs, 3), x=x),
    )
    return SimpleNamespace(**{**vars(one), **vars(two)})


def ffn_specs(kind, arrays, base, hidden, lines, width):
    specs = {}
    rows = lines * hidden
    if kind == "own":
        specs.update(up0=(arrays[0], pl.BlockSpec((2 * rows, width), lambda i, own: (i, 0))))
        for y in range(2):
            spec = pl.BlockSpec((rows, width), lambda i, own, y=y: (2 * y + i, 0))
            specs["down" + str(y)] = (arrays[1], spec)
        return specs
    shape = (1, lines, 1, 1, hidden, width)
    for which, name in enumerate(("up", "down")):
        for y in range(2):

            def index(i, own, y=y, which=which):
                core = base + i // 2
                return ((i % 2) ^ own[0], 0, y ^ own[1], core ^ own[2], which, 0)

            specs[name + str(y)] = (arrays[0], pl.BlockSpec(shape, index))
    return specs


def rows_of(*refs):
    parts = []
    for ref in refs:
        values = ref[...]
        parts.append(values.reshape(-1, values.shape[-1]))
    return jnp.concatenate(parts) if len(parts) > 1 else parts[0]


def up_rows(r):
    return rows_of(r.up0, r.up1) if hasattr(r, "up1") else rows_of(r.up0)


def ffn_forward(own, mid, vec, kind, arrays, bias, lines, hidden, base, steps, before):
    length, width = mid.shape
    block = 2 * lines * hidden
    b16 = jnp.bfloat16
    kept = pl.BlockSpec((1, length, block), lambda i, own: (i, 0, 0))

    def body(r):
        h_two = r.h_two if before is None else r.h_in

        @pl.when(pl.program_id(0) == 0)
        def _():
            if before is None:
                unit, _ = norm_parts(r.mid[...])
                h_two[...] = (unit * r.vec[6:7] + r.vec[7:8]).astype(b16)
                r.out[...] = r.mid[...] + r.vec[8:9]
            else:
                r.out[...] = jnp.zeros_like(r.out)

        pre = dot_nt(h_two[...], up_rows(r)) + r.bias[0]
        cdf = 0.5 * (1.0 + lax.erf(pre * (0.5**0.5)))
        act = (pre * cdf).astype(b16)
        r.act[0] = act
        slope = cdf + pre * (jnp.exp(-0.5 * pre * pre) * (1.0 / math.sqrt(2.0 * math.pi)))
        r.slope[0] = slope.astype(b16)
        r.out[...] += dot_nn(act, rows_of(r.down0, r.down1))
        if before is not None:

            @pl.when(pl.program_id(0) == steps - 1)
            def _():
                r.need(r.so_far)
                r.out[...] += r.so_far[...]

    lazy = {}
    ins = ffn_specs(kind, arrays, base, hidden, lines, width)
    ins.update(
        bias=(
            bias.reshape(steps, 1, block),
            pl.BlockSpec((1, 1, block), lambda i, own: (i, 0, 0)),
        ),
    )
    outs = dict(
        out=((length, width), jnp.float32, None),
        act=((steps, length, block), b16, kept),
        slope=((steps, length, block), b16, kept),
    )
    if before is None:
        ins.update(mid=(mid, None), vec=(vec, None))
        outs.update(h_two=((length, width), b16, None))
    else:
        ins.update(h_in=(before.h_two, None))
        lazy.update(so_far=before.out)
    name = "ffn_fwd_one" if before is None else "ffn_fwd_two"
    return call(body, name, (steps,), ins, outs, {}, 5_000_000_000, 10_000_000, prefetch=own, lazy=lazy)


def ffn_backward(
    own, grad, mid, vec, kept, at, h_two, kind, arrays, lines, hidden, base, gh_in
):
    length, width = mid.shape
    block = 2 * lines * hidden
    b16, f32 = jnp.bfloat16, jnp.float32
    last = gh_in is not None
    wide = pl.BlockSpec((1, length, block), lambda i, own: (i + at, 0, 0))

    def body(r):
        @pl.when(pl.program_id(0) == 0)
        def _():
            r.gf[...] = r.g[...].astype(b16)
            r.gh[...] = jnp.zeros_like(r.gh)

        gf = r.gf[...]
        g_down = dot_tn(r.act[0], gf)
        g_act = dot_nt(gf, rows_of(r.down0, r.down1))
        g_pre = (g_act * r.slope[0].astype(f32)).astype(b16)
        g_up = dot_tn(g_pre, r.h_two[...])
        for n in range(2 * lines):
            rows = slice(n * hidden, (n + 1) * hidden)
            r.grads[0, n // lines, n % lines, 0] = g_up[rows].astype(b16)
            r.grads[0, n // lines, n % lines, 1] = g_down[rows].astype(b16)
        r.gbias[0] = jnp.sum(g_pre.astype(f32), axis=0, keepdims=True)
        r.gh[...] += dot_nn(g_pre, up_rows(r))
        if last:

            @pl.when(pl.program_id(0) == 1)
            def _():
                r.need(r.gh_in, r.mid)
                into, grad_gain, grad_shift = norm_grad(
                    r.gh[...] + r.gh_in[...], r.mid[...], r.vec[6:7]
                )
                r.gmid[...] = r.g[...] + into
                r.sums[...] = jnp.zeros_like(r.sums)
                r.sums[0:1] = grad_gain
                r.sums[1:2] = grad_shift
                r.sums[2:3] = jnp.sum(r.gf[...].astype(f32), axis=0, keepdims=True)

    ins = dict(
        g=(grad, None),
        h_two=(h_two, None),
        act=(kept.act, wide),
        slope=(kept.slope, wide),
        **ffn_specs(kind, arrays, base, hidden, lines, width),
    )
    outs = dict(
        grads=(
            (2, 2, lines, 2, hidden, width),
            b16,
            pl.BlockSpec((1, 2, lines, 2, hidden, width), lambda i, own: (i, 0, 0, 0, 0, 0)),
        ),
        gbias=((2, 1, block), f32, pl.BlockSpec((1, 1, block), lambda i, own: (i, 0, 0))),
    )
    scratch = dict(gf=((length, width), b16))
    lazy = {}
    if last:
        ins.update(vec=(vec, None))
        lazy.update(gh_in=gh_in, mid=mid)
        outs.update(gmid=((length, width), f32, None), sums=((8, width), f32, None))
        scratch.update(gh=((length, width), f32))
    else:
        outs.update(gh=((length, width), f32, None))
    name = "ffn_bwd_two" if last else "ffn_bwd_one"
    return call(
        body, name, (2,), ins, outs, scratch, 9_000_000_000, 15_000_000, prefetch=own, lazy=lazy
    )


def put_pieces(r, index, values):
    count, _, slots, _ = r.kept.shape
    for piece in range(2 * count):
        ref = r.kept if piece < count else r.sent
        ref[piece % count, index] = values[piece * slots : (piece + 1) * slots].astype(ref.dtype)
    r.flush(r.sent, index)
    r.flush(r.kept, index)


def attn_grad_open(r):
    b16 = jnp.bfloat16
    r.need(r.gmid, r.w3)
    r.ga[...] = r.gmid[...].astype(b16)
    gatt = dot_nt(r.ga[...], r.w3[...]).astype(b16)
    r.need(r.q, r.v)
    for start in range(gatt.shape[1] // 128):
        lanes = slice(128 * start, 128 * start + 128)
        r.gatt[start] = gatt[:, lanes]
        r.qs[start] = r.q[:, lanes]
        r.vs[start] = r.v[:, lanes]
    gatt_t = gatt.astype(jnp.float32).T
    r.gatt_t[...] = gatt_t.astype(b16)
    r.need(r.att_t)
    for head in range(HEADS):
        rows = slice(head * HEAD_DIM, (head + 1) * HEAD_DIM)
        r.inner[head] = jnp.sum(gatt_t[rows] * r.att_t[rows], axis=0, keepdims=True)
    r.need(r.kt)


def attn_grad_heads(r, group):
    gatt_block, q_block, v_block = r.gatt[group], r.qs[group], r.vs[group]
    gatt_t = r.gatt_t[pl.ds(pl.multiple_of(group * 128, 128), 128), :]
    dk = jnp.zeros(q_block.shape, jnp.float32)
    dv = jnp.zeros(q_block.shape, jnp.float32)
    for head in range(GROUP):
        probs = r.probs[head]
        gprobs = dot_nn(head_lanes(v_block, head), gatt_t)
        inner = r.inner[group * GROUP + head]
        gscores = (probs.astype(jnp.float32) * (gprobs - inner)).astype(jnp.bfloat16)
        dv += dot_nn(probs, head_lanes(gatt_block, head))
        dk += dot_nn(gscores, head_lanes(q_block, head))
        rows = pl.ds(pl.multiple_of(group * 128 + head * HEAD_DIM, HEAD_DIM), HEAD_DIM)
        r.dqt[rows, :] = dot_nn(r.kt[rows, :], gscores)
    r.dk[group] = dk
    r.dv[group] = dv


def attn_grad_close(r):
    b16, f32 = jnp.bfloat16, jnp.float32

    def joined(ref):
        return jnp.concatenate([ref[i] for i in range(ref.shape[0])], axis=1)

    def rounded(values):
        return values.astype(b16).astype(f32)

    r.need(r.att_rel, r.cos, r.sin, r.h_rel, r.w0, r.w1, r.w2, r.x)
    put_pieces(r, 3, dot_tn(r.att_rel[...], r.ga[...]))
    gq = rounded(r.dqt[...].T) * HEAD_DIM ** (-0.5)
    gproj = [
        turn(gq, r.cos, r.sin, -1.0).astype(b16),
        turn(rounded(joined(r.dk)), r.cos, r.sin, -1.0).astype(b16),
        joined(r.dv).astype(b16),
    ]
    r.sums[...] = jnp.zeros_like(r.sums)
    gh = jnp.zeros(r.gx.shape, f32)
    for j in range(3):
        put_pieces(r, j, dot_tn(r.h_rel[...], gproj[j]))
        r.sums[j : j + 1] = jnp.sum(gproj[j].astype(f32), axis=0, keepdims=True)
        gh += dot_nt(gproj[j], (r.w0, r.w1, r.w2)[j][...])
    into, grad_gain, grad_shift = norm_grad(gh, r.x[...], r.vec[4:5])
    r.gx[...] = r.gmid[...] + into
    r.sums[3:4] = jnp.sum(r.ga[...].astype(f32), axis=0, keepdims=True)
    r.sums[4:5] = grad_gain
    r.sums[5:6] = grad_shift


def attn_backward(slots, gmid, x, vec, cos, sin, saved):
    length, width = x.shape
    spots = saved.h_rel.shape[1]
    half = spots // slots // 2
    groups = width // 128
    b16, f32 = jnp.bfloat16, jnp.float32

    def body(r):
        step = pl.program_id(0)
        pl.when(step == 0)(lambda: attn_grad_open(r))
        attn_grad_heads(r, step)
        pl.when(step == groups - 1)(lambda: attn_grad_close(r))

    lazy = dict(
        gmid=gmid, w3=(saved.wabs, 3), q=saved.q, v=saved.v, att_t=saved.att_t, kt=saved.kt,
        att_rel=saved.att_rel, cos=cos, sin=sin, h_rel=saved.h_rel, w0=(saved.wabs, 0),
        w1=(saved.wabs, 1), w2=(saved.wabs, 2), x=x,
    )
    ins = dict(
        vec=(vec, None),
        probs=(saved.probs, pl.BlockSpec((GROUP, length, length), lambda i: (i, 0, 0))),
    )
    split = ((groups, length, 128), b16)
    sums = ((groups, length, 128), f32)
    return call(
        body, "attn_bwd", (groups,), ins,
        dict(
            gx=((length, width), f32, None),
            kept=((half, 4, slots, width), b16, EAGER),
            sent=((half, 4, slots, width), b16, EAGER),
            sums=((8, width), f32, None),
        ),
        dict(
            ga=((length, width), b16),
            gatt=split,
            qs=split,
            vs=split,
            gatt_t=((width, length), b16),
            inner=((HEADS, 1, length), f32),
            dqt=((width, length), f32),
            dk=sums,
            dv=sums,
        ),
        30_000_000_000, 30_000_000, lazy=lazy,
    )


def total_of(one, two):
    return one.astype(jnp.float32) + two.astype(jnp.float32)


def add_core(kept, came):
    _, _, lines, _, rows, width = kept.shape
    b16 = jnp.bfloat16
    both = pl.BlockSpec((2, 2, 1, 2, rows, width), lambda i: (0, 0, i, 0, 0, 0))
    one = ((2, lines, rows, width), b16, pl.BlockSpec((2, 1, rows, width), lambda i: (0, i, 0, 0)))

    def body(r):
        for n in range(2):
            r.ak[n, 0] = total_of(r.kept[0, n, 0, 0], r.came[0, n, 0, 0]).astype(b16)
            r.at[n, 0] = total_of(r.kept[1, n, 0, 0], r.came[1, n, 0, 0]).astype(b16)
            r.bk[n, 0] = total_of(r.kept[n, 0, 0, 1], r.came[n, 0, 0, 1]).astype(b16)
            r.bt[n, 0] = total_of(r.kept[n, 1, 0, 1], r.came[n, 1, 0, 1]).astype(b16)

    made = call(
        body, "add_core", (lines,), dict(kept=(kept, both), came=(came, both)),
        dict(ak=one, at=one, bk=one, bt=one), {}, 10_000_000, 10_000_000, limit=SMALL_LIMIT,
    )
    return (made.ak, made.at, made.bk, made.bt)


def add_first(ak, ac, bk, bc):
    _, lines, rows, width = ak.shape
    b16 = jnp.bfloat16
    steps = max(1, lines // 2)
    block = lines // steps
    both = pl.BlockSpec((2, block, rows, width), lambda i: (0, i, 0, 0))
    one = ((lines, rows, width), b16, pl.BlockSpec((block, rows, width), lambda i: (i, 0, 0)))

    def body(r):
        r.a0[...] = total_of(r.ak[0], r.ac[0]).astype(b16)
        r.a1[...] = total_of(r.ak[1], r.ac[1]).astype(b16)
        r.b0[...] = total_of(r.bk[0], r.bc[0]).astype(b16)
        r.b1[...] = total_of(r.bk[1], r.bc[1]).astype(b16)

    made = call(
        body, "add_first", (steps,),
        dict(ak=(ak, both), ac=(ac, both), bk=(bk, both), bc=(bc, both)),
        dict(a0=one, a1=one, b0=one, b1=one), {}, 10_000_000, 10_000_000, limit=SMALL_LIMIT,
    )
    return (made.a0, made.a1, made.b0, made.b1)


def add_second(own, ak, ac, bk, bc):
    lines, rows, width = ak.shape
    b16 = jnp.bfloat16
    half = lines // 2

    def place(i):
        order, unit, left = 0, 1, half
        while left:
            order += (i // left % 2) * unit
            unit, left = unit * 2, left // 2
        return order

    shape = (half, 2, rows, width)

    def body(r):
        for n in range(lines):
            line = place(n) ^ r.own[3]
            ref = r.kept if n < half else r.sent
            ref[n % half, 0] = total_of(r.ak[line], r.ac[line]).astype(b16)
            ref[n % half, 1] = total_of(r.bk[line], r.bc[line]).astype(b16)

    made = call(
        body, "add_second", (1,),
        dict(ak=(ak, None), ac=(ac, None), bk=(bk, None), bc=(bc, None)),
        dict(kept=(shape, b16, None), sent=(shape, b16, None)), {},
        10_000_000, 5_000_000, prefetch=own, limit=SMALL_LIMIT,
    )
    return (made.kept, made.sent)


def add_line(kept, came):
    half, _, rows, width = kept.shape
    shape = (half // 2, 2, rows, width)

    def body(r):
        total = total_of(r.kept[...], r.came[...])
        r.low[...] = total[: half // 2]
        r.high[...] = total[half // 2 :].astype(jnp.bfloat16)

    made = call(
        body, "add_line", (1,), dict(kept=(kept, None), came=(came, None)),
        dict(low=(shape, jnp.float32, None), high=(shape, jnp.bfloat16, None)), {},
        10_000_000, 2_000_000, limit=SMALL_LIMIT,
    )
    return (made.low, made.high)


def shards(
    sizes,
    tokens,
    qkv_weight,
    out_weight,
    proj_bias,
    norm_gain,
    norm_shift,
    up_weight,
    down_weight,
    up_bias,
    seq_order,
    seq_length,
    mlm_mask,
    cotangent,
):
    _, length, width = tokens.shape
    layer_count = qkv_weight.shape[0]
    _, ffn_size, core_size = sizes
    lines = ffn_size // 2
    count = 2 * ffn_size * core_size
    x_bit, y_bit, core_bit, line_unit = ffn_size * core_size, core_size, 1, 2 * core_size
    own_id = lax.axis_index(AXES)
    own_x = (own_id // x_bit) % 2
    own_y = (own_id // y_bit) % 2
    own_core = own_id % 2
    own_line = (own_id // line_unit) % lines
    own = jnp.stack([own_x, own_y, own_core, own_line]).astype(jnp.int32)
    rows = qkv_weight.shape[2]
    slots = pad_rows(rows)
    hidden = up_weight.shape[1]
    b16, f32 = jnp.bfloat16, jnp.float32

    def device(x, y, line, core):
        return (x * ffn_size + line * 2 + y) * core_size + core

    def swap(values, bits):
        return lax.ppermute(values, AXES, [(i, i ^ bits) for i in range(count)])

    def grow(values, bits, axis):
        return jnp.concatenate([values, swap(values, bits)], axis=axis)

    def line_swaps(values):
        return [swap(values, n * line_unit) for n in range(1, lines)]

    def line_join(values, came):
        joined = jnp.stack([values] + list(came))
        bit = lines // 2
        while bit:
            pairs = joined.reshape(lines // (2 * bit), 2, bit, *values.shape)
            joined = jnp.where((own_line & bit) > 0, jnp.flip(pairs, 1), pairs)
            joined = joined.reshape(lines, *values.shape)
            bit //= 2
        return joined

    def attn_lines(values, came):
        joined = line_join(values, came).transpose(1, 0, 2, 3)
        joined = joined.reshape(4, lines * slots, width)
        return (joined[:2], joined[2:])

    def hold(value, *others):
        return lax.optimization_barrier((value, *others))

    def along(values, came):
        return jnp.concatenate([values, came], axis=1)

    order_ids = jnp.arange(seq_length.shape[0], dtype=jnp.int32)
    slot_length = jnp.sum(jnp.where(seq_order[0] == order_ids, seq_length, 0))
    key_ok = jnp.arange(length, dtype=jnp.int32) < slot_length
    loss_weight = jnp.where(key_ok & (mlm_mask[0] > 0), 1.0, 0.0).astype(f32)
    local_count = jnp.sum(loss_weight)
    count_high = jnp.floor(local_count / 256.0)
    count_low = local_count - 256.0 * count_high
    small_len = 9 * rows + hidden
    layers = range(layer_count)
    small_row = jnp.concatenate(
        [
            part.reshape(-1)
            for layer in layers
            for part in (proj_bias[layer], norm_gain[layer], norm_shift[layer], up_bias[layer])
        ]
        + [count_high[None], count_low[None]]
    ).astype(b16)
    small_row = jnp.pad(small_row, (0, width - small_row.shape[0]))
    spare = jnp.zeros((4, slots - rows, width), b16)
    spare_at = jnp.arange(4 * (slots - rows)).reshape(4, slots - rows, 1) == 0
    spare = jnp.where(spare_at, small_row[None, None], spare)
    attn = jnp.concatenate([qkv_weight[0], out_weight[0][None]]).astype(b16)
    attn = jnp.concatenate([attn, spare], axis=1)
    attn, up_weight, down_weight, qkv_late, out_late = lax.optimization_barrier(
        (attn, up_weight, down_weight, qkv_weight[1], out_weight[1])
    )

    def ffn_piece(layer):
        return jnp.stack([up_weight[layer], down_weight[layer]]).astype(b16)

    def pair(values, came, bit):
        high = (own_line & bit) > 0
        return jnp.stack(
            [jnp.where(high, came, values), jnp.where(high, values, came)], axis=1
        ).reshape(-1, *values.shape[1:])

    part_a, part_b = attn_lines(attn, line_swaps(attn))
    ffn = after(ffn_piece(0), part_a)[None]
    bit = lines // 2
    came_a, came_b, came = (swap(part_a, y_bit), swap(part_b, x_bit), swap(ffn, bit * line_unit))
    came_a, came_b, came = hold(came_a, came_b, came)
    part_a, part_b = along(part_a, came_a), along(part_b, came_b)
    ffn = pair(ffn, came, bit)
    bit //= 2
    came_a, came_b, came = (swap(part_a, x_bit), swap(part_b, y_bit), swap(ffn, bit * line_unit))
    came_a, came_b, came = hold(came_a, came_b, came)
    part_a, part_b = along(part_a, came_a), along(part_b, came_b)
    ffn = pair(ffn, came, bit)
    while bit > 1:
        bit //= 2
        ffn = pair(ffn, swap(ffn, bit * line_unit), bit)
    half_a, half_b = (swap(part_a, core_bit), swap(part_b, core_bit))
    up_all = ffn[:, 0].reshape(lines * hidden, width)
    down_all = ffn[:, 1].reshape(lines * hidden, width)
    up_came, down_came = (swap(up_all, y_bit), swap(down_all, x_bit))

    next_attn = jnp.concatenate([qkv_late, out_late[None]]).astype(b16)
    next_attn = jnp.pad(next_attn, ((0, 0), (0, slots - rows), (0, 0)))
    next_attn = after(next_attn, ffn)
    next_came = line_swaps(next_attn)
    late = after(ffn_piece(1).reshape(2 * hidden, width), part_a, part_b)
    late = lax.all_gather(late, AXES, axis=0, tiled=False)
    late = late.reshape(2, lines, 2, 2, late.shape[1], width)
    late_kind = "own" if hidden % 16 else "late"
    late_weights = [(late,), (late,)]
    if late_kind == "own":
        turned = late[:, :, :, :, : 2 * hidden].reshape(2, lines, 2, 2, 2, hidden, width)
        for axis, odd in ((0, own_x), (2, own_y), (3, own_core)):
            turned = jnp.where(odd > 0, jnp.flip(turned, axis), turned)
        late_up = turned[:, :, :, :, 0].transpose(3, 0, 2, 1, 4, 5)
        late_down = turned[:, :, :, :, 1].transpose(3, 2, 0, 1, 4, 5)
        late_weights = [
            (late_up[n].reshape(-1, width), late_down[n].reshape(-1, width)) for n in range(2)
        ]

    index = jnp.arange(count, dtype=jnp.int32)
    line_at = index % lines
    low_at = index // lines % 2
    high_at = index // (2 * lines) % 2
    core_at = (index // (4 * lines)) ^ own_core
    owners_a = device(high_at ^ own_x, low_at ^ own_y, line_at, core_at)
    owners_b = device(low_at ^ own_x, high_at ^ own_y, line_at, core_at)

    def spread_of(owners, size):
        slot_ids = jnp.arange(size, dtype=jnp.int32)
        source_row = jnp.where(
            slot_ids[None, :] < rows, owners[:, None] * rows + slot_ids[None, :], -1
        ).reshape(count * size)
        return (jnp.arange(width, dtype=jnp.int32)[:, None] == source_row[None, :]).astype(b16)

    spread_a, spread_b = spread_of(owners_a, slots), spread_of(owners_b, slots)
    hot = owners_a[:, None] == index[None, :]
    cos_half, sin_half = rope_tables(length, HEAD_DIM)
    cos = jnp.tile(jnp.concatenate([cos_half, cos_half], axis=1), (1, GROUP))
    sin = jnp.tile(jnp.concatenate([-sin_half, sin_half], axis=1), (1, GROUP))
    mask = jnp.where(key_ok, 0.0, mask_value).astype(f32)[:, None]

    small_own = jnp.concatenate(
        [part[0].reshape(-1, slots, width)[:, rows, :] for part in (part_a, half_a)]
    )
    small_all = dot_tn(hot.astype(b16), small_own)
    spot = layer_count * small_len
    masked_total = jnp.sum(small_all[:, spot] * 256.0 + small_all[:, spot + 1])
    factor = seq_length.shape[0] * length / jnp.maximum(masked_total, 1.0)

    vecs, biases = [], []
    for layer in layers:
        start = layer * small_len
        vec = small_all[:, start : start + 9 * rows]
        vec = vec.reshape(count, 9, rows).transpose(1, 0, 2).reshape(9, width)
        vec = jnp.concatenate([vec[:4], vec[5:6], vec[7:8], vec[6:7], vec[8:9], vec[4:5]])
        vecs.append(jnp.pad(vec, ((0, 7), (0, 0))))
        bias = small_own[:, start + 9 * rows : start + small_len]
        biases.append(bias.reshape(count * hidden).astype(f32))

    kinds = ("own", late_kind)
    groups = width // 128
    streams, attns, ffns = [tokens[0]], [], []

    def between(value):
        nonlocal up_all, down_all, up_came, down_came, next_came
        value, up_came, down_came, *next_came = hold(value, up_came, down_came, *next_came)
        up_all = jnp.concatenate([up_all, up_came])
        down_all = jnp.concatenate([down_all, down_came])
        up_came, down_came = (swap(up_all, x_bit), swap(down_all, y_bit))
        return value

    attns.append(
        attn_forward(
            streams[0],
            dict(wa=part_a, wa2=half_a, wb=part_b, wb2=half_b),
            dict(sa=spread_a, sb=spread_b),
            vecs[0], cos, sin, mask, CUT, between,
        )
    )
    next_a, next_b = attn_lines(next_attn, next_came)
    attns[0].mid, up_came, down_came, next_a, next_b = hold(
        attns[0].mid, up_came, down_came, next_a, next_b
    )
    up_all = jnp.concatenate([up_all, up_came])
    down_all = jnp.concatenate([down_all, down_came])
    up_came, down_came = (swap(up_all, core_bit), swap(down_all, core_bit))
    came_a, came_b = (swap(next_a, y_bit), swap(next_b, x_bit))
    weights = [[(up_all, down_all), (up_came, down_came)], late_weights]

    def ffn_front(layer, base, before):
        halves = 1 if kinds[layer] == "late" else 2
        bias = biases[layer].reshape(halves, -1)[base]
        return ffn_forward(
            own, attns[layer].mid, vecs[layer], kinds[layer], weights[layer][base], bias, lines,
            hidden, base, 4 // halves, before,
        )

    first = ffn_front(0, 0, None)
    first.out, came_a, came_b, up_came, down_came = hold(
        first.out, came_a, came_b, up_came, down_came
    )
    weights[0][1] = (up_came, down_came)
    next_a, next_b = (along(next_a, came_a), along(next_b, came_b))
    came_a, came_b = (swap(next_a, x_bit), swap(next_b, y_bit))
    ffns.append([first, ffn_front(0, 1, first)])
    stream, came_a, came_b = hold(ffns[0][1].out, came_a, came_b)
    streams.append(stream)
    next_a, next_b = (along(next_a, came_a), along(next_b, came_b))
    attns.append(
        attn_forward(
            stream,
            dict(
                wa=next_a, wa2=swap(next_a, core_bit), wb=next_b, wb2=swap(next_b, core_bit),
            ),
            dict(sa=spread_a, sb=spread_b),
            vecs[1], cos, sin, mask, groups, None,
        )
    )
    ffns.append([ffn_front(1, 0, None)])
    if kinds[1] == "own":
        ffns[1].append(ffn_front(1, 1, ffns[1][0]))
    result = ffns[1][-1].out

    def ffn_back(layer, grad, base, gh_in):
        joint = len(ffns[layer]) == 1
        return ffn_backward(
            own, grad, attns[layer].mid, vecs[layer], ffns[layer][0 if joint else base],
            2 * base if joint else 0, ffns[layer][0].h_two, kinds[layer], weights[layer][base],
            lines, hidden, base, gh_in,
        )

    def attn_back(layer, grad_mid):
        return attn_backward(slots, grad_mid, streams[layer], vecs[layer], cos, sin, attns[layer])

    def core_step(kept, sent):
        return (kept, swap(sent, core_bit))

    def first_step(kept, came):
        ak, at, bk, bt = add_core(kept, came)
        return (ak, swap(at, x_bit), bk, swap(bt, y_bit))

    def second_step(*parts):
        a0, a1, b0, b1 = add_first(*parts)
        return (a0, swap(a1, y_bit), b0, swap(b1, x_bit))

    def third_step(*parts):
        kept, sent = add_second(own, *parts)
        return (kept, swap(sent, line_unit))

    def line_step(unit, kept, came):
        kept, sent = add_line(kept, came)
        return (kept, swap(sent, unit))

    def split_attn(values):
        return values.reshape(2, 2, lines, 2, 2 * slots, width)

    grad = cotangent[0] * (loss_weight[:, None] * factor)
    one1 = ffn_back(1, grad, 1, None)
    came = swap(one1.grads, core_bit)
    two1 = ffn_back(1, grad, 0, one1.gh)
    gmid, f1k, f1c = hold(two1.gmid, two1.grads, came)
    f1 = first_step(f1k, f1c)
    attn_g1 = attn_back(1, after(gmid, f1[0]))
    grad, kept, sent, sums, *f1 = hold(
        attn_g1.gx, attn_g1.kept, attn_g1.sent, attn_g1.sums, *f1
    )
    attn_g1.sums = sums
    a1k, a1c = core_step(split_attn(kept), split_attn(sent))
    f1 = second_step(*f1)
    a1k, a1c, *_ = hold(a1k, a1c, f1[0])
    a1 = first_step(a1k, a1c)
    one0 = ffn_back(0, after(grad, f1[0], a1[0]), 1, None)
    gh, sent, *parts = hold(one0.gh, one0.grads, *f1, *a1)
    f0 = swap(sent, core_bit)
    f1 = third_step(*parts[:4])
    a1 = second_step(*parts[4:])
    two0 = ffn_back(0, grad, 0, after(gh, f1[0], a1[0]))
    gmid, f0k, f0c, *parts = hold(two0.gmid, two0.grads, f0, *f1, *a1)
    f0 = first_step(f0k, f0c)
    unit = 2 * line_unit
    f1 = line_step(unit, *parts[:2])
    a1 = third_step(*parts[2:])
    attn_g0 = attn_back(0, after(gmid, f0[0], a1[0], f1[0]))
    kept, sent, sums, *parts = hold(attn_g0.kept, attn_g0.sent, attn_g0.sums, *f1, *a1, *f0)
    a0k, a0c = core_step(split_attn(kept), split_attn(sent))
    f1 = parts[:2]
    f0 = second_step(*parts[4:])
    a0k, a0c, *_ = hold(a0k, a0c, f0[0])
    a0 = first_step(a0k, a0c)
    attn_g0.sums, a1k, a1c, *f0 = hold(sums, *parts[2:4], *f0, a0[0])[:-1]
    a1 = line_step(unit, a1k, a1c)
    f0 = third_step(*f0)
    a0 = second_step(*a0)
    f0 = line_step(unit, *f0)
    a0 = third_step(*a0)
    a0 = line_step(unit, *a0)
    while unit * 2 < lines * line_unit:
        unit *= 2
        f1, a1, f0, a0 = [line_step(unit, *parts) for parts in (f1, a1, f0, a0)]
    ffn_grads = [(two0, one0), (two1, one1)]

    small = []
    for layer, attn_g in ((0, attn_g0), (1, attn_g1)):
        two, one = ffn_grads[layer]
        a, f = attn_g.sums, two.sums
        sums = jnp.concatenate([a[:4], f[2:3], a[4:5], f[0:1], a[5:6], f[1:2]])
        sums = sums.reshape(9, count, rows).transpose(1, 0, 2).reshape(count, 9 * rows)
        bias = jnp.concatenate([two.gbias, one.gbias]).reshape(count, hidden)
        bias = lax.dot_general(
            hot.astype(f32), bias, (((0,), (0,)), ((), ())), precision=lax.Precision.HIGHEST
        )
        small += [sums, bias]
    small = lax.all_to_all(jnp.concatenate(small, axis=1), AXES, 0, 0, tiled=True)
    small = jnp.sum(small, axis=0).reshape(layer_count, small_len)

    own_attn = jnp.stack([total_of(*a0), total_of(*a1)]).reshape(layer_count, 4, slots, width)
    own_ffn = jnp.stack([total_of(*f0), total_of(*f1)]).reshape(layer_count, 2, hidden, width)
    return (
        result[None],
        attn_g0.gx[None],
        own_attn[:, :3, :rows],
        own_attn[:, 3, :rows],
        small[:, : 5 * rows].reshape(layer_count, 5, rows),
        small[:, 5 * rows : 7 * rows].reshape(layer_count, 2, rows),
        small[:, 7 * rows : 9 * rows].reshape(layer_count, 2, rows),
        own_ffn[:, 0],
        own_ffn[:, 1],
        small[:, 9 * rows :],
    )


def solution(mesh):
    in_specs = (
        P(("batch", "ffn", "mp"), None, None),
        P(None, None, ("batch", "ffn", "mp"), None),
        P(None, ("batch", "ffn", "mp"), None),
        P(None, None, ("batch", "ffn", "mp")),
        P(None, None, ("batch", "ffn", "mp")),
        P(None, None, ("batch", "ffn", "mp")),
        P(None, ("batch", "ffn", "mp"), None),
        P(None, ("batch", "ffn", "mp"), None),
        P(None, ("batch", "ffn", "mp")),
        P(("batch", "ffn", "mp")),
        P(),
        P(("batch", "ffn", "mp"), None),
        P(("batch", "ffn", "mp"), None, None),
    )
    out_specs = (
        P(("batch", "ffn", "mp"), None, None),
        P(("batch", "ffn", "mp"), None, None),
        P(None, None, ("batch", "ffn", "mp"), None),
        P(None, ("batch", "ffn", "mp"), None),
        P(None, None, ("batch", "ffn", "mp")),
        P(None, None, ("batch", "ffn", "mp")),
        P(None, None, ("batch", "ffn", "mp")),
        P(None, ("batch", "ffn", "mp"), None),
        P(None, ("batch", "ffn", "mp"), None),
        P(None, ("batch", "ffn", "mp")),
    )
    sizes = tuple(mesh.shape[name] for name in AXES)
    return jax.shard_map(partial(shards, sizes), mesh=mesh, in_specs=in_specs, out_specs=out_specs, check_vma=False)
```

```python
from functools import partial
import math
from types import SimpleNamespace

import jax
import jax.numpy as jnp
from jax import lax
from jax.experimental import pallas as pl
from jax.experimental.pallas import tpu as pltpu
from jax.sharding import PartitionSpec as P

HEADS = 20
HEAD_DIM = 32


norm_eps = 1e-05
mask_value = -1e30


def rope_tables(length, head_width):
    half_width = head_width // 2
    freqs = jnp.exp(
        jnp.arange(half_width, dtype=jnp.float32) * (-2.0 * math.log(10000.0) / head_width)
    )
    angles = jnp.arange(length, dtype=jnp.float32)[:, None] * freqs[None, :]
    return (jnp.cos(angles), jnp.sin(angles))


AXES = ("batch", "ffn", "mp")
CUT = 2


def after(value, *others):
    return lax.optimization_barrier((value, *others))[0]


def pad_rows(rows):
    return -(-(rows + 1) // 8) * 8


GROUP = 128 // HEAD_DIM
VMEM_LIMIT = 56 * 1024 * 1024
SMALL_LIMIT = 24 * 1024 * 1024


def dot_nn(left, right):
    return lax.dot_general(
        left, right, (((1,), (0,)), ((), ())), preferred_element_type=jnp.float32
    )


def dot_nt(left, right):
    return lax.dot_general(
        left, right, (((1,), (1,)), ((), ())), preferred_element_type=jnp.float32
    )


def dot_tn(left, right):
    return lax.dot_general(
        left, right, (((0,), (0,)), ((), ())), preferred_element_type=jnp.float32
    )


def norm_parts(values):
    centred = values - jnp.mean(values, axis=-1, keepdims=True)
    variance = jnp.mean(centred * centred, axis=-1, keepdims=True)
    inverse = lax.rsqrt(variance + norm_eps)
    return (centred * inverse, inverse)


def norm_grad(grad, values, gain_row):
    unit, inverse = norm_parts(values)
    scaled = grad * gain_row
    mean_one = jnp.mean(scaled, axis=-1, keepdims=True)
    mean_two = jnp.mean(scaled * unit, axis=-1, keepdims=True)
    into = inverse * (scaled - mean_one - unit * mean_two)
    grad_gain = jnp.sum(grad * unit, axis=0, keepdims=True)
    grad_shift = jnp.sum(grad, axis=0, keepdims=True)
    return (into, grad_gain, grad_shift)


def turn(values, cos_ref, sin_ref, sign):
    half = HEAD_DIM // 2
    lanes = lax.broadcasted_iota(jnp.int32, (values.shape[0], 128), 1)
    low_half = lanes % HEAD_DIM < half
    parts = []
    for start in range(0, values.shape[1], 128):
        part = values[:, start : start + 128]
        partner = jnp.where(
            low_half, pltpu.roll(part, 128 - half, 1), pltpu.roll(part, half, 1)
        )
        parts.append(part * cos_ref[...] + sign * (partner * sin_ref[...]))
    return jnp.concatenate(parts, axis=1)


def head_lanes(block, head):
    lanes = lax.broadcasted_iota(jnp.int32, block.shape, 1)
    return jnp.where(lanes // HEAD_DIM == head, block, jnp.zeros_like(block))


def sds(shape, dtype):
    return jax.ShapeDtypeStruct(shape, dtype)


def whole(shape):
    return pl.BlockSpec(shape, lambda *_: (0,) * len(shape))


EAGER = object()


def call(
    body, name, grid, ins, outs, scratch, flops, moved, prefetch=None, aliases=None, limit=None,
    lazy=None,
):
    lazy = {n: a if isinstance(a, tuple) else (a, None) for n, a in (lazy or {}).items()}
    eager = {n: (shape, dtype) for n, (shape, dtype, spec) in outs.items() if spec is EAGER}
    names = list(ins) + list(lazy) + list(outs) + list(scratch) + list(lazy) + list(eager)
    lead = 0 if prefetch is None else 1

    def picked(array, index):
        return array.shape if index is None else array.shape[1:]

    def kernel(*refs):
        named = dict(zip(names, refs[lead:]))
        if lead:
            named.update(own=refs[0])
        if lazy:
            sources = refs[lead + len(ins) : lead + len(ins) + len(lazy)]
            copies = {}
            for n, (name, (_, index)) in enumerate(lazy.items()):
                source = sources[n] if index is None else sources[n].at[index]
                copies[name] = pltpu.make_async_copy(source, named[name], refs[-1].at[n])

            @pl.when(pl.program_id(0) == 0)
            def _():
                for copy in copies.values():
                    copy.start()

            def need(*wanted):
                for name in lazy:
                    if any(named[name] is ref for ref in wanted):
                        copies[name].wait()

            named.update(need=need)
        flushed = []
        if eager:
            out_at = lead + len(ins) + len(lazy)
            targets = dict(zip(outs, refs[out_at : out_at + len(outs)]))
            sems = refs[-2] if lazy else refs[-1]

            def copy_out(name, index, n):
                source, target = named[name], targets[name]
                if index is not None:
                    source, target = source.at[:, index], target.at[:, index]
                return pltpu.make_async_copy(source, target, sems.at[n])

            def flush(ref, index=None):
                for name in eager:
                    if named[name] is ref:
                        flushed.append((name, index, len(flushed)))
                        copy_out(*flushed[-1]).start()

            named.update(flush=flush)
        body(SimpleNamespace(**named))
        if eager:

            @pl.when(pl.program_id(0) == grid[0] - 1)
            def _():
                for entry in flushed:
                    copy_out(*entry).wait()

    raw = pl.BlockSpec(memory_space=pl.ANY)
    in_specs = [spec or whole(array.shape) for array, spec in ins.values()] + [raw] * len(lazy)
    out_specs = [
        raw if spec is EAGER else spec or whole(shape) for shape, _, spec in outs.values()
    ]
    out_shape = [sds(shape, dtype) for shape, dtype, _ in outs.values()]
    scratch_shapes = [pltpu.VMEM(shape, dtype) for shape, dtype in scratch.values()]
    scratch_shapes += [pltpu.VMEM(picked(a, index), a.dtype) for a, index in lazy.values()]
    scratch_shapes += [pltpu.VMEM(shape, dtype) for shape, dtype in eager.values()]
    if eager:
        scratch_shapes.append(pltpu.SemaphoreType.DMA((16,)))
    if lazy:
        scratch_shapes.append(pltpu.SemaphoreType.DMA((len(lazy),)))
    operands = ([] if prefetch is None else [prefetch]) + [array for array, _ in ins.values()]
    operands += [array for array, _ in lazy.values()]
    in_names, out_names = list(ins), list(outs)
    pairs = {
        in_names.index(a) + lead: out_names.index(b) for a, b in (aliases or {}).items()
    }
    results = pl.pallas_call(
        kernel,
        grid_spec=pltpu.PrefetchScalarGridSpec(
            num_scalar_prefetch=lead,
            grid=grid,
            in_specs=in_specs,
            out_specs=out_specs,
            scratch_shapes=scratch_shapes,
        ),
        out_shape=out_shape,
        input_output_aliases=pairs,
        compiler_params=pltpu.CompilerParams(vmem_limit_bytes=limit or VMEM_LIMIT),
        cost_estimate=pl.CostEstimate(flops=flops, bytes_accessed=moved, transcendentals=0),
        name=name,
    )(*operands)
    return SimpleNamespace(**dict(zip(out_names, results)))


def attn_open(r, shared):
    r.need(r.x)
    unit, _ = norm_parts(r.x[...])
    h_one = (unit * r.vec[4:5] + r.vec[5:6]).astype(jnp.bfloat16)
    r.need(r.sa)
    r.h_rel[...] = dot_nn(h_one, r.sa[...]).astype(jnp.bfloat16)
    r.flush(r.h_rel)

    def place(j, spread, own, came):
        half = own.shape[1]
        placed = dot_nn(spread[:, :half], own[j % 2])
        placed += dot_nn(spread[:, half:], came[j % 2])
        r.wabs[j] = placed.astype(jnp.bfloat16)

    r.need(r.wa, r.wa2)
    place(0, r.sa, r.wa, r.wa2)
    place(1, r.sa, r.wa, r.wa2)
    r.need(r.cos, r.sin)
    query = dot_nn(h_one, r.wabs[0]) + r.vec[0:1]
    query = turn(query, r.cos, r.sin, 1.0) * HEAD_DIM ** (-0.5)
    r.q[...] = query.astype(jnp.bfloat16)
    r.flush(r.q)
    r.qt[...] = query.T.astype(jnp.bfloat16)
    key = turn(dot_nn(h_one, r.wabs[1]) + r.vec[1:2], r.cos, r.sin, 1.0)
    key_bf = key.astype(jnp.bfloat16)
    for start in range(key.shape[1] // 128):
        r.k[start] = key_bf[:, 128 * start : 128 * start + 128]
    r.kt[...] = key.T.astype(jnp.bfloat16)
    r.flush(r.kt)
    r.need(r.sb, r.wb, r.wb2)
    place(2, r.sb, r.wb, r.wb2)
    place(3, r.sb, r.wb, r.wb2)
    r.flush(r.wabs)
    value = dot_nn(h_one, r.wabs[2]) + r.vec[2:3]
    r.v[...] = value.astype(jnp.bfloat16)
    r.flush(r.v)
    r.vt[...] = value.T.astype(jnp.bfloat16)
    if shared:
        for ref in (r.qt, r.k, r.vt):
            r.flush(ref)


def attn_heads(r, group):
    key_block = r.k[group]
    query_t = r.qt[pl.ds(pl.multiple_of(group * 128, 128), 128), :]
    for head in range(GROUP):
        scores = dot_nn(head_lanes(key_block, head), query_t) + r.mask[...]
        top = jnp.max(scores, axis=0, keepdims=True)
        shifted = jnp.exp(scores - top)
        total = jnp.sum(shifted, axis=0, keepdims=True)
        probs = (shifted * (1.0 / total)).astype(jnp.bfloat16)
        r.probs[head] = probs
        rows = pl.ds(pl.multiple_of(group * 128 + head * HEAD_DIM, HEAD_DIM), HEAD_DIM)
        r.att_t[rows, :] = dot_nn(r.vt[rows, :], probs)


def attn_close(r, wo):
    att = r.att_t[...].T.astype(jnp.bfloat16)
    r.att_rel[...] = dot_nn(att, r.sa[...]).astype(jnp.bfloat16)
    r.mid[...] = r.x[...] + (dot_nn(att, wo) + r.vec[3:4])


def attn_forward(x, parts, spreads, vec, cos, sin, mask, cut, between):
    length, width = x.shape
    spots = spreads["sa"].shape[1]
    groups = width // 128
    b16, f32 = jnp.bfloat16, jnp.float32
    opening = dict(
        x=x, sa=spreads["sa"], wa=parts["wa"], wa2=parts["wa2"], cos=cos, sin=sin,
        sb=spreads["sb"], wb=parts["wb"], wb2=parts["wb2"],
    )
    tables = dict(vec=vec, mask=mask)
    made = dict(
        wabs=((4, width, width), b16, EAGER),
        h_rel=((length, spots), b16, EAGER),
        q=((length, width), b16, EAGER),
        kt=((width, length), b16, EAGER),
        v=((length, width), b16, EAGER),
    )
    work = dict(
        qt=((width, length), b16),
        k=((groups, length, 128), b16),
        vt=((width, length), b16),
    )
    att_t = dict(att_t=((width, length), f32, None))
    closing = dict(att_rel=((length, spots), b16, None), mid=((length, width), f32, None))

    def probs_out(base):
        spec = pl.BlockSpec((GROUP, length, length), lambda i: (i + base, 0, 0))
        return dict(probs=((HEADS, length, length), b16, spec))

    def plain(arrays):
        return {
            name: array if isinstance(array, tuple) else (array, None)
            for name, array in arrays.items()
        }

    def body(first, last, base, steps):
        def run(r):
            step = pl.program_id(0)
            if first:
                pl.when(step == 0)(lambda: attn_open(r, not last))

            attn_heads(r, step + base)
            if last:

                @pl.when(step == steps - 1)
                def _():
                    if not first:
                        r.need(r.att_in, r.sa, r.wo, r.x)
                        r.att_t[: base * 128, :] = r.att_in[: base * 128, :]
                    attn_close(r, r.wabs[3] if first else r.wo[...])

        return run

    if cut == groups:
        return call(
            body(True, True, 0, groups), "attn_fwd", (groups,),
            plain(tables), {**made, **att_t, **closing, **probs_out(0)}, work,
            20_000_000_000, 25_000_000, lazy=opening,
        )
    shared = {name: (shape, dtype, EAGER) for name, (shape, dtype) in work.items()}
    one = call(
        body(True, False, 0, cut), "attn_fwd_one", (cut,),
        plain(tables), {**made, **att_t, **shared, **probs_out(0)}, {},
        10_000_000_000, 15_000_000, lazy=opening,
    )
    att_in = between(one.att_t)
    ins = plain(
        dict(
            vec=vec, mask=mask, k=one.k, qt=one.qt, vt=one.vt,
        )
    )
    ins.update(probs_in=(one.probs, pl.BlockSpec(memory_space=pl.ANY)))
    two = call(
        body(False, True, cut, groups - cut), "attn_fwd_two", (groups - cut,),
        ins, {**att_t, **closing, **probs_out(cut)}, {},
        10_000_000_000, 15_000_000, aliases=dict(probs_in="probs"),
        lazy=dict(att_in=att_in, sa=spreads["sa"], wo=(one.wabs, 3), x=x),
    )
    return SimpleNamespace(**{**vars(one), **vars(two)})


def ffn_specs(kind, arrays, base, hidden, lines, width):
    specs = {}
    rows = lines * hidden
    if kind == "own":
        specs.update(up0=(arrays[0], pl.BlockSpec((2 * rows, width), lambda i, own: (i, 0))))
        for y in range(2):
            spec = pl.BlockSpec((rows, width), lambda i, own, y=y: (2 * y + i, 0))
            specs["down" + str(y)] = (arrays[1], spec)
        return specs
    shape = (1, lines, 1, 1, hidden, width)
    for which, name in enumerate(("up", "down")):
        for y in range(2):

            def index(i, own, y=y, which=which):
                core = base + i // 2
                return ((i % 2) ^ own[0], 0, y ^ own[1], core ^ own[2], which, 0)

            specs[name + str(y)] = (arrays[0], pl.BlockSpec(shape, index))
    return specs


def rows_of(*refs):
    parts = []
    for ref in refs:
        values = ref[...]
        parts.append(values.reshape(-1, values.shape[-1]))
    return jnp.concatenate(parts) if len(parts) > 1 else parts[0]


def up_rows(r):
    return rows_of(r.up0, r.up1) if hasattr(r, "up1") else rows_of(r.up0)


def ffn_forward(own, mid, vec, kind, arrays, bias, lines, hidden, base, steps, before):
    length, width = mid.shape
    block = 2 * lines * hidden
    b16 = jnp.bfloat16
    kept = pl.BlockSpec((1, length, block), lambda i, own: (i, 0, 0))

    def body(r):
        h_two = r.h_two if before is None else r.h_in

        @pl.when(pl.program_id(0) == 0)
        def _():
            if before is None:
                unit, _ = norm_parts(r.mid[...])
                h_two[...] = (unit * r.vec[6:7] + r.vec[7:8]).astype(b16)
                r.out[...] = r.mid[...] + r.vec[8:9]
            else:
                r.out[...] = jnp.zeros_like(r.out)

        pre = dot_nt(h_two[...], up_rows(r)) + r.bias[0]
        cdf = 0.5 * (1.0 + lax.erf(pre * (0.5**0.5)))
        act = (pre * cdf).astype(b16)
        r.act[0] = act
        slope = cdf + pre * (jnp.exp(-0.5 * pre * pre) * (1.0 / math.sqrt(2.0 * math.pi)))
        r.slope[0] = slope.astype(b16)
        r.out[...] += dot_nn(act, rows_of(r.down0, r.down1))
        if before is not None:

            @pl.when(pl.program_id(0) == steps - 1)
            def _():
                r.need(r.so_far)
                r.out[...] += r.so_far[...]

    lazy = {}
    ins = ffn_specs(kind, arrays, base, hidden, lines, width)
    ins.update(
        bias=(
            bias.reshape(steps, 1, block),
            pl.BlockSpec((1, 1, block), lambda i, own: (i, 0, 0)),
        ),
    )
    outs = dict(
        out=((length, width), jnp.float32, None),
        act=((steps, length, block), b16, kept),
        slope=((steps, length, block), b16, kept),
    )
    if before is None:
        ins.update(mid=(mid, None), vec=(vec, None))
        outs.update(h_two=((length, width), b16, None))
    else:
        ins.update(h_in=(before.h_two, None))
        lazy.update(so_far=before.out)
    name = "ffn_fwd_one" if before is None else "ffn_fwd_two"
    return call(body, name, (steps,), ins, outs, {}, 5_000_000_000, 10_000_000, prefetch=own, lazy=lazy)


def ffn_backward(
    own, grad, mid, vec, kept, at, h_two, kind, arrays, lines, hidden, base, gh_in
):
    length, width = mid.shape
    block = 2 * lines * hidden
    b16, f32 = jnp.bfloat16, jnp.float32
    last = gh_in is not None
    wide = pl.BlockSpec((1, length, block), lambda i, own: (i + at, 0, 0))

    def body(r):
        @pl.when(pl.program_id(0) == 0)
        def _():
            r.gf[...] = r.g[...].astype(b16)
            r.gh[...] = jnp.zeros_like(r.gh)

        gf = r.gf[...]
        g_down = dot_tn(r.act[0], gf)
        g_act = dot_nt(gf, rows_of(r.down0, r.down1))
        g_pre = (g_act * r.slope[0].astype(f32)).astype(b16)
        g_up = dot_tn(g_pre, r.h_two[...])
        for n in range(2 * lines):
            rows = slice(n * hidden, (n + 1) * hidden)
            r.grads[0, n // lines, n % lines, 0] = g_up[rows].astype(b16)
            r.grads[0, n // lines, n % lines, 1] = g_down[rows].astype(b16)
        r.gbias[0] = jnp.sum(g_pre.astype(f32), axis=0, keepdims=True)
        r.gh[...] += dot_nn(g_pre, up_rows(r))
        if last:

            @pl.when(pl.program_id(0) == 1)
            def _():
                r.need(r.gh_in, r.mid)
                into, grad_gain, grad_shift = norm_grad(
                    r.gh[...] + r.gh_in[...], r.mid[...], r.vec[6:7]
                )
                r.gmid[...] = r.g[...] + into
                r.sums[...] = jnp.zeros_like(r.sums)
                r.sums[0:1] = grad_gain
                r.sums[1:2] = grad_shift
                r.sums[2:3] = jnp.sum(r.gf[...].astype(f32), axis=0, keepdims=True)

    ins = dict(
        g=(grad, None),
        h_two=(h_two, None),
        act=(kept.act, wide),
        slope=(kept.slope, wide),
        **ffn_specs(kind, arrays, base, hidden, lines, width),
    )
    outs = dict(
        grads=(
            (2, 2, lines, 2, hidden, width),
            b16,
            pl.BlockSpec((1, 2, lines, 2, hidden, width), lambda i, own: (i, 0, 0, 0, 0, 0)),
        ),
        gbias=((2, 1, block), f32, pl.BlockSpec((1, 1, block), lambda i, own: (i, 0, 0))),
    )
    scratch = dict(gf=((length, width), b16))
    lazy = {}
    if last:
        ins.update(vec=(vec, None))
        lazy.update(gh_in=gh_in, mid=mid)
        outs.update(gmid=((length, width), f32, None), sums=((8, width), f32, None))
        scratch.update(gh=((length, width), f32))
    else:
        outs.update(gh=((length, width), f32, None))
    name = "ffn_bwd_two" if last else "ffn_bwd_one"
    return call(
        body, name, (2,), ins, outs, scratch, 9_000_000_000, 15_000_000, prefetch=own, lazy=lazy
    )


def put_pieces(r, index, values):
    count, _, slots, _ = r.kept.shape
    for piece in range(2 * count):
        ref = r.kept if piece < count else r.sent
        ref[piece % count, index] = values[piece * slots : (piece + 1) * slots].astype(ref.dtype)
    r.flush(r.sent, index)
    r.flush(r.kept, index)


def attn_grad_open(r):
    b16 = jnp.bfloat16
    r.need(r.gmid, r.w3)
    r.ga[...] = r.gmid[...].astype(b16)
    gatt = dot_nt(r.ga[...], r.w3[...]).astype(b16)
    r.need(r.q, r.v)
    for start in range(gatt.shape[1] // 128):
        lanes = slice(128 * start, 128 * start + 128)
        r.gatt[start] = gatt[:, lanes]
        r.qs[start] = r.q[:, lanes]
        r.vs[start] = r.v[:, lanes]
    gatt_t = gatt.astype(jnp.float32).T
    r.gatt_t[...] = gatt_t.astype(b16)
    r.need(r.att_t)
    for head in range(HEADS):
        rows = slice(head * HEAD_DIM, (head + 1) * HEAD_DIM)
        r.inner[head] = jnp.sum(gatt_t[rows] * r.att_t[rows], axis=0, keepdims=True)
    r.need(r.kt)


def attn_grad_heads(r, group):
    gatt_block, q_block, v_block = r.gatt[group], r.qs[group], r.vs[group]
    gatt_t = r.gatt_t[pl.ds(pl.multiple_of(group * 128, 128), 128), :]
    dk = jnp.zeros(q_block.shape, jnp.float32)
    dv = jnp.zeros(q_block.shape, jnp.float32)
    for head in range(GROUP):
        probs = r.probs[head]
        gprobs = dot_nn(head_lanes(v_block, head), gatt_t)
        inner = r.inner[group * GROUP + head]
        gscores = (probs.astype(jnp.float32) * (gprobs - inner)).astype(jnp.bfloat16)
        dv += dot_nn(probs, head_lanes(gatt_block, head))
        dk += dot_nn(gscores, head_lanes(q_block, head))
        rows = pl.ds(pl.multiple_of(group * 128 + head * HEAD_DIM, HEAD_DIM), HEAD_DIM)
        r.dqt[rows, :] = dot_nn(r.kt[rows, :], gscores)
    r.dk[group] = dk
    r.dv[group] = dv


def attn_grad_close(r):
    b16, f32 = jnp.bfloat16, jnp.float32

    def joined(ref):
        return jnp.concatenate([ref[i] for i in range(ref.shape[0])], axis=1)

    def rounded(values):
        return values.astype(b16).astype(f32)

    r.need(r.att_rel, r.cos, r.sin, r.h_rel, r.w0, r.w1, r.w2, r.x)
    put_pieces(r, 3, dot_tn(r.att_rel[...], r.ga[...]))
    gq = rounded(r.dqt[...].T) * HEAD_DIM ** (-0.5)
    gproj = [
        turn(gq, r.cos, r.sin, -1.0).astype(b16),
        turn(rounded(joined(r.dk)), r.cos, r.sin, -1.0).astype(b16),
        joined(r.dv).astype(b16),
    ]
    r.sums[...] = jnp.zeros_like(r.sums)
    gh = jnp.zeros(r.gx.shape, f32)
    for j in range(3):
        put_pieces(r, j, dot_tn(r.h_rel[...], gproj[j]))
        r.sums[j : j + 1] = jnp.sum(gproj[j].astype(f32), axis=0, keepdims=True)
        gh += dot_nt(gproj[j], (r.w0, r.w1, r.w2)[j][...])
    into, grad_gain, grad_shift = norm_grad(gh, r.x[...], r.vec[4:5])
    r.gx[...] = r.gmid[...] + into
    r.sums[3:4] = jnp.sum(r.ga[...].astype(f32), axis=0, keepdims=True)
    r.sums[4:5] = grad_gain
    r.sums[5:6] = grad_shift


def attn_backward(slots, gmid, x, vec, cos, sin, saved):
    length, width = x.shape
    spots = saved.h_rel.shape[1]
    half = spots // slots // 2
    groups = width // 128
    b16, f32 = jnp.bfloat16, jnp.float32

    def body(r):
        step = pl.program_id(0)
        pl.when(step == 0)(lambda: attn_grad_open(r))
        attn_grad_heads(r, step)
        pl.when(step == groups - 1)(lambda: attn_grad_close(r))

    lazy = dict(
        gmid=gmid, w3=(saved.wabs, 3), q=saved.q, v=saved.v, att_t=saved.att_t, kt=saved.kt,
        att_rel=saved.att_rel, cos=cos, sin=sin, h_rel=saved.h_rel, w0=(saved.wabs, 0),
        w1=(saved.wabs, 1), w2=(saved.wabs, 2), x=x,
    )
    ins = dict(
        vec=(vec, None),
        probs=(saved.probs, pl.BlockSpec((GROUP, length, length), lambda i: (i, 0, 0))),
    )
    split = ((groups, length, 128), b16)
    sums = ((groups, length, 128), f32)
    return call(
        body, "attn_bwd", (groups,), ins,
        dict(
            gx=((length, width), f32, None),
            kept=((half, 4, slots, width), b16, EAGER),
            sent=((half, 4, slots, width), b16, EAGER),
            sums=((8, width), f32, None),
        ),
        dict(
            ga=((length, width), b16),
            gatt=split,
            qs=split,
            vs=split,
            gatt_t=((width, length), b16),
            inner=((HEADS, 1, length), f32),
            dqt=((width, length), f32),
            dk=sums,
            dv=sums,
        ),
        30_000_000_000, 30_000_000, lazy=lazy,
    )


def total_of(one, two):
    return one.astype(jnp.float32) + two.astype(jnp.float32)


def add_core(kept, came):
    _, _, lines, _, rows, width = kept.shape
    b16 = jnp.bfloat16
    both = pl.BlockSpec((2, 2, 1, 2, rows, width), lambda i: (0, 0, i, 0, 0, 0))
    one = ((2, lines, rows, width), b16, pl.BlockSpec((2, 1, rows, width), lambda i: (0, i, 0, 0)))

    def body(r):
        for n in range(2):
            r.ak[n, 0] = total_of(r.kept[0, n, 0, 0], r.came[0, n, 0, 0]).astype(b16)
            r.at[n, 0] = total_of(r.kept[1, n, 0, 0], r.came[1, n, 0, 0]).astype(b16)
            r.bk[n, 0] = total_of(r.kept[n, 0, 0, 1], r.came[n, 0, 0, 1]).astype(b16)
            r.bt[n, 0] = total_of(r.kept[n, 1, 0, 1], r.came[n, 1, 0, 1]).astype(b16)

    made = call(
        body, "add_core", (lines,), dict(kept=(kept, both), came=(came, both)),
        dict(ak=one, at=one, bk=one, bt=one), {}, 10_000_000, 10_000_000, limit=SMALL_LIMIT,
    )
    return (made.ak, made.at, made.bk, made.bt)


def add_first(ak, ac, bk, bc):
    _, lines, rows, width = ak.shape
    b16 = jnp.bfloat16
    steps = max(1, lines // 2)
    block = lines // steps
    both = pl.BlockSpec((2, block, rows, width), lambda i: (0, i, 0, 0))
    one = ((lines, rows, width), b16, pl.BlockSpec((block, rows, width), lambda i: (i, 0, 0)))

    def body(r):
        r.a0[...] = total_of(r.ak[0], r.ac[0]).astype(b16)
        r.a1[...] = total_of(r.ak[1], r.ac[1]).astype(b16)
        r.b0[...] = total_of(r.bk[0], r.bc[0]).astype(b16)
        r.b1[...] = total_of(r.bk[1], r.bc[1]).astype(b16)

    made = call(
        body, "add_first", (steps,),
        dict(ak=(ak, both), ac=(ac, both), bk=(bk, both), bc=(bc, both)),
        dict(a0=one, a1=one, b0=one, b1=one), {}, 10_000_000, 10_000_000, limit=SMALL_LIMIT,
    )
    return (made.a0, made.a1, made.b0, made.b1)


def add_second(own, ak, ac, bk, bc):
    lines, rows, width = ak.shape
    b16 = jnp.bfloat16
    half = lines // 2

    def place(i):
        order, unit, left = 0, 1, half
        while left:
            order += (i // left % 2) * unit
            unit, left = unit * 2, left // 2
        return order

    shape = (half, 2, rows, width)

    def body(r):
        for n in range(lines):
            line = place(n) ^ r.own[3]
            ref = r.kept if n < half else r.sent
            ref[n % half, 0] = total_of(r.ak[line], r.ac[line]).astype(b16)
            ref[n % half, 1] = total_of(r.bk[line], r.bc[line]).astype(b16)

    made = call(
        body, "add_second", (1,),
        dict(ak=(ak, None), ac=(ac, None), bk=(bk, None), bc=(bc, None)),
        dict(kept=(shape, b16, None), sent=(shape, b16, None)), {},
        10_000_000, 5_000_000, prefetch=own, limit=SMALL_LIMIT,
    )
    return (made.kept, made.sent)


def add_line(kept, came):
    half, _, rows, width = kept.shape
    shape = (half // 2, 2, rows, width)

    def body(r):
        total = total_of(r.kept[...], r.came[...])
        r.low[...] = total[: half // 2]
        r.high[...] = total[half // 2 :].astype(jnp.bfloat16)

    made = call(
        body, "add_line", (1,), dict(kept=(kept, None), came=(came, None)),
        dict(low=(shape, jnp.float32, None), high=(shape, jnp.bfloat16, None)), {},
        10_000_000, 2_000_000, limit=SMALL_LIMIT,
    )
    return (made.low, made.high)


def shards(
    sizes,
    tokens,
    qkv_weight,
    out_weight,
    proj_bias,
    norm_gain,
    norm_shift,
    up_weight,
    down_weight,
    up_bias,
    seq_order,
    seq_length,
    mlm_mask,
    cotangent,
):
    _, length, width = tokens.shape
    layer_count = qkv_weight.shape[0]
    _, ffn_size, core_size = sizes
    lines = ffn_size // 2
    count = 2 * ffn_size * core_size
    x_bit, y_bit, core_bit, line_unit = ffn_size * core_size, core_size, 1, 2 * core_size
    own_id = lax.axis_index(AXES)
    own_x = (own_id // x_bit) % 2
    own_y = (own_id // y_bit) % 2
    own_core = own_id % 2
    own_line = (own_id // line_unit) % lines
    own = jnp.stack([own_x, own_y, own_core, own_line]).astype(jnp.int32)
    rows = qkv_weight.shape[2]
    slots = pad_rows(rows)
    hidden = up_weight.shape[1]
    b16, f32 = jnp.bfloat16, jnp.float32

    def device(x, y, line, core):
        return (x * ffn_size + line * 2 + y) * core_size + core

    def swap(values, bits):
        return lax.ppermute(values, AXES, [(i, i ^ bits) for i in range(count)])

    def grow(values, bits, axis):
        return jnp.concatenate([values, swap(values, bits)], axis=axis)

    def line_swaps(values):
        return [swap(values, n * line_unit) for n in range(1, lines)]

    def line_join(values, came):
        joined = jnp.stack([values] + list(came))
        bit = lines // 2
        while bit:
            pairs = joined.reshape(lines // (2 * bit), 2, bit, *values.shape)
            joined = jnp.where((own_line & bit) > 0, jnp.flip(pairs, 1), pairs)
            joined = joined.reshape(lines, *values.shape)
            bit //= 2
        return joined

    def attn_lines(values, came):
        joined = line_join(values, came).transpose(1, 0, 2, 3)
        joined = joined.reshape(4, lines * slots, width)
        return (joined[:2], joined[2:])

    def hold(value, *others):
        return lax.optimization_barrier((value, *others))

    def along(values, came):
        return jnp.concatenate([values, came], axis=1)

    order_ids = jnp.arange(seq_length.shape[0], dtype=jnp.int32)
    slot_length = jnp.sum(jnp.where(seq_order[0] == order_ids, seq_length, 0))
    key_ok = jnp.arange(length, dtype=jnp.int32) < slot_length
    loss_weight = jnp.where(key_ok & (mlm_mask[0] > 0), 1.0, 0.0).astype(f32)
    local_count = jnp.sum(loss_weight)
    count_high = jnp.floor(local_count / 256.0)
    count_low = local_count - 256.0 * count_high
    small_len = 9 * rows + hidden
    layers = range(layer_count)
    small_row = jnp.concatenate(
        [
            part.reshape(-1)
            for layer in layers
            for part in (proj_bias[layer], norm_gain[layer], norm_shift[layer], up_bias[layer])
        ]
        + [count_high[None], count_low[None]]
    ).astype(b16)
    small_row = jnp.pad(small_row, (0, width - small_row.shape[0]))
    spare = jnp.zeros((4, slots - rows, width), b16)
    spare_at = jnp.arange(4 * (slots - rows)).reshape(4, slots - rows, 1) == 0
    spare = jnp.where(spare_at, small_row[None, None], spare)
    attn = jnp.concatenate([qkv_weight[0], out_weight[0][None]]).astype(b16)
    attn = jnp.concatenate([attn, spare], axis=1)
    attn, up_weight, down_weight, qkv_late, out_late = lax.optimization_barrier(
        (attn, up_weight, down_weight, qkv_weight[1], out_weight[1])
    )

    def ffn_piece(layer):
        return jnp.stack([up_weight[layer], down_weight[layer]]).astype(b16)

    def pair(values, came, bit):
        high = (own_line & bit) > 0
        return jnp.stack(
            [jnp.where(high, came, values), jnp.where(high, values, came)], axis=1
        ).reshape(-1, *values.shape[1:])

    part_a, part_b = attn_lines(attn, line_swaps(attn))
    ffn = after(ffn_piece(0), part_a)[None]
    bit = lines // 2
    came_a, came_b, came = (swap(part_a, y_bit), swap(part_b, x_bit), swap(ffn, bit * line_unit))
    came_a, came_b, came = hold(came_a, came_b, came)
    part_a, part_b = along(part_a, came_a), along(part_b, came_b)
    ffn = pair(ffn, came, bit)
    bit //= 2
    came_a, came_b, came = (swap(part_a, x_bit), swap(part_b, y_bit), swap(ffn, bit * line_unit))
    came_a, came_b, came = hold(came_a, came_b, came)
    part_a, part_b = along(part_a, came_a), along(part_b, came_b)
    ffn = pair(ffn, came, bit)
    while bit > 1:
        bit //= 2
        ffn = pair(ffn, swap(ffn, bit * line_unit), bit)
    half_a, half_b = (swap(part_a, core_bit), swap(part_b, core_bit))
    up_all = ffn[:, 0].reshape(lines * hidden, width)
    down_all = ffn[:, 1].reshape(lines * hidden, width)
    up_came, down_came = (swap(up_all, y_bit), swap(down_all, x_bit))

    next_attn = jnp.concatenate([qkv_late, out_late[None]]).astype(b16)
    next_attn = jnp.pad(next_attn, ((0, 0), (0, slots - rows), (0, 0)))
    next_attn = after(next_attn, ffn)
    next_came = line_swaps(next_attn)
    index = jnp.arange(count, dtype=jnp.int32)
    line_at = index % lines
    low_at = index // lines % 2
    high_at = index // (2 * lines) % 2
    core_at = (index // (4 * lines)) ^ own_core
    owners_a = device(high_at ^ own_x, low_at ^ own_y, line_at, core_at)
    owners_b = device(low_at ^ own_x, high_at ^ own_y, line_at, core_at)

    def spread_of(owners, size):
        slot_ids = jnp.arange(size, dtype=jnp.int32)
        source_row = jnp.where(
            slot_ids[None, :] < rows, owners[:, None] * rows + slot_ids[None, :], -1
        ).reshape(count * size)
        return (jnp.arange(width, dtype=jnp.int32)[:, None] == source_row[None, :]).astype(b16)

    spread_a, spread_b = spread_of(owners_a, slots), spread_of(owners_b, slots)
    hot = owners_a[:, None] == index[None, :]
    cos_half, sin_half = rope_tables(length, HEAD_DIM)
    cos = jnp.tile(jnp.concatenate([cos_half, cos_half], axis=1), (1, GROUP))
    sin = jnp.tile(jnp.concatenate([-sin_half, sin_half], axis=1), (1, GROUP))
    mask = jnp.where(key_ok, 0.0, mask_value).astype(f32)[:, None]

    small_own = jnp.concatenate(
        [part[0].reshape(-1, slots, width)[:, rows, :] for part in (part_a, half_a)]
    )
    small_all = dot_tn(hot.astype(b16), small_own)
    spot = layer_count * small_len
    masked_total = jnp.sum(small_all[:, spot] * 256.0 + small_all[:, spot + 1])
    factor = seq_length.shape[0] * length / jnp.maximum(masked_total, 1.0)

    vecs, biases = [], []
    for layer in layers:
        start = layer * small_len
        vec = small_all[:, start : start + 9 * rows]
        vec = vec.reshape(count, 9, rows).transpose(1, 0, 2).reshape(9, width)
        vec = jnp.concatenate([vec[:4], vec[5:6], vec[7:8], vec[6:7], vec[8:9], vec[4:5]])
        vecs.append(jnp.pad(vec, ((0, 7), (0, 0))))
        bias = small_own[:, start + 9 * rows : start + small_len]
        biases.append(bias.reshape(count * hidden).astype(f32))

    kinds = ("own", "own" if hidden % 16 else "late")
    groups = width // 128
    streams, attns, ffns = [tokens[0]], [], []

    late_start = None

    next_a = next_b = came_a = came_b = None

    def between(value):
        nonlocal up_all, down_all, up_came, down_came, next_came, late_start
        nonlocal next_a, next_b, came_a, came_b
        value, up_came, down_came, *next_came = hold(value, up_came, down_came, *next_came)
        late_start = value
        up_all = jnp.concatenate([up_all, up_came])
        down_all = jnp.concatenate([down_all, down_came])
        up_came, down_came = (swap(up_all, x_bit), swap(down_all, y_bit))
        next_a, next_b = attn_lines(next_attn, next_came)
        came_a, came_b = (swap(next_a, y_bit), swap(next_b, x_bit))
        return value

    attns.append(
        attn_forward(
            streams[0],
            dict(wa=part_a, wa2=half_a, wb=part_b, wb2=half_b),
            dict(sa=spread_a, sb=spread_b),
            vecs[0], cos, sin, mask, CUT, between,
        )
    )
    late = after(ffn_piece(1).reshape(2 * hidden, width), late_start)
    late = lax.all_gather(late, AXES, axis=0, tiled=False)
    late = late.reshape(2, lines, 2, 2, late.shape[1], width)
    late_weights = [(late,), (late,)]
    if kinds[1] == "own":
        turned = late[:, :, :, :, : 2 * hidden].reshape(2, lines, 2, 2, 2, hidden, width)
        for axis, odd in ((0, own_x), (2, own_y), (3, own_core)):
            turned = jnp.where(odd > 0, jnp.flip(turned, axis), turned)
        late_up = turned[:, :, :, :, 0].transpose(3, 0, 2, 1, 4, 5)
        late_down = turned[:, :, :, :, 1].transpose(3, 2, 0, 1, 4, 5)
        late_weights = [
            (late_up[n].reshape(-1, width), late_down[n].reshape(-1, width)) for n in range(2)
        ]

    attns[0].mid, up_came, down_came, came_a, came_b = hold(
        attns[0].mid, up_came, down_came, came_a, came_b
    )
    next_a, next_b = (along(next_a, came_a), along(next_b, came_b))
    up_all = jnp.concatenate([up_all, up_came])
    down_all = jnp.concatenate([down_all, down_came])
    up_came, down_came = (swap(up_all, core_bit), swap(down_all, core_bit))
    came_a, came_b = (swap(next_a, x_bit), swap(next_b, y_bit))
    weights = [[(up_all, down_all), (up_came, down_came)], late_weights]

    def ffn_front(layer, base, before):
        halves = 1 if kinds[layer] == "late" else 2
        bias = biases[layer].reshape(halves, -1)[base]
        return ffn_forward(
            own, attns[layer].mid, vecs[layer], kinds[layer], weights[layer][base], bias, lines,
            hidden, base, 4 // halves, before,
        )

    first = ffn_front(0, 0, None)
    first.out, came_a, came_b, up_came, down_came = hold(
        first.out, came_a, came_b, up_came, down_came
    )
    weights[0][1] = (up_came, down_came)
    next_a, next_b = (along(next_a, came_a), along(next_b, came_b))
    came_a, came_b = (swap(next_a, core_bit), swap(next_b, core_bit))
    ffns.append([first, ffn_front(0, 1, first)])
    stream, came_a, came_b = hold(ffns[0][1].out, came_a, came_b)
    streams.append(stream)
    attns.append(
        attn_forward(
            stream,
            dict(
                wa=next_a, wa2=came_a, wb=next_b, wb2=came_b,
            ),
            dict(sa=spread_a, sb=spread_b),
            vecs[1], cos, sin, mask, groups, None,
        )
    )
    ffns.append([ffn_front(1, 0, None)])
    if kinds[1] == "own":
        ffns[1].append(ffn_front(1, 1, ffns[1][0]))
    result = ffns[1][-1].out

    def ffn_back(layer, grad, base, gh_in):
        joint = len(ffns[layer]) == 1
        return ffn_backward(
            own, grad, attns[layer].mid, vecs[layer], ffns[layer][0 if joint else base],
            2 * base if joint else 0, ffns[layer][0].h_two, kinds[layer], weights[layer][base],
            lines, hidden, base, gh_in,
        )

    def attn_back(layer, grad_mid):
        return attn_backward(slots, grad_mid, streams[layer], vecs[layer], cos, sin, attns[layer])

    def core_step(kept, sent):
        return (kept, swap(sent, core_bit))

    def first_step(kept, came):
        ak, at, bk, bt = add_core(kept, came)
        return (ak, swap(at, x_bit), bk, swap(bt, y_bit))

    def second_step(*parts):
        a0, a1, b0, b1 = add_first(*parts)
        return (a0, swap(a1, y_bit), b0, swap(b1, x_bit))

    def third_step(*parts):
        kept, sent = add_second(own, *parts)
        return (kept, swap(sent, line_unit))

    def line_step(unit, kept, came):
        kept, sent = add_line(kept, came)
        return (kept, swap(sent, unit))

    def split_attn(values):
        return values.reshape(2, 2, lines, 2, 2 * slots, width)

    grad = cotangent[0] * (loss_weight[:, None] * factor)
    one1 = ffn_back(1, grad, 1, None)
    came = swap(one1.grads, core_bit)
    two1 = ffn_back(1, grad, 0, one1.gh)
    gmid, f1k, f1c = hold(two1.gmid, two1.grads, came)
    f1 = first_step(f1k, f1c)
    attn_g1 = attn_back(1, after(gmid, f1[0]))
    grad, kept, sent, sums, *f1 = hold(
        attn_g1.gx, attn_g1.kept, attn_g1.sent, attn_g1.sums, *f1
    )
    attn_g1.sums = sums
    a1k, a1c = core_step(split_attn(kept), split_attn(sent))
    f1 = second_step(*f1)
    a1k, a1c, *_ = hold(a1k, a1c, f1[0])
    a1 = first_step(a1k, a1c)
    one0 = ffn_back(0, after(grad, f1[0], a1[0]), 1, None)
    gh, sent, *parts = hold(one0.gh, one0.grads, *f1, *a1)
    f0 = swap(sent, core_bit)
    f1 = third_step(*parts[:4])
    a1 = second_step(*parts[4:])
    two0 = ffn_back(0, grad, 0, after(gh, f1[0], a1[0]))
    gmid, f0k, f0c, *parts = hold(two0.gmid, two0.grads, f0, *f1, *a1)
    f0 = first_step(f0k, f0c)
    unit = 2 * line_unit
    f1 = line_step(unit, *parts[:2])
    a1 = third_step(*parts[2:])
    attn_g0 = attn_back(0, after(gmid, f0[0], a1[0], f1[0]))
    kept, sent, sums, *parts = hold(attn_g0.kept, attn_g0.sent, attn_g0.sums, *f1, *a1, *f0)
    a0k, a0c = core_step(split_attn(kept), split_attn(sent))
    f1 = parts[:2]
    f0 = second_step(*parts[4:])
    a0k, a0c, *_ = hold(a0k, a0c, f0[0])
    a0 = first_step(a0k, a0c)
    attn_g0.sums, a1k, a1c, *f0 = hold(sums, *parts[2:4], *f0, a0[0])[:-1]
    a1 = line_step(unit, a1k, a1c)
    f0 = third_step(*f0)
    a0 = second_step(*a0)
    f0 = line_step(unit, *f0)
    a0 = third_step(*a0)
    a0 = line_step(unit, *a0)
    while unit * 2 < lines * line_unit:
        unit *= 2
        f1, a1, f0, a0 = [line_step(unit, *parts) for parts in (f1, a1, f0, a0)]
    ffn_grads = [(two0, one0), (two1, one1)]

    small = []
    for layer, attn_g in ((0, attn_g0), (1, attn_g1)):
        two, one = ffn_grads[layer]
        a, f = attn_g.sums, two.sums
        sums = jnp.concatenate([a[:4], f[2:3], a[4:5], f[0:1], a[5:6], f[1:2]])
        sums = sums.reshape(9, count, rows).transpose(1, 0, 2).reshape(count, 9 * rows)
        bias = jnp.concatenate([two.gbias, one.gbias]).reshape(count, hidden)
        bias = lax.dot_general(
            hot.astype(f32), bias, (((0,), (0,)), ((), ())), precision=lax.Precision.HIGHEST
        )
        small += [sums, bias]
    small = lax.all_to_all(jnp.concatenate(small, axis=1), AXES, 0, 0, tiled=True)
    small = jnp.sum(small, axis=0).reshape(layer_count, small_len)

    own_attn = jnp.stack([total_of(*a0), total_of(*a1)]).reshape(layer_count, 4, slots, width)
    own_ffn = jnp.stack([total_of(*f0), total_of(*f1)]).reshape(layer_count, 2, hidden, width)
    return (
        result[None],
        attn_g0.gx[None],
        own_attn[:, :3, :rows],
        own_attn[:, 3, :rows],
        small[:, : 5 * rows].reshape(layer_count, 5, rows),
        small[:, 5 * rows : 7 * rows].reshape(layer_count, 2, rows),
        small[:, 7 * rows : 9 * rows].reshape(layer_count, 2, rows),
        own_ffn[:, 0],
        own_ffn[:, 1],
        small[:, 9 * rows :],
    )


def solution(mesh):
    in_specs = (
        P(("batch", "ffn", "mp"), None, None),
        P(None, None, ("batch", "ffn", "mp"), None),
        P(None, ("batch", "ffn", "mp"), None),
        P(None, None, ("batch", "ffn", "mp")),
        P(None, None, ("batch", "ffn", "mp")),
        P(None, None, ("batch", "ffn", "mp")),
        P(None, ("batch", "ffn", "mp"), None),
        P(None, ("batch", "ffn", "mp"), None),
        P(None, ("batch", "ffn", "mp")),
        P(("batch", "ffn", "mp")),
        P(),
        P(("batch", "ffn", "mp"), None),
        P(("batch", "ffn", "mp"), None, None),
    )
    out_specs = (
        P(("batch", "ffn", "mp"), None, None),
        P(("batch", "ffn", "mp"), None, None),
        P(None, None, ("batch", "ffn", "mp"), None),
        P(None, ("batch", "ffn", "mp"), None),
        P(None, None, ("batch", "ffn", "mp")),
        P(None, None, ("batch", "ffn", "mp")),
        P(None, None, ("batch", "ffn", "mp")),
        P(None, ("batch", "ffn", "mp"), None),
        P(None, ("batch", "ffn", "mp"), None),
        P(None, ("batch", "ffn", "mp")),
    )
    sizes = tuple(mesh.shape[name] for name in AXES)
    return jax.shard_map(partial(shards, sizes), mesh=mesh, in_specs=in_specs, out_specs=out_specs, check_vma=False)
```

```python
from functools import partial
import math
from types import SimpleNamespace

import jax
import jax.numpy as jnp
from jax import lax
from jax.experimental import pallas as pl
from jax.experimental.pallas import tpu as pltpu
from jax.sharding import PartitionSpec as P

HEADS = 20
HEAD_DIM = 32


norm_eps = 1e-05
mask_value = -1e30


def rope_tables(length, head_width):
    half_width = head_width // 2
    freqs = jnp.exp(
        jnp.arange(half_width, dtype=jnp.float32) * (-2.0 * math.log(10000.0) / head_width)
    )
    angles = jnp.arange(length, dtype=jnp.float32)[:, None] * freqs[None, :]
    return (jnp.cos(angles), jnp.sin(angles))


AXES = ("batch", "ffn", "mp")
CUT = 1


def after(value, *others):
    return lax.optimization_barrier((value, *others))[0]


def pad_rows(rows):
    return -(-(rows + 1) // 8) * 8


GROUP = 128 // HEAD_DIM
VMEM_LIMIT = 56 * 1024 * 1024
SMALL_LIMIT = 24 * 1024 * 1024


def dot_nn(left, right):
    return lax.dot_general(
        left, right, (((1,), (0,)), ((), ())), preferred_element_type=jnp.float32
    )


def dot_nt(left, right):
    return lax.dot_general(
        left, right, (((1,), (1,)), ((), ())), preferred_element_type=jnp.float32
    )


def dot_tn(left, right):
    return lax.dot_general(
        left, right, (((0,), (0,)), ((), ())), preferred_element_type=jnp.float32
    )


def norm_parts(values):
    centred = values - jnp.mean(values, axis=-1, keepdims=True)
    variance = jnp.mean(centred * centred, axis=-1, keepdims=True)
    inverse = lax.rsqrt(variance + norm_eps)
    return (centred * inverse, inverse)


def norm_grad(grad, values, gain_row):
    unit, inverse = norm_parts(values)
    scaled = grad * gain_row
    mean_one = jnp.mean(scaled, axis=-1, keepdims=True)
    mean_two = jnp.mean(scaled * unit, axis=-1, keepdims=True)
    into = inverse * (scaled - mean_one - unit * mean_two)
    grad_gain = jnp.sum(grad * unit, axis=0, keepdims=True)
    grad_shift = jnp.sum(grad, axis=0, keepdims=True)
    return (into, grad_gain, grad_shift)


def turn(values, cos_ref, sin_ref, sign):
    half = HEAD_DIM // 2
    lanes = lax.broadcasted_iota(jnp.int32, (values.shape[0], 128), 1)
    low_half = lanes % HEAD_DIM < half
    parts = []
    for start in range(0, values.shape[1], 128):
        part = values[:, start : start + 128]
        partner = jnp.where(
            low_half, pltpu.roll(part, 128 - half, 1), pltpu.roll(part, half, 1)
        )
        parts.append(part * cos_ref[...] + sign * (partner * sin_ref[...]))
    return jnp.concatenate(parts, axis=1)


def head_lanes(block, head):
    lanes = lax.broadcasted_iota(jnp.int32, block.shape, 1)
    return jnp.where(lanes // HEAD_DIM == head, block, jnp.zeros_like(block))


def sds(shape, dtype):
    return jax.ShapeDtypeStruct(shape, dtype)


def whole(shape):
    return pl.BlockSpec(shape, lambda *_: (0,) * len(shape))


EAGER = object()


def call(
    body, name, grid, ins, outs, scratch, flops, moved, prefetch=None, aliases=None, limit=None,
    lazy=None,
):
    lazy = {n: a if isinstance(a, tuple) else (a, None) for n, a in (lazy or {}).items()}
    eager = {n: (shape, dtype) for n, (shape, dtype, spec) in outs.items() if spec is EAGER}
    names = list(ins) + list(lazy) + list(outs) + list(scratch) + list(lazy) + list(eager)
    lead = 0 if prefetch is None else 1

    def picked(array, index):
        return array.shape if index is None else array.shape[1:]

    def kernel(*refs):
        named = dict(zip(names, refs[lead:]))
        if lead:
            named.update(own=refs[0])
        if lazy:
            sources = refs[lead + len(ins) : lead + len(ins) + len(lazy)]
            copies = {}
            for n, (name, (_, index)) in enumerate(lazy.items()):
                source = sources[n] if index is None else sources[n].at[index]
                copies[name] = pltpu.make_async_copy(source, named[name], refs[-1].at[n])

            @pl.when(pl.program_id(0) == 0)
            def _():
                for copy in copies.values():
                    copy.start()

            def need(*wanted):
                for name in lazy:
                    if any(named[name] is ref for ref in wanted):
                        copies[name].wait()

            named.update(need=need)
        flushed = []
        if eager:
            out_at = lead + len(ins) + len(lazy)
            targets = dict(zip(outs, refs[out_at : out_at + len(outs)]))
            sems = refs[-2] if lazy else refs[-1]

            def copy_out(name, index, n):
                source, target = named[name], targets[name]
                if index is not None:
                    source, target = source.at[:, index], target.at[:, index]
                return pltpu.make_async_copy(source, target, sems.at[n])

            def flush(ref, index=None):
                for name in eager:
                    if named[name] is ref:
                        flushed.append((name, index, len(flushed)))
                        copy_out(*flushed[-1]).start()

            named.update(flush=flush)
        body(SimpleNamespace(**named))
        if eager:

            @pl.when(pl.program_id(0) == grid[0] - 1)
            def _():
                for entry in flushed:
                    copy_out(*entry).wait()

    raw = pl.BlockSpec(memory_space=pl.ANY)
    in_specs = [spec or whole(array.shape) for array, spec in ins.values()] + [raw] * len(lazy)
    out_specs = [
        raw if spec is EAGER else spec or whole(shape) for shape, _, spec in outs.values()
    ]
    out_shape = [sds(shape, dtype) for shape, dtype, _ in outs.values()]
    scratch_shapes = [pltpu.VMEM(shape, dtype) for shape, dtype in scratch.values()]
    scratch_shapes += [pltpu.VMEM(picked(a, index), a.dtype) for a, index in lazy.values()]
    scratch_shapes += [pltpu.VMEM(shape, dtype) for shape, dtype in eager.values()]
    if eager:
        scratch_shapes.append(pltpu.SemaphoreType.DMA((16,)))
    if lazy:
        scratch_shapes.append(pltpu.SemaphoreType.DMA((len(lazy),)))
    operands = ([] if prefetch is None else [prefetch]) + [array for array, _ in ins.values()]
    operands += [array for array, _ in lazy.values()]
    in_names, out_names = list(ins), list(outs)
    pairs = {
        in_names.index(a) + lead: out_names.index(b) for a, b in (aliases or {}).items()
    }
    results = pl.pallas_call(
        kernel,
        grid_spec=pltpu.PrefetchScalarGridSpec(
            num_scalar_prefetch=lead,
            grid=grid,
            in_specs=in_specs,
            out_specs=out_specs,
            scratch_shapes=scratch_shapes,
        ),
        out_shape=out_shape,
        input_output_aliases=pairs,
        compiler_params=pltpu.CompilerParams(vmem_limit_bytes=limit or VMEM_LIMIT),
        cost_estimate=pl.CostEstimate(flops=flops, bytes_accessed=moved, transcendentals=0),
        name=name,
    )(*operands)
    return SimpleNamespace(**dict(zip(out_names, results)))


def attn_open(r, shared):
    r.need(r.x)
    unit, _ = norm_parts(r.x[...])
    h_one = (unit * r.vec[4:5] + r.vec[5:6]).astype(jnp.bfloat16)
    r.need(r.sa)
    r.h_rel[...] = dot_nn(h_one, r.sa[...]).astype(jnp.bfloat16)
    r.flush(r.h_rel)

    def place(j, spread, own, came):
        half = own.shape[1]
        placed = dot_nn(spread[:, :half], own[j % 2])
        placed += dot_nn(spread[:, half:], came[j % 2])
        r.wabs[j] = placed.astype(jnp.bfloat16)

    r.need(r.wa, r.wa2)
    place(0, r.sa, r.wa, r.wa2)
    place(1, r.sa, r.wa, r.wa2)
    r.need(r.cos, r.sin)
    query = dot_nn(h_one, r.wabs[0]) + r.vec[0:1]
    query = turn(query, r.cos, r.sin, 1.0) * HEAD_DIM ** (-0.5)
    r.q[...] = query.astype(jnp.bfloat16)
    r.flush(r.q)
    r.qt[...] = query.T.astype(jnp.bfloat16)
    key = turn(dot_nn(h_one, r.wabs[1]) + r.vec[1:2], r.cos, r.sin, 1.0)
    key_bf = key.astype(jnp.bfloat16)
    for start in range(key.shape[1] // 128):
        r.k[start] = key_bf[:, 128 * start : 128 * start + 128]
    r.kt[...] = key.T.astype(jnp.bfloat16)
    r.flush(r.kt)
    r.need(r.sb, r.wb, r.wb2)
    place(2, r.sb, r.wb, r.wb2)
    place(3, r.sb, r.wb, r.wb2)
    r.flush(r.wabs)
    value = dot_nn(h_one, r.wabs[2]) + r.vec[2:3]
    r.v[...] = value.astype(jnp.bfloat16)
    r.flush(r.v)
    r.vt[...] = value.T.astype(jnp.bfloat16)
    if shared:
        for ref in (r.qt, r.k, r.vt):
            r.flush(ref)


def attn_heads(r, group):
    key_block = r.k[group]
    query_t = r.qt[pl.ds(pl.multiple_of(group * 128, 128), 128), :]
    for head in range(GROUP):
        scores = dot_nn(head_lanes(key_block, head), query_t) + r.mask[...]
        top = jnp.max(scores, axis=0, keepdims=True)
        shifted = jnp.exp(scores - top)
        total = jnp.sum(shifted, axis=0, keepdims=True)
        probs = (shifted * (1.0 / total)).astype(jnp.bfloat16)
        r.probs[head] = probs
        rows = pl.ds(pl.multiple_of(group * 128 + head * HEAD_DIM, HEAD_DIM), HEAD_DIM)
        r.att_t[rows, :] = dot_nn(r.vt[rows, :], probs)


def attn_close(r, wo):
    att = r.att_t[...].T.astype(jnp.bfloat16)
    r.att_rel[...] = dot_nn(att, r.sa[...]).astype(jnp.bfloat16)
    r.mid[...] = r.x[...] + (dot_nn(att, wo) + r.vec[3:4])


def attn_forward(x, parts, spreads, vec, cos, sin, mask, cut, between):
    length, width = x.shape
    spots = spreads["sa"].shape[1]
    groups = width // 128
    b16, f32 = jnp.bfloat16, jnp.float32
    opening = dict(
        x=x, sa=spreads["sa"], wa=parts["wa"], wa2=parts["wa2"], cos=cos, sin=sin,
        sb=spreads["sb"], wb=parts["wb"], wb2=parts["wb2"],
    )
    tables = dict(vec=vec, mask=mask)
    made = dict(
        wabs=((4, width, width), b16, EAGER),
        h_rel=((length, spots), b16, EAGER),
        q=((length, width), b16, EAGER),
        kt=((width, length), b16, EAGER),
        v=((length, width), b16, EAGER),
    )
    work = dict(
        qt=((width, length), b16),
        k=((groups, length, 128), b16),
        vt=((width, length), b16),
    )
    att_t = dict(att_t=((width, length), f32, None))
    closing = dict(att_rel=((length, spots), b16, None), mid=((length, width), f32, None))

    def probs_out(base):
        spec = pl.BlockSpec((GROUP, length, length), lambda i: (i + base, 0, 0))
        return dict(probs=((HEADS, length, length), b16, spec))

    def plain(arrays):
        return {
            name: array if isinstance(array, tuple) else (array, None)
            for name, array in arrays.items()
        }

    def body(first, last, base, steps):
        def run(r):
            step = pl.program_id(0)
            if first:
                pl.when(step == 0)(lambda: attn_open(r, not last))

            attn_heads(r, step + base)
            if last:

                @pl.when(step == steps - 1)
                def _():
                    if not first:
                        r.need(r.att_in, r.sa, r.wo, r.x)
                        r.att_t[: base * 128, :] = r.att_in[: base * 128, :]
                    attn_close(r, r.wabs[3] if first else r.wo[...])

        return run

    if cut == groups:
        return call(
            body(True, True, 0, groups), "attn_fwd", (groups,),
            plain(tables), {**made, **att_t, **closing, **probs_out(0)}, work,
            20_000_000_000, 25_000_000, lazy=opening,
        )
    shared = {name: (shape, dtype, EAGER) for name, (shape, dtype) in work.items()}
    one = call(
        body(True, False, 0, cut), "attn_fwd_one", (cut,),
        plain(tables), {**made, **att_t, **shared, **probs_out(0)}, {},
        10_000_000_000, 15_000_000, lazy=opening,
    )
    att_in = between(one.att_t)
    ins = plain(
        dict(
            vec=vec, mask=mask, k=one.k, qt=one.qt, vt=one.vt,
        )
    )
    ins.update(probs_in=(one.probs, pl.BlockSpec(memory_space=pl.ANY)))
    two = call(
        body(False, True, cut, groups - cut), "attn_fwd_two", (groups - cut,),
        ins, {**att_t, **closing, **probs_out(cut)}, {},
        10_000_000_000, 15_000_000, aliases=dict(probs_in="probs"),
        lazy=dict(att_in=att_in, sa=spreads["sa"], wo=(one.wabs, 3), x=x),
    )
    return SimpleNamespace(**{**vars(one), **vars(two)})


def ffn_specs(kind, arrays, base, hidden, lines, width):
    specs = {}
    rows = lines * hidden
    if kind == "own":
        specs.update(up0=(arrays[0], pl.BlockSpec((2 * rows, width), lambda i, own: (i, 0))))
        for y in range(2):
            spec = pl.BlockSpec((rows, width), lambda i, own, y=y: (2 * y + i, 0))
            specs["down" + str(y)] = (arrays[1], spec)
        return specs
    shape = (1, lines, 1, 1, hidden, width)
    for which, name in enumerate(("up", "down")):
        for y in range(2):

            def index(i, own, y=y, which=which):
                core = base + i // 2
                return ((i % 2) ^ own[0], 0, y ^ own[1], core ^ own[2], which, 0)

            specs[name + str(y)] = (arrays[0], pl.BlockSpec(shape, index))
    return specs


def rows_of(*refs):
    parts = []
    for ref in refs:
        values = ref[...]
        parts.append(values.reshape(-1, values.shape[-1]))
    return jnp.concatenate(parts) if len(parts) > 1 else parts[0]


def up_rows(r):
    return rows_of(r.up0, r.up1) if hasattr(r, "up1") else rows_of(r.up0)


def ffn_forward(own, mid, vec, kind, arrays, bias, lines, hidden, base, steps, before):
    length, width = mid.shape
    block = 2 * lines * hidden
    b16 = jnp.bfloat16
    kept = pl.BlockSpec((1, length, block), lambda i, own: (i, 0, 0))

    def body(r):
        h_two = r.h_two if before is None else r.h_in

        @pl.when(pl.program_id(0) == 0)
        def _():
            if before is None:
                unit, _ = norm_parts(r.mid[...])
                h_two[...] = (unit * r.vec[6:7] + r.vec[7:8]).astype(b16)
                r.out[...] = r.mid[...] + r.vec[8:9]
            else:
                r.out[...] = jnp.zeros_like(r.out)

        pre = dot_nt(h_two[...], up_rows(r)) + r.bias[0]
        cdf = 0.5 * (1.0 + lax.erf(pre * (0.5**0.5)))
        act = (pre * cdf).astype(b16)
        r.act[0] = act
        slope = cdf + pre * (jnp.exp(-0.5 * pre * pre) * (1.0 / math.sqrt(2.0 * math.pi)))
        r.slope[0] = slope.astype(b16)
        r.out[...] += dot_nn(act, rows_of(r.down0, r.down1))
        if before is not None:

            @pl.when(pl.program_id(0) == steps - 1)
            def _():
                r.need(r.so_far)
                r.out[...] += r.so_far[...]

    lazy = {}
    ins = ffn_specs(kind, arrays, base, hidden, lines, width)
    ins.update(
        bias=(
            bias.reshape(steps, 1, block),
            pl.BlockSpec((1, 1, block), lambda i, own: (i, 0, 0)),
        ),
    )
    outs = dict(
        out=((length, width), jnp.float32, None),
        act=((steps, length, block), b16, kept),
        slope=((steps, length, block), b16, kept),
    )
    if before is None:
        ins.update(mid=(mid, None), vec=(vec, None))
        outs.update(h_two=((length, width), b16, None))
    else:
        ins.update(h_in=(before.h_two, None))
        lazy.update(so_far=before.out)
    name = "ffn_fwd_one" if before is None else "ffn_fwd_two"
    return call(body, name, (steps,), ins, outs, {}, 5_000_000_000, 10_000_000, prefetch=own, lazy=lazy)


def ffn_backward(
    own, grad, mid, vec, kept, at, h_two, kind, arrays, lines, hidden, base, gh_in
):
    length, width = mid.shape
    block = 2 * lines * hidden
    b16, f32 = jnp.bfloat16, jnp.float32
    last = gh_in is not None
    wide = pl.BlockSpec((1, length, block), lambda i, own: (i + at, 0, 0))

    def body(r):
        @pl.when(pl.program_id(0) == 0)
        def _():
            r.gf[...] = r.g[...].astype(b16)
            r.gh[...] = jnp.zeros_like(r.gh)

        gf = r.gf[...]
        g_down = dot_tn(r.act[0], gf)
        g_act = dot_nt(gf, rows_of(r.down0, r.down1))
        g_pre = (g_act * r.slope[0].astype(f32)).astype(b16)
        g_up = dot_tn(g_pre, r.h_two[...])
        for n in range(2 * lines):
            rows = slice(n * hidden, (n + 1) * hidden)
            r.grads[0, n // lines, n % lines, 0] = g_up[rows].astype(b16)
            r.grads[0, n // lines, n % lines, 1] = g_down[rows].astype(b16)
        r.gbias[0] = jnp.sum(g_pre.astype(f32), axis=0, keepdims=True)
        r.gh[...] += dot_nn(g_pre, up_rows(r))
        if last:

            @pl.when(pl.program_id(0) == 1)
            def _():
                r.need(r.gh_in, r.mid)
                into, grad_gain, grad_shift = norm_grad(
                    r.gh[...] + r.gh_in[...], r.mid[...], r.vec[6:7]
                )
                r.gmid[...] = r.g[...] + into
                r.sums[...] = jnp.zeros_like(r.sums)
                r.sums[0:1] = grad_gain
                r.sums[1:2] = grad_shift
                r.sums[2:3] = jnp.sum(r.gf[...].astype(f32), axis=0, keepdims=True)

    ins = dict(
        g=(grad, None),
        h_two=(h_two, None),
        act=(kept.act, wide),
        slope=(kept.slope, wide),
        **ffn_specs(kind, arrays, base, hidden, lines, width),
    )
    outs = dict(
        grads=(
            (2, 2, lines, 2, hidden, width),
            b16,
            pl.BlockSpec((1, 2, lines, 2, hidden, width), lambda i, own: (i, 0, 0, 0, 0, 0)),
        ),
        gbias=((2, 1, block), f32, pl.BlockSpec((1, 1, block), lambda i, own: (i, 0, 0))),
    )
    scratch = dict(gf=((length, width), b16))
    lazy = {}
    if last:
        ins.update(vec=(vec, None))
        lazy.update(gh_in=gh_in, mid=mid)
        outs.update(gmid=((length, width), f32, None), sums=((8, width), f32, None))
        scratch.update(gh=((length, width), f32))
    else:
        outs.update(gh=((length, width), f32, None))
    name = "ffn_bwd_two" if last else "ffn_bwd_one"
    return call(
        body, name, (2,), ins, outs, scratch, 9_000_000_000, 15_000_000, prefetch=own, lazy=lazy
    )


def put_pieces(r, index, values):
    count, _, slots, _ = r.kept.shape
    for piece in range(2 * count):
        ref = r.kept if piece < count else r.sent
        ref[piece % count, index] = values[piece * slots : (piece + 1) * slots].astype(ref.dtype)
    r.flush(r.sent, index)
    r.flush(r.kept, index)


def attn_grad_open(r):
    b16 = jnp.bfloat16
    r.need(r.gmid, r.w3)
    r.ga[...] = r.gmid[...].astype(b16)
    gatt = dot_nt(r.ga[...], r.w3[...]).astype(b16)
    r.need(r.q, r.v)
    for start in range(gatt.shape[1] // 128):
        lanes = slice(128 * start, 128 * start + 128)
        r.gatt[start] = gatt[:, lanes]
        r.qs[start] = r.q[:, lanes]
        r.vs[start] = r.v[:, lanes]
    gatt_t = gatt.astype(jnp.float32).T
    r.gatt_t[...] = gatt_t.astype(b16)
    r.need(r.att_t)
    for head in range(HEADS):
        rows = slice(head * HEAD_DIM, (head + 1) * HEAD_DIM)
        r.inner[head] = jnp.sum(gatt_t[rows] * r.att_t[rows], axis=0, keepdims=True)
    r.need(r.kt)


def attn_grad_heads(r, group):
    gatt_block, q_block, v_block = r.gatt[group], r.qs[group], r.vs[group]
    gatt_t = r.gatt_t[pl.ds(pl.multiple_of(group * 128, 128), 128), :]
    dk = jnp.zeros(q_block.shape, jnp.float32)
    dv = jnp.zeros(q_block.shape, jnp.float32)
    for head in range(GROUP):
        probs = r.probs[head]
        gprobs = dot_nn(head_lanes(v_block, head), gatt_t)
        inner = r.inner[group * GROUP + head]
        gscores = (probs.astype(jnp.float32) * (gprobs - inner)).astype(jnp.bfloat16)
        dv += dot_nn(probs, head_lanes(gatt_block, head))
        dk += dot_nn(gscores, head_lanes(q_block, head))
        rows = pl.ds(pl.multiple_of(group * 128 + head * HEAD_DIM, HEAD_DIM), HEAD_DIM)
        r.dqt[rows, :] = dot_nn(r.kt[rows, :], gscores)
    r.dk[group] = dk
    r.dv[group] = dv


def attn_grad_close(r):
    b16, f32 = jnp.bfloat16, jnp.float32

    def joined(ref):
        return jnp.concatenate([ref[i] for i in range(ref.shape[0])], axis=1)

    def rounded(values):
        return values.astype(b16).astype(f32)

    r.need(r.att_rel, r.cos, r.sin, r.h_rel, r.w0, r.w1, r.w2, r.x)
    put_pieces(r, 3, dot_tn(r.att_rel[...], r.ga[...]))
    gq = rounded(r.dqt[...].T) * HEAD_DIM ** (-0.5)
    gproj = [
        turn(gq, r.cos, r.sin, -1.0).astype(b16),
        turn(rounded(joined(r.dk)), r.cos, r.sin, -1.0).astype(b16),
        joined(r.dv).astype(b16),
    ]
    r.sums[...] = jnp.zeros_like(r.sums)
    gh = jnp.zeros(r.gx.shape, f32)
    for j in range(3):
        put_pieces(r, j, dot_tn(r.h_rel[...], gproj[j]))
        r.sums[j : j + 1] = jnp.sum(gproj[j].astype(f32), axis=0, keepdims=True)
        gh += dot_nt(gproj[j], (r.w0, r.w1, r.w2)[j][...])
    into, grad_gain, grad_shift = norm_grad(gh, r.x[...], r.vec[4:5])
    r.gx[...] = r.gmid[...] + into
    r.sums[3:4] = jnp.sum(r.ga[...].astype(f32), axis=0, keepdims=True)
    r.sums[4:5] = grad_gain
    r.sums[5:6] = grad_shift


def attn_backward(slots, gmid, x, vec, cos, sin, saved):
    length, width = x.shape
    spots = saved.h_rel.shape[1]
    half = spots // slots // 2
    groups = width // 128
    b16, f32 = jnp.bfloat16, jnp.float32

    def body(r):
        step = pl.program_id(0)
        pl.when(step == 0)(lambda: attn_grad_open(r))
        attn_grad_heads(r, step)
        pl.when(step == groups - 1)(lambda: attn_grad_close(r))

    lazy = dict(
        gmid=gmid, w3=(saved.wabs, 3), q=saved.q, v=saved.v, att_t=saved.att_t, kt=saved.kt,
        att_rel=saved.att_rel, cos=cos, sin=sin, h_rel=saved.h_rel, w0=(saved.wabs, 0),
        w1=(saved.wabs, 1), w2=(saved.wabs, 2), x=x,
    )
    ins = dict(
        vec=(vec, None),
        probs=(saved.probs, pl.BlockSpec((GROUP, length, length), lambda i: (i, 0, 0))),
    )
    split = ((groups, length, 128), b16)
    sums = ((groups, length, 128), f32)
    return call(
        body, "attn_bwd", (groups,), ins,
        dict(
            gx=((length, width), f32, None),
            kept=((half, 4, slots, width), b16, EAGER),
            sent=((half, 4, slots, width), b16, EAGER),
            sums=((8, width), f32, None),
        ),
        dict(
            ga=((length, width), b16),
            gatt=split,
            qs=split,
            vs=split,
            gatt_t=((width, length), b16),
            inner=((HEADS, 1, length), f32),
            dqt=((width, length), f32),
            dk=sums,
            dv=sums,
        ),
        30_000_000_000, 30_000_000, lazy=lazy,
    )


def total_of(one, two):
    return one.astype(jnp.float32) + two.astype(jnp.float32)


def add_core(kept, came):
    _, _, lines, _, rows, width = kept.shape
    b16 = jnp.bfloat16
    both = pl.BlockSpec((2, 2, 1, 2, rows, width), lambda i: (0, 0, i, 0, 0, 0))
    one = ((2, lines, rows, width), b16, pl.BlockSpec((2, 1, rows, width), lambda i: (0, i, 0, 0)))

    def body(r):
        for n in range(2):
            r.ak[n, 0] = total_of(r.kept[0, n, 0, 0], r.came[0, n, 0, 0]).astype(b16)
            r.at[n, 0] = total_of(r.kept[1, n, 0, 0], r.came[1, n, 0, 0]).astype(b16)
            r.bk[n, 0] = total_of(r.kept[n, 0, 0, 1], r.came[n, 0, 0, 1]).astype(b16)
            r.bt[n, 0] = total_of(r.kept[n, 1, 0, 1], r.came[n, 1, 0, 1]).astype(b16)

    made = call(
        body, "add_core", (lines,), dict(kept=(kept, both), came=(came, both)),
        dict(ak=one, at=one, bk=one, bt=one), {}, 10_000_000, 10_000_000, limit=SMALL_LIMIT,
    )
    return (made.ak, made.at, made.bk, made.bt)


def add_first(ak, ac, bk, bc):
    _, lines, rows, width = ak.shape
    b16 = jnp.bfloat16
    steps = max(1, lines // 2)
    block = lines // steps
    both = pl.BlockSpec((2, block, rows, width), lambda i: (0, i, 0, 0))
    one = ((lines, rows, width), b16, pl.BlockSpec((block, rows, width), lambda i: (i, 0, 0)))

    def body(r):
        r.a0[...] = total_of(r.ak[0], r.ac[0]).astype(b16)
        r.a1[...] = total_of(r.ak[1], r.ac[1]).astype(b16)
        r.b0[...] = total_of(r.bk[0], r.bc[0]).astype(b16)
        r.b1[...] = total_of(r.bk[1], r.bc[1]).astype(b16)

    made = call(
        body, "add_first", (steps,),
        dict(ak=(ak, both), ac=(ac, both), bk=(bk, both), bc=(bc, both)),
        dict(a0=one, a1=one, b0=one, b1=one), {}, 10_000_000, 10_000_000, limit=SMALL_LIMIT,
    )
    return (made.a0, made.a1, made.b0, made.b1)


def add_second(own, ak, ac, bk, bc):
    lines, rows, width = ak.shape
    b16 = jnp.bfloat16
    half = lines // 2

    def place(i):
        order, unit, left = 0, 1, half
        while left:
            order += (i // left % 2) * unit
            unit, left = unit * 2, left // 2
        return order

    shape = (half, 2, rows, width)

    def body(r):
        for n in range(lines):
            line = place(n) ^ r.own[3]
            ref = r.kept if n < half else r.sent
            ref[n % half, 0] = total_of(r.ak[line], r.ac[line]).astype(b16)
            ref[n % half, 1] = total_of(r.bk[line], r.bc[line]).astype(b16)

    made = call(
        body, "add_second", (1,),
        dict(ak=(ak, None), ac=(ac, None), bk=(bk, None), bc=(bc, None)),
        dict(kept=(shape, b16, None), sent=(shape, b16, None)), {},
        10_000_000, 5_000_000, prefetch=own, limit=SMALL_LIMIT,
    )
    return (made.kept, made.sent)


def add_line(kept, came):
    half, _, rows, width = kept.shape
    shape = (half // 2, 2, rows, width)

    def body(r):
        total = total_of(r.kept[...], r.came[...])
        r.low[...] = total[: half // 2]
        r.high[...] = total[half // 2 :].astype(jnp.bfloat16)

    made = call(
        body, "add_line", (1,), dict(kept=(kept, None), came=(came, None)),
        dict(low=(shape, jnp.float32, None), high=(shape, jnp.bfloat16, None)), {},
        10_000_000, 2_000_000, limit=SMALL_LIMIT,
    )
    return (made.low, made.high)


def shards(
    sizes,
    tokens,
    qkv_weight,
    out_weight,
    proj_bias,
    norm_gain,
    norm_shift,
    up_weight,
    down_weight,
    up_bias,
    seq_order,
    seq_length,
    mlm_mask,
    cotangent,
):
    _, length, width = tokens.shape
    layer_count = qkv_weight.shape[0]
    _, ffn_size, core_size = sizes
    lines = ffn_size // 2
    count = 2 * ffn_size * core_size
    x_bit, y_bit, core_bit, line_unit = ffn_size * core_size, core_size, 1, 2 * core_size
    own_id = lax.axis_index(AXES)
    own_x = (own_id // x_bit) % 2
    own_y = (own_id // y_bit) % 2
    own_core = own_id % 2
    own_line = (own_id // line_unit) % lines
    own = jnp.stack([own_x, own_y, own_core, own_line]).astype(jnp.int32)
    rows = qkv_weight.shape[2]
    slots = pad_rows(rows)
    hidden = up_weight.shape[1]
    b16, f32 = jnp.bfloat16, jnp.float32

    def device(x, y, line, core):
        return (x * ffn_size + line * 2 + y) * core_size + core

    def swap(values, bits):
        return lax.ppermute(values, AXES, [(i, i ^ bits) for i in range(count)])

    def grow(values, bits, axis):
        return jnp.concatenate([values, swap(values, bits)], axis=axis)

    def line_swaps(values):
        return [swap(values, n * line_unit) for n in range(1, lines)]

    def line_join(values, came):
        joined = jnp.stack([values] + list(came))
        bit = lines // 2
        while bit:
            pairs = joined.reshape(lines // (2 * bit), 2, bit, *values.shape)
            joined = jnp.where((own_line & bit) > 0, jnp.flip(pairs, 1), pairs)
            joined = joined.reshape(lines, *values.shape)
            bit //= 2
        return joined

    def attn_lines(values, came):
        joined = line_join(values, came).transpose(1, 0, 2, 3)
        joined = joined.reshape(4, lines * slots, width)
        return (joined[:2], joined[2:])

    def hold(value, *others):
        return lax.optimization_barrier((value, *others))

    def along(values, came):
        return jnp.concatenate([values, came], axis=1)

    order_ids = jnp.arange(seq_length.shape[0], dtype=jnp.int32)
    slot_length = jnp.sum(jnp.where(seq_order[0] == order_ids, seq_length, 0))
    key_ok = jnp.arange(length, dtype=jnp.int32) < slot_length
    loss_weight = jnp.where(key_ok & (mlm_mask[0] > 0), 1.0, 0.0).astype(f32)
    local_count = jnp.sum(loss_weight)
    count_high = jnp.floor(local_count / 256.0)
    count_low = local_count - 256.0 * count_high
    small_len = 9 * rows + hidden
    layers = range(layer_count)
    small_row = jnp.concatenate(
        [
            part.reshape(-1)
            for layer in layers
            for part in (proj_bias[layer], norm_gain[layer], norm_shift[layer], up_bias[layer])
        ]
        + [count_high[None], count_low[None]]
    ).astype(b16)
    small_row = jnp.pad(small_row, (0, width - small_row.shape[0]))
    spare = jnp.zeros((4, slots - rows, width), b16)
    spare_at = jnp.arange(4 * (slots - rows)).reshape(4, slots - rows, 1) == 0
    spare = jnp.where(spare_at, small_row[None, None], spare)
    attn = jnp.concatenate([qkv_weight[0], out_weight[0][None]]).astype(b16)
    attn = jnp.concatenate([attn, spare], axis=1)
    attn, up_weight, down_weight, qkv_late, out_late = lax.optimization_barrier(
        (attn, up_weight, down_weight, qkv_weight[1], out_weight[1])
    )

    def ffn_piece(layer):
        return jnp.stack([up_weight[layer], down_weight[layer]]).astype(b16)

    def pair(values, came, bit):
        high = (own_line & bit) > 0
        return jnp.stack(
            [jnp.where(high, came, values), jnp.where(high, values, came)], axis=1
        ).reshape(-1, *values.shape[1:])

    part_a, part_b = attn_lines(attn, line_swaps(attn))
    ffn = after(ffn_piece(0), part_a)[None]
    bit = lines // 2
    came_a, came_b, came = (swap(part_a, y_bit), swap(part_b, x_bit), swap(ffn, bit * line_unit))
    came_a, came_b, came = hold(came_a, came_b, came)
    part_a, part_b = along(part_a, came_a), along(part_b, came_b)
    ffn = pair(ffn, came, bit)
    bit //= 2
    came_a, came_b, came = (swap(part_a, x_bit), swap(part_b, y_bit), swap(ffn, bit * line_unit))
    came_a, came_b, came = hold(came_a, came_b, came)
    part_a, part_b = along(part_a, came_a), along(part_b, came_b)
    ffn = pair(ffn, came, bit)
    while bit > 1:
        bit //= 2
        ffn = pair(ffn, swap(ffn, bit * line_unit), bit)
    half_a, half_b = (swap(part_a, core_bit), swap(part_b, core_bit))
    up_all = ffn[:, 0].reshape(lines * hidden, width)
    down_all = ffn[:, 1].reshape(lines * hidden, width)
    up_came, down_came = (swap(up_all, y_bit), swap(down_all, x_bit))

    next_attn = jnp.concatenate([qkv_late, out_late[None]]).astype(b16)
    next_attn = jnp.pad(next_attn, ((0, 0), (0, slots - rows), (0, 0)))
    next_attn = after(next_attn, ffn)
    next_came = line_swaps(next_attn)
    index = jnp.arange(count, dtype=jnp.int32)
    line_at = index % lines
    low_at = index // lines % 2
    high_at = index // (2 * lines) % 2
    core_at = (index // (4 * lines)) ^ own_core
    owners_a = device(high_at ^ own_x, low_at ^ own_y, line_at, core_at)
    owners_b = device(low_at ^ own_x, high_at ^ own_y, line_at, core_at)

    def spread_of(owners, size):
        slot_ids = jnp.arange(size, dtype=jnp.int32)
        source_row = jnp.where(
            slot_ids[None, :] < rows, owners[:, None] * rows + slot_ids[None, :], -1
        ).reshape(count * size)
        return (jnp.arange(width, dtype=jnp.int32)[:, None] == source_row[None, :]).astype(b16)

    spread_a, spread_b = spread_of(owners_a, slots), spread_of(owners_b, slots)
    hot = owners_a[:, None] == index[None, :]
    cos_half, sin_half = rope_tables(length, HEAD_DIM)
    cos = jnp.tile(jnp.concatenate([cos_half, cos_half], axis=1), (1, GROUP))
    sin = jnp.tile(jnp.concatenate([-sin_half, sin_half], axis=1), (1, GROUP))
    mask = jnp.where(key_ok, 0.0, mask_value).astype(f32)[:, None]

    small_own = jnp.concatenate(
        [part[0].reshape(-1, slots, width)[:, rows, :] for part in (part_a, half_a)]
    )
    small_all = dot_tn(hot.astype(b16), small_own)
    spot = layer_count * small_len
    masked_total = jnp.sum(small_all[:, spot] * 256.0 + small_all[:, spot + 1])
    factor = seq_length.shape[0] * length / jnp.maximum(masked_total, 1.0)

    vecs, biases = [], []
    for layer in layers:
        start = layer * small_len
        vec = small_all[:, start : start + 9 * rows]
        vec = vec.reshape(count, 9, rows).transpose(1, 0, 2).reshape(9, width)
        vec = jnp.concatenate([vec[:4], vec[5:6], vec[7:8], vec[6:7], vec[8:9], vec[4:5]])
        vecs.append(jnp.pad(vec, ((0, 7), (0, 0))))
        bias = small_own[:, start + 9 * rows : start + small_len]
        biases.append(bias.reshape(count * hidden).astype(f32))

    kinds = ("own", "own" if hidden % 16 else "late")
    groups = width // 128
    streams, attns, ffns = [tokens[0]], [], []

    late_start = None

    next_a = next_b = came_a = came_b = None

    def between(value):
        nonlocal up_all, down_all, up_came, down_came, next_came, late_start
        nonlocal next_a, next_b, came_a, came_b
        value, up_came, down_came, *next_came = hold(value, up_came, down_came, *next_came)
        late_start = value
        up_all = jnp.concatenate([up_all, up_came])
        down_all = jnp.concatenate([down_all, down_came])
        up_came, down_came = (swap(up_all, x_bit), swap(down_all, y_bit))
        next_a, next_b = attn_lines(next_attn, next_came)
        came_a, came_b = (swap(next_a, y_bit), swap(next_b, x_bit))
        return value

    attns.append(
        attn_forward(
            streams[0],
            dict(wa=part_a, wa2=half_a, wb=part_b, wb2=half_b),
            dict(sa=spread_a, sb=spread_b),
            vecs[0], cos, sin, mask, CUT, between,
        )
    )
    late = after(ffn_piece(1).reshape(2 * hidden, width), late_start)
    late = lax.all_gather(late, AXES, axis=0, tiled=False)
    late = late.reshape(2, lines, 2, 2, late.shape[1], width)
    late_weights = [(late,), (late,)]
    if kinds[1] == "own":
        turned = late[:, :, :, :, : 2 * hidden].reshape(2, lines, 2, 2, 2, hidden, width)
        for axis, odd in ((0, own_x), (2, own_y), (3, own_core)):
            turned = jnp.where(odd > 0, jnp.flip(turned, axis), turned)
        late_up = turned[:, :, :, :, 0].transpose(3, 0, 2, 1, 4, 5)
        late_down = turned[:, :, :, :, 1].transpose(3, 2, 0, 1, 4, 5)
        late_weights = [
            (late_up[n].reshape(-1, width), late_down[n].reshape(-1, width)) for n in range(2)
        ]

    attns[0].mid, up_came, down_came, came_a, came_b = hold(
        attns[0].mid, up_came, down_came, came_a, came_b
    )
    next_a, next_b = (along(next_a, came_a), along(next_b, came_b))
    up_all = jnp.concatenate([up_all, up_came])
    down_all = jnp.concatenate([down_all, down_came])
    up_came, down_came = (swap(up_all, core_bit), swap(down_all, core_bit))
    came_a, came_b = (swap(next_a, x_bit), swap(next_b, y_bit))
    weights = [[(up_all, down_all), (up_came, down_came)], late_weights]

    def ffn_front(layer, base, before):
        halves = 1 if kinds[layer] == "late" else 2
        bias = biases[layer].reshape(halves, -1)[base]
        return ffn_forward(
            own, attns[layer].mid, vecs[layer], kinds[layer], weights[layer][base], bias, lines,
            hidden, base, 4 // halves, before,
        )

    first = ffn_front(0, 0, None)
    first.out, came_a, came_b, up_came, down_came = hold(
        first.out, came_a, came_b, up_came, down_came
    )
    weights[0][1] = (up_came, down_came)
    next_a, next_b = (along(next_a, came_a), along(next_b, came_b))
    came_a, came_b = (swap(next_a, core_bit), swap(next_b, core_bit))
    ffns.append([first, ffn_front(0, 1, first)])
    stream, came_a, came_b = hold(ffns[0][1].out, came_a, came_b)
    streams.append(stream)
    attns.append(
        attn_forward(
            stream,
            dict(
                wa=next_a, wa2=came_a, wb=next_b, wb2=came_b,
            ),
            dict(sa=spread_a, sb=spread_b),
            vecs[1], cos, sin, mask, groups, None,
        )
    )
    ffns.append([ffn_front(1, 0, None)])
    if kinds[1] == "own":
        ffns[1].append(ffn_front(1, 1, ffns[1][0]))
    result = ffns[1][-1].out

    def ffn_back(layer, grad, base, gh_in):
        joint = len(ffns[layer]) == 1
        return ffn_backward(
            own, grad, attns[layer].mid, vecs[layer], ffns[layer][0 if joint else base],
            2 * base if joint else 0, ffns[layer][0].h_two, kinds[layer], weights[layer][base],
            lines, hidden, base, gh_in,
        )

    def attn_back(layer, grad_mid):
        return attn_backward(slots, grad_mid, streams[layer], vecs[layer], cos, sin, attns[layer])

    def core_step(kept, sent):
        return (kept, swap(sent, core_bit))

    def first_step(kept, came):
        ak, at, bk, bt = add_core(kept, came)
        return (ak, swap(at, x_bit), bk, swap(bt, y_bit))

    def second_step(*parts):
        a0, a1, b0, b1 = add_first(*parts)
        return (a0, swap(a1, y_bit), b0, swap(b1, x_bit))

    def third_step(*parts):
        kept, sent = add_second(own, *parts)
        return (kept, swap(sent, line_unit))

    def line_step(unit, kept, came):
        kept, sent = add_line(kept, came)
        return (kept, swap(sent, unit))

    def split_attn(values):
        return values.reshape(2, 2, lines, 2, 2 * slots, width)

    grad = cotangent[0] * (loss_weight[:, None] * factor)
    one1 = ffn_back(1, grad, 1, None)
    came = swap(one1.grads, core_bit)
    two1 = ffn_back(1, grad, 0, one1.gh)
    gmid, f1k, f1c = hold(two1.gmid, two1.grads, came)
    f1 = first_step(f1k, f1c)
    attn_g1 = attn_back(1, after(gmid, f1[0]))
    grad, kept, sent, sums, *f1 = hold(
        attn_g1.gx, attn_g1.kept, attn_g1.sent, attn_g1.sums, *f1
    )
    attn_g1.sums = sums
    a1k, a1c = core_step(split_attn(kept), split_attn(sent))
    f1 = second_step(*f1)
    a1k, a1c, *_ = hold(a1k, a1c, f1[0])
    a1 = first_step(a1k, a1c)
    one0 = ffn_back(0, after(grad, f1[0], a1[0]), 1, None)
    gh, sent, *parts = hold(one0.gh, one0.grads, *f1, *a1)
    f0 = swap(sent, core_bit)
    f1 = third_step(*parts[:4])
    a1 = second_step(*parts[4:])
    two0 = ffn_back(0, grad, 0, after(gh, f1[0], a1[0]))
    gmid, f0k, f0c, *parts = hold(two0.gmid, two0.grads, f0, *f1, *a1)
    f0 = first_step(f0k, f0c)
    unit = 2 * line_unit
    f1 = line_step(unit, *parts[:2])
    a1 = third_step(*parts[2:])
    attn_g0 = attn_back(0, after(gmid, f0[0], a1[0], f1[0]))
    kept, sent, sums, *parts = hold(attn_g0.kept, attn_g0.sent, attn_g0.sums, *f1, *a1, *f0)
    a0k, a0c = core_step(split_attn(kept), split_attn(sent))
    f1 = parts[:2]
    f0 = second_step(*parts[4:])
    a0k, a0c, *_ = hold(a0k, a0c, f0[0])
    a0 = first_step(a0k, a0c)
    attn_g0.sums, a1k, a1c, *f0 = hold(sums, *parts[2:4], *f0, a0[0])[:-1]
    a1 = line_step(unit, a1k, a1c)
    f0 = third_step(*f0)
    a0 = second_step(*a0)
    f0 = line_step(unit, *f0)
    a0 = third_step(*a0)
    a0 = line_step(unit, *a0)
    while unit * 2 < lines * line_unit:
        unit *= 2
        f1, a1, f0, a0 = [line_step(unit, *parts) for parts in (f1, a1, f0, a0)]
    ffn_grads = [(two0, one0), (two1, one1)]

    small = []
    for layer, attn_g in ((0, attn_g0), (1, attn_g1)):
        two, one = ffn_grads[layer]
        a, f = attn_g.sums, two.sums
        sums = jnp.concatenate([a[:4], f[2:3], a[4:5], f[0:1], a[5:6], f[1:2]])
        sums = sums.reshape(9, count, rows).transpose(1, 0, 2).reshape(count, 9 * rows)
        bias = jnp.concatenate([two.gbias, one.gbias]).reshape(count, hidden)
        bias = lax.dot_general(
            hot.astype(f32), bias, (((0,), (0,)), ((), ())), precision=lax.Precision.HIGHEST
        )
        small += [sums, bias]
    small = lax.all_to_all(jnp.concatenate(small, axis=1), AXES, 0, 0, tiled=True)
    small = jnp.sum(small, axis=0).reshape(layer_count, small_len)

    own_attn = jnp.stack([total_of(*a0), total_of(*a1)]).reshape(layer_count, 4, slots, width)
    own_ffn = jnp.stack([total_of(*f0), total_of(*f1)]).reshape(layer_count, 2, hidden, width)
    return (
        result[None],
        attn_g0.gx[None],
        own_attn[:, :3, :rows],
        own_attn[:, 3, :rows],
        small[:, : 5 * rows].reshape(layer_count, 5, rows),
        small[:, 5 * rows : 7 * rows].reshape(layer_count, 2, rows),
        small[:, 7 * rows : 9 * rows].reshape(layer_count, 2, rows),
        own_ffn[:, 0],
        own_ffn[:, 1],
        small[:, 9 * rows :],
    )


def solution(mesh):
    in_specs = (
        P(("batch", "ffn", "mp"), None, None),
        P(None, None, ("batch", "ffn", "mp"), None),
        P(None, ("batch", "ffn", "mp"), None),
        P(None, None, ("batch", "ffn", "mp")),
        P(None, None, ("batch", "ffn", "mp")),
        P(None, None, ("batch", "ffn", "mp")),
        P(None, ("batch", "ffn", "mp"), None),
        P(None, ("batch", "ffn", "mp"), None),
        P(None, ("batch", "ffn", "mp")),
        P(("batch", "ffn", "mp")),
        P(),
        P(("batch", "ffn", "mp"), None),
        P(("batch", "ffn", "mp"), None, None),
    )
    out_specs = (
        P(("batch", "ffn", "mp"), None, None),
        P(("batch", "ffn", "mp"), None, None),
        P(None, None, ("batch", "ffn", "mp"), None),
        P(None, ("batch", "ffn", "mp"), None),
        P(None, None, ("batch", "ffn", "mp")),
        P(None, None, ("batch", "ffn", "mp")),
        P(None, None, ("batch", "ffn", "mp")),
        P(None, ("batch", "ffn", "mp"), None),
        P(None, ("batch", "ffn", "mp"), None),
        P(None, ("batch", "ffn", "mp")),
    )
    sizes = tuple(mesh.shape[name] for name in AXES)
    return jax.shard_map(partial(shards, sizes), mesh=mesh, in_specs=in_specs, out_specs=out_specs, check_vma=False)
```

```python
from functools import partial
import math
from types import SimpleNamespace

import jax
import jax.numpy as jnp
from jax import lax
from jax.experimental import pallas as pl
from jax.experimental.pallas import tpu as pltpu
from jax.sharding import PartitionSpec as P

HEADS = 20
HEAD_DIM = 32


norm_eps = 1e-05
mask_value = -1e30


def rope_tables(length, head_width):
    half_width = head_width // 2
    freqs = jnp.exp(
        jnp.arange(half_width, dtype=jnp.float32) * (-2.0 * math.log(10000.0) / head_width)
    )
    angles = jnp.arange(length, dtype=jnp.float32)[:, None] * freqs[None, :]
    return (jnp.cos(angles), jnp.sin(angles))


AXES = ("batch", "ffn", "mp")
CUT = 2


def after(value, *others):
    return lax.optimization_barrier((value, *others))[0]


def pad_rows(rows):
    return -(-(rows + 1) // 8) * 8


GROUP = 128 // HEAD_DIM
VMEM_LIMIT = 56 * 1024 * 1024
SMALL_LIMIT = 24 * 1024 * 1024


def dot_nn(left, right):
    return lax.dot_general(
        left, right, (((1,), (0,)), ((), ())), preferred_element_type=jnp.float32
    )


def dot_nt(left, right):
    return lax.dot_general(
        left, right, (((1,), (1,)), ((), ())), preferred_element_type=jnp.float32
    )


def dot_tn(left, right):
    return lax.dot_general(
        left, right, (((0,), (0,)), ((), ())), preferred_element_type=jnp.float32
    )


def norm_parts(values):
    centred = values - jnp.mean(values, axis=-1, keepdims=True)
    variance = jnp.mean(centred * centred, axis=-1, keepdims=True)
    inverse = lax.rsqrt(variance + norm_eps)
    return (centred * inverse, inverse)


def norm_grad(grad, values, gain_row):
    unit, inverse = norm_parts(values)
    scaled = grad * gain_row
    mean_one = jnp.mean(scaled, axis=-1, keepdims=True)
    mean_two = jnp.mean(scaled * unit, axis=-1, keepdims=True)
    into = inverse * (scaled - mean_one - unit * mean_two)
    grad_gain = jnp.sum(grad * unit, axis=0, keepdims=True)
    grad_shift = jnp.sum(grad, axis=0, keepdims=True)
    return (into, grad_gain, grad_shift)


def turn(values, cos_ref, sin_ref, sign):
    half = HEAD_DIM // 2
    lanes = lax.broadcasted_iota(jnp.int32, (values.shape[0], 128), 1)
    low_half = lanes % HEAD_DIM < half
    parts = []
    for start in range(0, values.shape[1], 128):
        part = values[:, start : start + 128]
        partner = jnp.where(
            low_half, pltpu.roll(part, 128 - half, 1), pltpu.roll(part, half, 1)
        )
        parts.append(part * cos_ref[...] + sign * (partner * sin_ref[...]))
    return jnp.concatenate(parts, axis=1)


def head_lanes(block, head):
    lanes = lax.broadcasted_iota(jnp.int32, block.shape, 1)
    return jnp.where(lanes // HEAD_DIM == head, block, jnp.zeros_like(block))


def sds(shape, dtype):
    return jax.ShapeDtypeStruct(shape, dtype)


def whole(shape):
    return pl.BlockSpec(shape, lambda *_: (0,) * len(shape))


EAGER = object()


def call(
    body, name, grid, ins, outs, scratch, flops, moved, prefetch=None, aliases=None, limit=None,
    lazy=None,
):
    lazy = {n: a if isinstance(a, tuple) else (a, None) for n, a in (lazy or {}).items()}
    eager = {n: (shape, dtype) for n, (shape, dtype, spec) in outs.items() if spec is EAGER}
    names = list(ins) + list(lazy) + list(outs) + list(scratch) + list(lazy) + list(eager)
    lead = 0 if prefetch is None else 1

    def picked(array, index):
        return array.shape if index is None else array.shape[1:]

    def kernel(*refs):
        named = dict(zip(names, refs[lead:]))
        if lead:
            named.update(own=refs[0])
        if lazy:
            sources = refs[lead + len(ins) : lead + len(ins) + len(lazy)]
            copies = {}
            for n, (name, (_, index)) in enumerate(lazy.items()):
                source = sources[n] if index is None else sources[n].at[index]
                copies[name] = pltpu.make_async_copy(source, named[name], refs[-1].at[n])

            @pl.when(pl.program_id(0) == 0)
            def _():
                for copy in copies.values():
                    copy.start()

            def need(*wanted):
                for name in lazy:
                    if any(named[name] is ref for ref in wanted):
                        copies[name].wait()

            named.update(need=need)
        flushed = []
        if eager:
            out_at = lead + len(ins) + len(lazy)
            targets = dict(zip(outs, refs[out_at : out_at + len(outs)]))
            sems = refs[-2] if lazy else refs[-1]

            def copy_out(name, index, n):
                source, target = named[name], targets[name]
                if index is not None:
                    source, target = source.at[:, index], target.at[:, index]
                return pltpu.make_async_copy(source, target, sems.at[n])

            def flush(ref, index=None):
                for name in eager:
                    if named[name] is ref:
                        flushed.append((name, index, len(flushed)))
                        copy_out(*flushed[-1]).start()

            named.update(flush=flush)
        body(SimpleNamespace(**named))
        if eager:

            @pl.when(pl.program_id(0) == grid[0] - 1)
            def _():
                for entry in flushed:
                    copy_out(*entry).wait()

    raw = pl.BlockSpec(memory_space=pl.ANY)
    in_specs = [spec or whole(array.shape) for array, spec in ins.values()] + [raw] * len(lazy)
    out_specs = [
        raw if spec is EAGER else spec or whole(shape) for shape, _, spec in outs.values()
    ]
    out_shape = [sds(shape, dtype) for shape, dtype, _ in outs.values()]
    scratch_shapes = [pltpu.VMEM(shape, dtype) for shape, dtype in scratch.values()]
    scratch_shapes += [pltpu.VMEM(picked(a, index), a.dtype) for a, index in lazy.values()]
    scratch_shapes += [pltpu.VMEM(shape, dtype) for shape, dtype in eager.values()]
    if eager:
        scratch_shapes.append(pltpu.SemaphoreType.DMA((16,)))
    if lazy:
        scratch_shapes.append(pltpu.SemaphoreType.DMA((len(lazy),)))
    operands = ([] if prefetch is None else [prefetch]) + [array for array, _ in ins.values()]
    operands += [array for array, _ in lazy.values()]
    in_names, out_names = list(ins), list(outs)
    pairs = {
        in_names.index(a) + lead: out_names.index(b) for a, b in (aliases or {}).items()
    }
    results = pl.pallas_call(
        kernel,
        grid_spec=pltpu.PrefetchScalarGridSpec(
            num_scalar_prefetch=lead,
            grid=grid,
            in_specs=in_specs,
            out_specs=out_specs,
            scratch_shapes=scratch_shapes,
        ),
        out_shape=out_shape,
        input_output_aliases=pairs,
        compiler_params=pltpu.CompilerParams(vmem_limit_bytes=limit or VMEM_LIMIT),
        cost_estimate=pl.CostEstimate(flops=flops, bytes_accessed=moved, transcendentals=0),
        name=name,
    )(*operands)
    return SimpleNamespace(**dict(zip(out_names, results)))


def attn_open(r, shared):
    r.need(r.x)
    unit, _ = norm_parts(r.x[...])
    h_one = (unit * r.vec[4:5] + r.vec[5:6]).astype(jnp.bfloat16)
    r.need(r.sa)
    r.h_rel[...] = dot_nn(h_one, r.sa[...]).astype(jnp.bfloat16)
    r.flush(r.h_rel)

    def place(j, spread, own, came):
        half = own.shape[1]
        placed = dot_nn(spread[:, :half], own[j % 2])
        placed += dot_nn(spread[:, half:], came[j % 2])
        r.wabs[j] = placed.astype(jnp.bfloat16)

    r.need(r.wa, r.wa2)
    place(0, r.sa, r.wa, r.wa2)
    place(1, r.sa, r.wa, r.wa2)
    r.need(r.cos, r.sin)
    query = dot_nn(h_one, r.wabs[0]) + r.vec[0:1]
    query = turn(query, r.cos, r.sin, 1.0) * HEAD_DIM ** (-0.5)
    r.q[...] = query.astype(jnp.bfloat16)
    r.flush(r.q)
    r.qt[...] = query.T.astype(jnp.bfloat16)
    key = turn(dot_nn(h_one, r.wabs[1]) + r.vec[1:2], r.cos, r.sin, 1.0)
    key_bf = key.astype(jnp.bfloat16)
    for start in range(key.shape[1] // 128):
        r.k[start] = key_bf[:, 128 * start : 128 * start + 128]
    r.kt[...] = key.T.astype(jnp.bfloat16)
    r.flush(r.kt)
    r.need(r.sb, r.wb, r.wb2)
    place(2, r.sb, r.wb, r.wb2)
    place(3, r.sb, r.wb, r.wb2)
    r.flush(r.wabs)
    value = dot_nn(h_one, r.wabs[2]) + r.vec[2:3]
    r.v[...] = value.astype(jnp.bfloat16)
    r.flush(r.v)
    r.vt[...] = value.T.astype(jnp.bfloat16)
    if shared:
        for ref in (r.qt, r.k, r.vt):
            r.flush(ref)


def attn_heads(r, group):
    key_block = r.k[group]
    query_t = r.qt[pl.ds(pl.multiple_of(group * 128, 128), 128), :]
    for head in range(GROUP):
        scores = dot_nn(head_lanes(key_block, head), query_t) + r.mask[...]
        top = jnp.max(scores, axis=0, keepdims=True)
        shifted = jnp.exp(scores - top)
        total = jnp.sum(shifted, axis=0, keepdims=True)
        probs = (shifted * (1.0 / total)).astype(jnp.bfloat16)
        r.probs[head] = probs
        rows = pl.ds(pl.multiple_of(group * 128 + head * HEAD_DIM, HEAD_DIM), HEAD_DIM)
        r.att_t[rows, :] = dot_nn(r.vt[rows, :], probs)


def attn_close(r, wo):
    att = r.att_t[...].T.astype(jnp.bfloat16)
    r.att_rel[...] = dot_nn(att, r.sa[...]).astype(jnp.bfloat16)
    r.mid[...] = r.x[...] + (dot_nn(att, wo) + r.vec[3:4])


def attn_forward(x, parts, spreads, vec, cos, sin, mask, cut, between):
    length, width = x.shape
    spots = spreads["sa"].shape[1]
    groups = width // 128
    b16, f32 = jnp.bfloat16, jnp.float32
    opening = dict(
        x=x, sa=spreads["sa"], wa=parts["wa"], wa2=parts["wa2"], cos=cos, sin=sin,
        sb=spreads["sb"], wb=parts["wb"], wb2=parts["wb2"],
    )
    tables = dict(vec=vec, mask=mask)
    made = dict(
        wabs=((4, width, width), b16, EAGER),
        h_rel=((length, spots), b16, EAGER),
        q=((length, width), b16, EAGER),
        kt=((width, length), b16, EAGER),
        v=((length, width), b16, EAGER),
    )
    work = dict(
        qt=((width, length), b16),
        k=((groups, length, 128), b16),
        vt=((width, length), b16),
    )
    att_t = dict(att_t=((width, length), f32, None))
    closing = dict(att_rel=((length, spots), b16, None), mid=((length, width), f32, None))

    def probs_out(base):
        spec = pl.BlockSpec((GROUP, length, length), lambda i: (i + base, 0, 0))
        return dict(probs=((HEADS, length, length), b16, spec))

    def plain(arrays):
        return {
            name: array if isinstance(array, tuple) else (array, None)
            for name, array in arrays.items()
        }

    def body(first, last, base, steps):
        def run(r):
            step = pl.program_id(0)
            if first:
                pl.when(step == 0)(lambda: attn_open(r, not last))

            attn_heads(r, step + base)
            if last:

                @pl.when(step == steps - 1)
                def _():
                    if not first:
                        r.need(r.att_in, r.sa, r.wo, r.x)
                        r.att_t[: base * 128, :] = r.att_in[: base * 128, :]
                    attn_close(r, r.wabs[3] if first else r.wo[...])

        return run

    if cut == groups:
        return call(
            body(True, True, 0, groups), "attn_fwd", (groups,),
            plain(tables), {**made, **att_t, **closing, **probs_out(0)}, work,
            20_000_000_000, 25_000_000, lazy=opening,
        )
    shared = {name: (shape, dtype, EAGER) for name, (shape, dtype) in work.items()}
    one = call(
        body(True, False, 0, cut), "attn_fwd_one", (cut,),
        plain(tables), {**made, **att_t, **shared, **probs_out(0)}, {},
        10_000_000_000, 15_000_000, lazy=opening,
    )
    att_in = between(one.att_t)
    ins = plain(
        dict(
            vec=vec, mask=mask, k=one.k, qt=one.qt, vt=one.vt,
        )
    )
    ins.update(probs_in=(one.probs, pl.BlockSpec(memory_space=pl.ANY)))
    two = call(
        body(False, True, cut, groups - cut), "attn_fwd_two", (groups - cut,),
        ins, {**att_t, **closing, **probs_out(cut)}, {},
        10_000_000_000, 15_000_000, aliases=dict(probs_in="probs"),
        lazy=dict(att_in=att_in, sa=spreads["sa"], wo=(one.wabs, 3), x=x),
    )
    return SimpleNamespace(**{**vars(one), **vars(two)})


def ffn_specs(kind, arrays, base, hidden, lines, width):
    specs = {}
    rows = lines * hidden
    if kind == "own":
        specs.update(up0=(arrays[0], pl.BlockSpec((2 * rows, width), lambda i, own: (i, 0))))
        for y in range(2):
            spec = pl.BlockSpec((rows, width), lambda i, own, y=y: (2 * y + i, 0))
            specs["down" + str(y)] = (arrays[1], spec)
        return specs
    shape = (1, lines, 1, 1, hidden, width)
    for which, name in enumerate(("up", "down")):
        for y in range(2):

            def index(i, own, y=y, which=which):
                core = base + i // 2
                return ((i % 2) ^ own[0], 0, y ^ own[1], core ^ own[2], which, 0)

            specs[name + str(y)] = (arrays[0], pl.BlockSpec(shape, index))
    return specs


def rows_of(*refs):
    parts = []
    for ref in refs:
        values = ref[...]
        parts.append(values.reshape(-1, values.shape[-1]))
    return jnp.concatenate(parts) if len(parts) > 1 else parts[0]


def up_rows(r):
    return rows_of(r.up0, r.up1) if hasattr(r, "up1") else rows_of(r.up0)


def ffn_forward(own, mid, vec, kind, arrays, bias, lines, hidden, base, steps, before):
    length, width = mid.shape
    block = 2 * lines * hidden
    b16 = jnp.bfloat16
    kept = pl.BlockSpec((1, length, block), lambda i, own: (i, 0, 0))

    def body(r):
        h_two = r.h_two if before is None else r.h_in

        @pl.when(pl.program_id(0) == 0)
        def _():
            if before is None:
                unit, _ = norm_parts(r.mid[...])
                h_two[...] = (unit * r.vec[6:7] + r.vec[7:8]).astype(b16)
                r.out[...] = r.mid[...] + r.vec[8:9]
            else:
                r.out[...] = jnp.zeros_like(r.out)

        pre = dot_nt(h_two[...], up_rows(r)) + r.bias[0]
        cdf = 0.5 * (1.0 + lax.erf(pre * (0.5**0.5)))
        act = (pre * cdf).astype(b16)
        r.act[0] = act
        slope = cdf + pre * (jnp.exp(-0.5 * pre * pre) * (1.0 / math.sqrt(2.0 * math.pi)))
        r.slope[0] = slope.astype(b16)
        r.out[...] += dot_nn(act, rows_of(r.down0, r.down1))
        if before is not None:

            @pl.when(pl.program_id(0) == steps - 1)
            def _():
                r.need(r.so_far)
                r.out[...] += r.so_far[...]

    lazy = {}
    ins = ffn_specs(kind, arrays, base, hidden, lines, width)
    ins.update(
        bias=(
            bias.reshape(steps, 1, block),
            pl.BlockSpec((1, 1, block), lambda i, own: (i, 0, 0)),
        ),
    )
    outs = dict(
        out=((length, width), jnp.float32, None),
        act=((steps, length, block), b16, kept),
        slope=((steps, length, block), b16, kept),
    )
    if before is None:
        ins.update(mid=(mid, None), vec=(vec, None))
        outs.update(h_two=((length, width), b16, None))
    else:
        ins.update(h_in=(before.h_two, None))
        lazy.update(so_far=before.out)
    name = "ffn_fwd_one" if before is None else "ffn_fwd_two"
    return call(body, name, (steps,), ins, outs, {}, 5_000_000_000, 10_000_000, prefetch=own, lazy=lazy)


def ffn_backward(
    own, grad, mid, vec, kept, at, h_two, kind, arrays, lines, hidden, base, gh_in
):
    length, width = mid.shape
    block = 2 * lines * hidden
    b16, f32 = jnp.bfloat16, jnp.float32
    last = gh_in is not None
    wide = pl.BlockSpec((1, length, block), lambda i, own: (i + at, 0, 0))

    def body(r):
        @pl.when(pl.program_id(0) == 0)
        def _():
            r.gf[...] = r.g[...].astype(b16)
            r.gh[...] = jnp.zeros_like(r.gh)

        gf = r.gf[...]
        g_down = dot_tn(r.act[0], gf)
        g_act = dot_nt(gf, rows_of(r.down0, r.down1))
        g_pre = (g_act * r.slope[0].astype(f32)).astype(b16)
        g_up = dot_tn(g_pre, r.h_two[...])
        for n in range(2 * lines):
            rows = slice(n * hidden, (n + 1) * hidden)
            r.grads[0, n // lines, n % lines, 0] = g_up[rows].astype(b16)
            r.grads[0, n // lines, n % lines, 1] = g_down[rows].astype(b16)
        r.gbias[0] = jnp.sum(g_pre.astype(f32), axis=0, keepdims=True)
        r.gh[...] += dot_nn(g_pre, up_rows(r))
        if last:

            @pl.when(pl.program_id(0) == 1)
            def _():
                r.need(r.gh_in, r.mid)
                into, grad_gain, grad_shift = norm_grad(
                    r.gh[...] + r.gh_in[...], r.mid[...], r.vec[6:7]
                )
                r.gmid[...] = r.g[...] + into
                r.sums[...] = jnp.zeros_like(r.sums)
                r.sums[0:1] = grad_gain
                r.sums[1:2] = grad_shift
                r.sums[2:3] = jnp.sum(r.gf[...].astype(f32), axis=0, keepdims=True)

    ins = dict(
        g=(grad, None),
        h_two=(h_two, None),
        act=(kept.act, wide),
        slope=(kept.slope, wide),
        **ffn_specs(kind, arrays, base, hidden, lines, width),
    )
    outs = dict(
        grads=(
            (2, 2, lines, 2, hidden, width),
            b16,
            pl.BlockSpec((1, 2, lines, 2, hidden, width), lambda i, own: (i, 0, 0, 0, 0, 0)),
        ),
        gbias=((2, 1, block), f32, pl.BlockSpec((1, 1, block), lambda i, own: (i, 0, 0))),
    )
    scratch = dict(gf=((length, width), b16))
    lazy = {}
    if last:
        ins.update(vec=(vec, None))
        lazy.update(gh_in=gh_in, mid=mid)
        outs.update(gmid=((length, width), f32, None), sums=((8, width), f32, None))
        scratch.update(gh=((length, width), f32))
    else:
        outs.update(gh=((length, width), f32, None))
    name = "ffn_bwd_two" if last else "ffn_bwd_one"
    return call(
        body, name, (2,), ins, outs, scratch, 9_000_000_000, 15_000_000, prefetch=own, lazy=lazy
    )


def put_pieces(r, index, values):
    count, _, slots, _ = r.kept.shape
    for piece in range(2 * count):
        ref = r.kept if piece < count else r.sent
        ref[piece % count, index] = values[piece * slots : (piece + 1) * slots].astype(ref.dtype)
    r.flush(r.sent, index)
    r.flush(r.kept, index)


def attn_grad_open(r):
    b16 = jnp.bfloat16
    r.need(r.gmid, r.w3)
    r.ga[...] = r.gmid[...].astype(b16)
    gatt = dot_nt(r.ga[...], r.w3[...]).astype(b16)
    r.need(r.q, r.v)
    for start in range(gatt.shape[1] // 128):
        lanes = slice(128 * start, 128 * start + 128)
        r.gatt[start] = gatt[:, lanes]
        r.qs[start] = r.q[:, lanes]
        r.vs[start] = r.v[:, lanes]
    gatt_t = gatt.astype(jnp.float32).T
    r.gatt_t[...] = gatt_t.astype(b16)
    r.need(r.att_t)
    for head in range(HEADS):
        rows = slice(head * HEAD_DIM, (head + 1) * HEAD_DIM)
        r.inner[head] = jnp.sum(gatt_t[rows] * r.att_t[rows], axis=0, keepdims=True)
    r.need(r.kt)


def attn_grad_heads(r, group):
    gatt_block, q_block, v_block = r.gatt[group], r.qs[group], r.vs[group]
    gatt_t = r.gatt_t[pl.ds(pl.multiple_of(group * 128, 128), 128), :]
    dk = jnp.zeros(q_block.shape, jnp.float32)
    dv = jnp.zeros(q_block.shape, jnp.float32)
    for head in range(GROUP):
        probs = r.probs[head]
        gprobs = dot_nn(head_lanes(v_block, head), gatt_t)
        inner = r.inner[group * GROUP + head]
        gscores = (probs.astype(jnp.float32) * (gprobs - inner)).astype(jnp.bfloat16)
        dv += dot_nn(probs, head_lanes(gatt_block, head))
        dk += dot_nn(gscores, head_lanes(q_block, head))
        rows = pl.ds(pl.multiple_of(group * 128 + head * HEAD_DIM, HEAD_DIM), HEAD_DIM)
        r.dqt[rows, :] = dot_nn(r.kt[rows, :], gscores)
    r.dk[group] = dk
    r.dv[group] = dv


def attn_grad_close(r):
    b16, f32 = jnp.bfloat16, jnp.float32

    def joined(ref):
        return jnp.concatenate([ref[i] for i in range(ref.shape[0])], axis=1)

    def rounded(values):
        return values.astype(b16).astype(f32)

    r.need(r.att_rel, r.cos, r.sin, r.h_rel, r.w0, r.w1, r.w2, r.x)
    put_pieces(r, 3, dot_tn(r.att_rel[...], r.ga[...]))
    gq = rounded(r.dqt[...].T) * HEAD_DIM ** (-0.5)
    gproj = [
        turn(gq, r.cos, r.sin, -1.0).astype(b16),
        turn(rounded(joined(r.dk)), r.cos, r.sin, -1.0).astype(b16),
        joined(r.dv).astype(b16),
    ]
    r.sums[...] = jnp.zeros_like(r.sums)
    gh = jnp.zeros(r.gx.shape, f32)
    for j in range(3):
        put_pieces(r, j, dot_tn(r.h_rel[...], gproj[j]))
        r.sums[j : j + 1] = jnp.sum(gproj[j].astype(f32), axis=0, keepdims=True)
        gh += dot_nt(gproj[j], (r.w0, r.w1, r.w2)[j][...])
    into, grad_gain, grad_shift = norm_grad(gh, r.x[...], r.vec[4:5])
    r.gx[...] = r.gmid[...] + into
    r.sums[3:4] = jnp.sum(r.ga[...].astype(f32), axis=0, keepdims=True)
    r.sums[4:5] = grad_gain
    r.sums[5:6] = grad_shift


def attn_backward(slots, gmid, x, vec, cos, sin, saved):
    length, width = x.shape
    spots = saved.h_rel.shape[1]
    half = spots // slots // 2
    groups = width // 128
    b16, f32 = jnp.bfloat16, jnp.float32

    def body(r):
        step = pl.program_id(0)
        pl.when(step == 0)(lambda: attn_grad_open(r))
        attn_grad_heads(r, step)
        pl.when(step == groups - 1)(lambda: attn_grad_close(r))

    lazy = dict(
        gmid=gmid, w3=(saved.wabs, 3), q=saved.q, v=saved.v, att_t=saved.att_t, kt=saved.kt,
        att_rel=saved.att_rel, cos=cos, sin=sin, h_rel=saved.h_rel, w0=(saved.wabs, 0),
        w1=(saved.wabs, 1), w2=(saved.wabs, 2), x=x,
    )
    ins = dict(
        vec=(vec, None),
        probs=(saved.probs, pl.BlockSpec((GROUP, length, length), lambda i: (i, 0, 0))),
    )
    split = ((groups, length, 128), b16)
    sums = ((groups, length, 128), f32)
    return call(
        body, "attn_bwd", (groups,), ins,
        dict(
            gx=((length, width), f32, None),
            kept=((half, 4, slots, width), b16, EAGER),
            sent=((half, 4, slots, width), b16, EAGER),
            sums=((8, width), f32, None),
        ),
        dict(
            ga=((length, width), b16),
            gatt=split,
            qs=split,
            vs=split,
            gatt_t=((width, length), b16),
            inner=((HEADS, 1, length), f32),
            dqt=((width, length), f32),
            dk=sums,
            dv=sums,
        ),
        30_000_000_000, 30_000_000, lazy=lazy,
    )


def total_of(one, two):
    return one.astype(jnp.float32) + two.astype(jnp.float32)


def add_core(kept, came):
    _, _, lines, _, rows, width = kept.shape
    b16 = jnp.bfloat16
    both = pl.BlockSpec((2, 2, 1, 2, rows, width), lambda i: (0, 0, i, 0, 0, 0))
    one = ((2, lines, rows, width), b16, pl.BlockSpec((2, 1, rows, width), lambda i: (0, i, 0, 0)))

    def body(r):
        for n in range(2):
            r.ak[n, 0] = total_of(r.kept[0, n, 0, 0], r.came[0, n, 0, 0]).astype(b16)
            r.at[n, 0] = total_of(r.kept[1, n, 0, 0], r.came[1, n, 0, 0]).astype(b16)
            r.bk[n, 0] = total_of(r.kept[n, 0, 0, 1], r.came[n, 0, 0, 1]).astype(b16)
            r.bt[n, 0] = total_of(r.kept[n, 1, 0, 1], r.came[n, 1, 0, 1]).astype(b16)

    made = call(
        body, "add_core", (lines,), dict(kept=(kept, both), came=(came, both)),
        dict(ak=one, at=one, bk=one, bt=one), {}, 10_000_000, 10_000_000, limit=SMALL_LIMIT,
    )
    return (made.ak, made.at, made.bk, made.bt)


def add_first(ak, ac, bk, bc, limit=None):
    _, lines, rows, width = ak.shape
    b16 = jnp.bfloat16
    steps = max(1, lines // 2)
    block = lines // steps
    both = pl.BlockSpec((2, block, rows, width), lambda i: (0, i, 0, 0))
    one = ((lines, rows, width), b16, pl.BlockSpec((block, rows, width), lambda i: (i, 0, 0)))

    def body(r):
        r.a0[...] = total_of(r.ak[0], r.ac[0]).astype(b16)
        r.a1[...] = total_of(r.ak[1], r.ac[1]).astype(b16)
        r.b0[...] = total_of(r.bk[0], r.bc[0]).astype(b16)
        r.b1[...] = total_of(r.bk[1], r.bc[1]).astype(b16)

    made = call(
        body, "add_first", (steps,),
        dict(ak=(ak, both), ac=(ac, both), bk=(bk, both), bc=(bc, both)),
        dict(a0=one, a1=one, b0=one, b1=one), {}, 10_000_000, 10_000_000, limit=limit or SMALL_LIMIT,
    )
    return (made.a0, made.a1, made.b0, made.b1)


def add_second(own, ak, ac, bk, bc):
    lines, rows, width = ak.shape
    b16 = jnp.bfloat16
    half = lines // 2

    def place(i):
        order, unit, left = 0, 1, half
        while left:
            order += (i // left % 2) * unit
            unit, left = unit * 2, left // 2
        return order

    shape = (half, 2, rows, width)

    def body(r):
        for n in range(lines):
            line = place(n) ^ r.own[3]
            ref = r.kept if n < half else r.sent
            ref[n % half, 0] = total_of(r.ak[line], r.ac[line]).astype(b16)
            ref[n % half, 1] = total_of(r.bk[line], r.bc[line]).astype(b16)

    made = call(
        body, "add_second", (1,),
        dict(ak=(ak, None), ac=(ac, None), bk=(bk, None), bc=(bc, None)),
        dict(kept=(shape, b16, None), sent=(shape, b16, None)), {},
        10_000_000, 5_000_000, prefetch=own, limit=SMALL_LIMIT,
    )
    return (made.kept, made.sent)


def add_line(kept, came):
    half, _, rows, width = kept.shape
    shape = (half // 2, 2, rows, width)

    def body(r):
        total = total_of(r.kept[...], r.came[...])
        r.low[...] = total[: half // 2]
        r.high[...] = total[half // 2 :].astype(jnp.bfloat16)

    made = call(
        body, "add_line", (1,), dict(kept=(kept, None), came=(came, None)),
        dict(low=(shape, jnp.float32, None), high=(shape, jnp.bfloat16, None)), {},
        10_000_000, 2_000_000, limit=SMALL_LIMIT,
    )
    return (made.low, made.high)


def shards(
    sizes,
    tokens,
    qkv_weight,
    out_weight,
    proj_bias,
    norm_gain,
    norm_shift,
    up_weight,
    down_weight,
    up_bias,
    seq_order,
    seq_length,
    mlm_mask,
    cotangent,
):
    _, length, width = tokens.shape
    layer_count = qkv_weight.shape[0]
    _, ffn_size, core_size = sizes
    lines = ffn_size // 2
    count = 2 * ffn_size * core_size
    x_bit, y_bit, core_bit, line_unit = ffn_size * core_size, core_size, 1, 2 * core_size
    own_id = lax.axis_index(AXES)
    own_x = (own_id // x_bit) % 2
    own_y = (own_id // y_bit) % 2
    own_core = own_id % 2
    own_line = (own_id // line_unit) % lines
    own = jnp.stack([own_x, own_y, own_core, own_line]).astype(jnp.int32)
    rows = qkv_weight.shape[2]
    slots = pad_rows(rows)
    hidden = up_weight.shape[1]
    b16, f32 = jnp.bfloat16, jnp.float32

    def device(x, y, line, core):
        return (x * ffn_size + line * 2 + y) * core_size + core

    def swap(values, bits):
        return lax.ppermute(values, AXES, [(i, i ^ bits) for i in range(count)])

    def grow(values, bits, axis):
        return jnp.concatenate([values, swap(values, bits)], axis=axis)

    def line_swaps(values):
        return [swap(values, n * line_unit) for n in range(1, lines)]

    def line_join(values, came):
        joined = jnp.stack([values] + list(came))
        bit = lines // 2
        while bit:
            pairs = joined.reshape(lines // (2 * bit), 2, bit, *values.shape)
            joined = jnp.where((own_line & bit) > 0, jnp.flip(pairs, 1), pairs)
            joined = joined.reshape(lines, *values.shape)
            bit //= 2
        return joined

    def attn_lines(values, came):
        joined = line_join(values, came).transpose(1, 0, 2, 3)
        joined = joined.reshape(4, lines * slots, width)
        return (joined[:2], joined[2:])

    def hold(value, *others):
        return lax.optimization_barrier((value, *others))

    def along(values, came):
        return jnp.concatenate([values, came], axis=1)

    order_ids = jnp.arange(seq_length.shape[0], dtype=jnp.int32)
    slot_length = jnp.sum(jnp.where(seq_order[0] == order_ids, seq_length, 0))
    key_ok = jnp.arange(length, dtype=jnp.int32) < slot_length
    loss_weight = jnp.where(key_ok & (mlm_mask[0] > 0), 1.0, 0.0).astype(f32)
    local_count = jnp.sum(loss_weight)
    count_high = jnp.floor(local_count / 256.0)
    count_low = local_count - 256.0 * count_high
    small_len = 9 * rows + hidden
    layers = range(layer_count)
    small_row = jnp.concatenate(
        [
            part.reshape(-1)
            for layer in layers
            for part in (proj_bias[layer], norm_gain[layer], norm_shift[layer], up_bias[layer])
        ]
        + [count_high[None], count_low[None]]
    ).astype(b16)
    small_row = jnp.pad(small_row, (0, width - small_row.shape[0]))
    spare = jnp.zeros((4, slots - rows, width), b16)
    spare_at = jnp.arange(4 * (slots - rows)).reshape(4, slots - rows, 1) == 0
    spare = jnp.where(spare_at, small_row[None, None], spare)
    attn = jnp.concatenate([qkv_weight[0], out_weight[0][None]]).astype(b16)
    attn = jnp.concatenate([attn, spare], axis=1)
    attn, up_weight, down_weight, qkv_late, out_late = lax.optimization_barrier(
        (attn, up_weight, down_weight, qkv_weight[1], out_weight[1])
    )

    def ffn_piece(layer):
        return jnp.stack([up_weight[layer], down_weight[layer]]).astype(b16)

    def pair(values, came, bit):
        high = (own_line & bit) > 0
        return jnp.stack(
            [jnp.where(high, came, values), jnp.where(high, values, came)], axis=1
        ).reshape(-1, *values.shape[1:])

    part_a, part_b = attn_lines(attn, line_swaps(attn))
    ffn = after(ffn_piece(0), part_a)[None]
    bit = lines // 2
    came_a, came_b, came = (swap(part_a, y_bit), swap(part_b, x_bit), swap(ffn, bit * line_unit))
    came_a, came_b, came = hold(came_a, came_b, came)
    part_a, part_b = along(part_a, came_a), along(part_b, came_b)
    ffn = pair(ffn, came, bit)
    bit //= 2
    came_a, came_b, came = (swap(part_a, x_bit), swap(part_b, y_bit), swap(ffn, bit * line_unit))
    came_a, came_b, came = hold(came_a, came_b, came)
    part_a, part_b = along(part_a, came_a), along(part_b, came_b)
    ffn = pair(ffn, came, bit)
    while bit > 1:
        bit //= 2
        ffn = pair(ffn, swap(ffn, bit * line_unit), bit)
    half_a, half_b = (swap(part_a, core_bit), swap(part_b, core_bit))
    up_all = ffn[:, 0].reshape(lines * hidden, width)
    down_all = ffn[:, 1].reshape(lines * hidden, width)
    up_came, down_came = (swap(up_all, y_bit), swap(down_all, x_bit))

    next_attn = jnp.concatenate([qkv_late, out_late[None]]).astype(b16)
    next_attn = jnp.pad(next_attn, ((0, 0), (0, slots - rows), (0, 0)))
    next_attn = after(next_attn, ffn)
    next_came = line_swaps(next_attn)
    index = jnp.arange(count, dtype=jnp.int32)
    line_at = index % lines
    low_at = index // lines % 2
    high_at = index // (2 * lines) % 2
    core_at = (index // (4 * lines)) ^ own_core
    owners_a = device(high_at ^ own_x, low_at ^ own_y, line_at, core_at)
    owners_b = device(low_at ^ own_x, high_at ^ own_y, line_at, core_at)

    def spread_of(owners, size):
        slot_ids = jnp.arange(size, dtype=jnp.int32)
        source_row = jnp.where(
            slot_ids[None, :] < rows, owners[:, None] * rows + slot_ids[None, :], -1
        ).reshape(count * size)
        return (jnp.arange(width, dtype=jnp.int32)[:, None] == source_row[None, :]).astype(b16)

    spread_a, spread_b = spread_of(owners_a, slots), spread_of(owners_b, slots)
    hot = owners_a[:, None] == index[None, :]
    cos_half, sin_half = rope_tables(length, HEAD_DIM)
    cos = jnp.tile(jnp.concatenate([cos_half, cos_half], axis=1), (1, GROUP))
    sin = jnp.tile(jnp.concatenate([-sin_half, sin_half], axis=1), (1, GROUP))
    mask = jnp.where(key_ok, 0.0, mask_value).astype(f32)[:, None]

    small_own = jnp.concatenate(
        [part[0].reshape(-1, slots, width)[:, rows, :] for part in (part_a, half_a)]
    )
    small_all = dot_tn(hot.astype(b16), small_own)
    spot = layer_count * small_len
    masked_total = jnp.sum(small_all[:, spot] * 256.0 + small_all[:, spot + 1])
    factor = seq_length.shape[0] * length / jnp.maximum(masked_total, 1.0)

    vecs, biases = [], []
    for layer in layers:
        start = layer * small_len
        vec = small_all[:, start : start + 9 * rows]
        vec = vec.reshape(count, 9, rows).transpose(1, 0, 2).reshape(9, width)
        vec = jnp.concatenate([vec[:4], vec[5:6], vec[7:8], vec[6:7], vec[8:9], vec[4:5]])
        vecs.append(jnp.pad(vec, ((0, 7), (0, 0))))
        bias = small_own[:, start + 9 * rows : start + small_len]
        biases.append(bias.reshape(count * hidden).astype(f32))

    kinds = ("own", "own" if hidden % 16 else "late")
    groups = width // 128
    streams, attns, ffns = [tokens[0]], [], []

    late_start = None

    next_a = next_b = came_a = came_b = None

    def between(value):
        nonlocal up_all, down_all, up_came, down_came, next_came, late_start
        nonlocal next_a, next_b, came_a, came_b
        value, up_came, down_came, *next_came = hold(value, up_came, down_came, *next_came)
        late_start = value
        up_all = jnp.concatenate([up_all, up_came])
        down_all = jnp.concatenate([down_all, down_came])
        up_came, down_came = (swap(up_all, x_bit), swap(down_all, y_bit))
        next_a, next_b = attn_lines(next_attn, next_came)
        came_a, came_b = (swap(next_a, y_bit), swap(next_b, x_bit))
        return value

    attns.append(
        attn_forward(
            streams[0],
            dict(wa=part_a, wa2=half_a, wb=part_b, wb2=half_b),
            dict(sa=spread_a, sb=spread_b),
            vecs[0], cos, sin, mask, CUT, between,
        )
    )
    late = after(ffn_piece(1).reshape(2 * hidden, width), late_start)
    late = lax.all_gather(late, AXES, axis=0, tiled=False)
    late = late.reshape(2, lines, 2, 2, late.shape[1], width)
    late_weights = [(late,), (late,)]
    if kinds[1] == "own":
        turned = late[:, :, :, :, : 2 * hidden].reshape(2, lines, 2, 2, 2, hidden, width)
        for axis, odd in ((0, own_x), (2, own_y), (3, own_core)):
            turned = jnp.where(odd > 0, jnp.flip(turned, axis), turned)
        late_up = turned[:, :, :, :, 0].transpose(3, 0, 2, 1, 4, 5)
        late_down = turned[:, :, :, :, 1].transpose(3, 2, 0, 1, 4, 5)
        late_weights = [
            (late_up[n].reshape(-1, width), late_down[n].reshape(-1, width)) for n in range(2)
        ]

    attns[0].mid, up_came, down_came, came_a, came_b = hold(
        attns[0].mid, up_came, down_came, came_a, came_b
    )
    next_a, next_b = (along(next_a, came_a), along(next_b, came_b))
    up_all = jnp.concatenate([up_all, up_came])
    down_all = jnp.concatenate([down_all, down_came])
    up_came, down_came = (swap(up_all, core_bit), swap(down_all, core_bit))
    came_a, came_b = (swap(next_a, x_bit), swap(next_b, y_bit))
    weights = [[(up_all, down_all), (up_came, down_came)], late_weights]

    def ffn_front(layer, base, before):
        halves = 1 if kinds[layer] == "late" else 2
        bias = biases[layer].reshape(halves, -1)[base]
        return ffn_forward(
            own, attns[layer].mid, vecs[layer], kinds[layer], weights[layer][base], bias, lines,
            hidden, base, 4 // halves, before,
        )

    first = ffn_front(0, 0, None)
    first.out, came_a, came_b, up_came, down_came = hold(
        first.out, came_a, came_b, up_came, down_came
    )
    weights[0][1] = (up_came, down_came)
    next_a, next_b = (along(next_a, came_a), along(next_b, came_b))
    came_a, came_b = (swap(next_a, core_bit), swap(next_b, core_bit))
    ffns.append([first, ffn_front(0, 1, first)])
    stream, came_a, came_b = hold(ffns[0][1].out, came_a, came_b)
    streams.append(stream)
    attns.append(
        attn_forward(
            stream,
            dict(
                wa=next_a, wa2=came_a, wb=next_b, wb2=came_b,
            ),
            dict(sa=spread_a, sb=spread_b),
            vecs[1], cos, sin, mask, groups, None,
        )
    )
    ffns.append([ffn_front(1, 0, None)])
    if kinds[1] == "own":
        ffns[1].append(ffn_front(1, 1, ffns[1][0]))
    result = ffns[1][-1].out

    def ffn_back(layer, grad, base, gh_in):
        joint = len(ffns[layer]) == 1
        return ffn_backward(
            own, grad, attns[layer].mid, vecs[layer], ffns[layer][0 if joint else base],
            2 * base if joint else 0, ffns[layer][0].h_two, kinds[layer], weights[layer][base],
            lines, hidden, base, gh_in,
        )

    def attn_back(layer, grad_mid):
        return attn_backward(slots, grad_mid, streams[layer], vecs[layer], cos, sin, attns[layer])

    def core_step(kept, sent):
        return (kept, swap(sent, core_bit))

    def first_step(kept, came):
        ak, at, bk, bt = add_core(kept, came)
        return (ak, swap(at, x_bit), bk, swap(bt, y_bit))

    def second_step(*parts, limit=None):
        a0, a1, b0, b1 = add_first(*parts, limit=limit)
        return (a0, swap(a1, y_bit), b0, swap(b1, x_bit))

    def third_step(*parts):
        kept, sent = add_second(own, *parts)
        return (kept, swap(sent, line_unit))

    def line_step(unit, kept, came):
        kept, sent = add_line(kept, came)
        return (kept, swap(sent, unit))

    def split_attn(values):
        return values.reshape(2, 2, lines, 2, 2 * slots, width)

    grad = cotangent[0] * (loss_weight[:, None] * factor)
    one1 = ffn_back(1, grad, 1, None)
    came = swap(one1.grads, core_bit)
    two1 = ffn_back(1, grad, 0, one1.gh)
    gmid, f1k, f1c = hold(two1.gmid, two1.grads, came)
    f1 = first_step(f1k, f1c)
    attn_g1 = attn_back(1, after(gmid, f1[0]))
    grad, kept, sent, sums, *f1 = hold(
        attn_g1.gx, attn_g1.kept, attn_g1.sent, attn_g1.sums, *f1
    )
    attn_g1.sums = sums
    a1k, a1c = core_step(split_attn(kept), split_attn(sent))
    f1 = second_step(*f1)
    a1k, a1c, *_ = hold(a1k, a1c, f1[0])
    a1 = first_step(a1k, a1c)
    one0 = ffn_back(0, after(grad, f1[0], a1[0]), 1, None)
    gh, sent, *parts = hold(one0.gh, one0.grads, *f1, *a1)
    f0 = swap(sent, core_bit)
    f1 = third_step(*parts[:4])
    a1 = second_step(*parts[4:])
    two0 = ffn_back(0, grad, 0, after(gh, f1[0], a1[0]))
    gmid, f0k, f0c, *parts = hold(two0.gmid, two0.grads, f0, *f1, *a1)
    f0 = first_step(f0k, f0c)
    unit = 2 * line_unit
    f1 = line_step(unit, *parts[:2])
    a1 = third_step(*parts[2:])
    attn_g0 = attn_back(0, after(gmid, f0[0], a1[0], f1[0]))
    kept, sent, sums, *parts = hold(attn_g0.kept, attn_g0.sent, attn_g0.sums, *f1, *a1, *f0)
    a0k, a0c = core_step(split_attn(kept), split_attn(sent))
    f1 = parts[:2]
    f0 = second_step(*parts[4:], limit=VMEM_LIMIT)
    a0k, a0c, *_ = hold(a0k, a0c, f0[0])
    a0 = first_step(a0k, a0c)
    attn_g0.sums, a1k, a1c, *f0 = hold(sums, *parts[2:4], *f0, a0[0])[:-1]
    a1 = line_step(unit, a1k, a1c)
    f0 = third_step(*f0)
    a0 = second_step(*a0)
    f0 = line_step(unit, *f0)
    a0 = third_step(*a0)
    a0 = line_step(unit, *a0)
    while unit * 2 < lines * line_unit:
        unit *= 2
        f1, a1, f0, a0 = [line_step(unit, *parts) for parts in (f1, a1, f0, a0)]
    ffn_grads = [(two0, one0), (two1, one1)]

    small = []
    for layer, attn_g in ((0, attn_g0), (1, attn_g1)):
        two, one = ffn_grads[layer]
        a, f = attn_g.sums, two.sums
        sums = jnp.concatenate([a[:4], f[2:3], a[4:5], f[0:1], a[5:6], f[1:2]])
        sums = sums.reshape(9, count, rows).transpose(1, 0, 2).reshape(count, 9 * rows)
        bias = jnp.concatenate([two.gbias, one.gbias]).reshape(count, hidden)
        bias = lax.dot_general(
            hot.astype(f32), bias, (((0,), (0,)), ((), ())), precision=lax.Precision.HIGHEST
        )
        small += [sums, bias]
    small = lax.all_to_all(jnp.concatenate(small, axis=1), AXES, 0, 0, tiled=True)
    small = jnp.sum(small, axis=0).reshape(layer_count, small_len)

    own_attn = jnp.stack([total_of(*a0), total_of(*a1)]).reshape(layer_count, 4, slots, width)
    own_ffn = jnp.stack([total_of(*f0), total_of(*f1)]).reshape(layer_count, 2, hidden, width)
    return (
        result[None],
        attn_g0.gx[None],
        own_attn[:, :3, :rows],
        own_attn[:, 3, :rows],
        small[:, : 5 * rows].reshape(layer_count, 5, rows),
        small[:, 5 * rows : 7 * rows].reshape(layer_count, 2, rows),
        small[:, 7 * rows : 9 * rows].reshape(layer_count, 2, rows),
        own_ffn[:, 0],
        own_ffn[:, 1],
        small[:, 9 * rows :],
    )


def solution(mesh):
    in_specs = (
        P(("batch", "ffn", "mp"), None, None),
        P(None, None, ("batch", "ffn", "mp"), None),
        P(None, ("batch", "ffn", "mp"), None),
        P(None, None, ("batch", "ffn", "mp")),
        P(None, None, ("batch", "ffn", "mp")),
        P(None, None, ("batch", "ffn", "mp")),
        P(None, ("batch", "ffn", "mp"), None),
        P(None, ("batch", "ffn", "mp"), None),
        P(None, ("batch", "ffn", "mp")),
        P(("batch", "ffn", "mp")),
        P(),
        P(("batch", "ffn", "mp"), None),
        P(("batch", "ffn", "mp"), None, None),
    )
    out_specs = (
        P(("batch", "ffn", "mp"), None, None),
        P(("batch", "ffn", "mp"), None, None),
        P(None, None, ("batch", "ffn", "mp"), None),
        P(None, ("batch", "ffn", "mp"), None),
        P(None, None, ("batch", "ffn", "mp")),
        P(None, None, ("batch", "ffn", "mp")),
        P(None, None, ("batch", "ffn", "mp")),
        P(None, ("batch", "ffn", "mp"), None),
        P(None, ("batch", "ffn", "mp"), None),
        P(None, ("batch", "ffn", "mp")),
    )
    sizes = tuple(mesh.shape[name] for name in AXES)
    return jax.shard_map(partial(shards, sizes), mesh=mesh, in_specs=in_specs, out_specs=out_specs, check_vma=False)
```
